128 devices in a mesh: clip: 8 (over x, core), row: 16 (over y, z).
Axes of the slice: x: 4, y: 4, z: 4, core: 2. Of those that a mesh axis runs over, the one named last changes fastest.
Arguments:
- features: bfloat16 [8, 16, 256, 48, 128], P('clip', None, 'row'), may hold values from -6 to 6
- target: bfloat16 [8, 16, 256, 3, 48], P('clip', None, 'row'), may hold values from -6 to 6
- conv_weight: bfloat16 [3, 3, 3, 128], replicated, may hold values from -0.4375 to 0.4375
- disc_first: bfloat16 [4, 4, 3, 64], replicated, may hold values from -0.875 to 0.875
- disc_second: bfloat16 [4, 4, 64, 128], replicated, may hold values from -0.1875 to 0.1875
- disc_third: bfloat16 [4, 4, 128, 256], replicated, may hold values from -0.125 to 0.125
- disc_fourth: bfloat16 [4, 4, 256, 512], replicated, may hold values from -0.09375 to 0.09375
- disc_head: bfloat16 [4, 4, 512, 1], replicated, may hold values from -0.0625 to 0.0625
Outputs:
- feature_grad: bfloat16 [8, 16, 256, 48, 128], P('clip', None, 'row')
- gan_grad: bfloat16 [8, 16, 256, 3, 48], P('clip', None, 'row')
- weight_grad: float32 [3, 3, 3, 128], replicated
- adaptive: float32 [], replicated
The draws below stay inside these ranges and needn't reach their ends.
All inputs are finite; a program needn't handle non-finite values.
Results may differ from the reference program's by a relative error of at most 0.015.
Values may be sent and summed in bfloat16 or wider, within the bound.
A program may use at most 64 MiB of HBM per device.

```python
import jax
import jax.numpy as jnp
from jax import lax

C = 128
D1 = 64
D2 = 128
D3 = 256
D4 = 512
FRAMES = 16
WIDTH = 48
HEIGHT = 256
CLIPS = 8


def block_scale(stream_key, extent, split, smallest, top_value):
    loudness, own = 1.0, jax.random.fold_in(stream_key, 6)
    for dim, parts in split:
        steps = jnp.exp(jax.random.uniform(jax.random.fold_in(own, dim), (parts,), jnp.float32, smallest / len(split), top_value / len(split)))
        loudness = loudness * jnp.repeat(steps, extent[dim] // parts).reshape([-1 if axis == dim else 1 for axis in range(len(extent))])
    return loudness


def scatter_about(key, shape, scale, limit, split=(), kind=jnp.bfloat16):
    entries = scale * jax.random.normal(key, shape, jnp.float32)
    if split:
        entries = entries * block_scale(key, shape, split, -0.22, 0.18)
    return jnp.clip(entries, -limit, limit).astype(kind)


def setup_inputs(seed: int = 0) -> dict:
    seeds = jax.random.split(jax.random.key(seed), 9)
    features = scatter_about(seeds[0], (CLIPS, FRAMES, HEIGHT, WIDTH, C), 1.0, 6.0, ((0, 8), (2, 16)))
    target = scatter_about(seeds[1], (CLIPS, FRAMES, HEIGHT, 3, WIDTH), 1.0, 6.0, ((0, 8), (2, 16)))
    conv_weight = scatter_about(seeds[2], (3, 3, 3, C), 0.03, 0.4375)
    disc_first = scatter_about(seeds[3], (4, 4, 3, D1), 48 ** -0.5, 0.875)
    disc_second = scatter_about(seeds[4], (4, 4, D1, D2), (16 * D1) ** -0.5, 0.1875)
    disc_third = scatter_about(seeds[5], (4, 4, D2, D3), (16 * D2) ** -0.5, 0.125)
    disc_fourth = scatter_about(seeds[6], (4, 4, D3, D4), (16 * D3) ** -0.5, 0.09375)
    disc_head = scatter_about(seeds[7], (4, 4, D4, 1), (16 * D4) ** -0.5, 0.0625)
    return {"features": features, "target": target, "conv_weight": conv_weight, "disc_first": disc_first, "disc_second": disc_second, "disc_third": disc_third, "disc_fourth": disc_fourth, "disc_head": disc_head}


loss_scale = 64.0
epsilon = 0.0001

def forward_conv(padded, conv_weight):
    return lax.conv_general_dilated(padded, conv_weight, (1, 1), 'VALID', dimension_numbers=('NHWC', 'HWOI', 'NHCW'), preferred_element_type=jnp.float32)

def weight_terms(padded, grads):
    return lax.conv_general_dilated(padded, grads, (1, 1), 'VALID', dimension_numbers=('CHWN', 'IHOW', 'HWCN'), preferred_element_type=jnp.float32)

def input_grad(grad_rows, conv_weight):
    flipped = conv_weight[::-1, ::-1]
    result = lax.conv_general_dilated(grad_rows, flipped, (1, 1), ((0, 0), (1, 1)), dimension_numbers=('NHCW', 'HWIO', 'NHWC'), preferred_element_type=jnp.float32)
    return result.astype(jnp.bfloat16)

def down_conv(values, weight, stride, layout_spec):
    return lax.conv_general_dilated(values, weight, (stride, stride), ((1, 1), (1, 1)), dimension_numbers=layout_spec, preferred_element_type=jnp.float32)

def back_conv(cotangent, weight, stride, layout_spec):
    return lax.conv_general_dilated(cotangent, weight[::-1, ::-1], (1, 1), ((2, 2), (2, 2)), lhs_dilation=(stride, stride), dimension_numbers=layout_spec, preferred_element_type=jnp.float32)

def silu_slope(values):
    logistic = jax.nn.sigmoid(values)
    return logistic * (1.0 + values * (1.0 - logistic))

def disc_gradient(images, layer_one, layer_two, layer_three, layer_four, layer_head):
    plain = ('NHWC', 'HWIO', 'NHWC')
    pre_one = down_conv(images, layer_one, 2, ('NHCW', 'HWIO', 'NHWC'))
    act_one = jax.nn.silu(pre_one).astype(jnp.bfloat16)
    pre_two = down_conv(act_one, layer_two, 2, plain)
    act_two = jax.nn.silu(pre_two).astype(jnp.bfloat16)
    pre_three = down_conv(act_two, layer_three, 2, plain)
    act_three = jax.nn.silu(pre_three).astype(jnp.bfloat16)
    pre_four = down_conv(act_three, layer_four, 1, plain)
    act_four = jax.nn.silu(pre_four).astype(jnp.bfloat16)
    back_spec = ('NHWC', 'HWOI', 'NHWC')
    cot_head = jnp.full((act_four.shape[0], act_four.shape[1] - 1, act_four.shape[2] - 1, 1), -loss_scale, jnp.bfloat16)
    cot_four = (back_conv(cot_head, layer_head, 1, back_spec) * silu_slope(pre_four)).astype(jnp.bfloat16)
    cot_three = (back_conv(cot_four, layer_four, 1, back_spec) * silu_slope(pre_three)).astype(jnp.bfloat16)
    cot_two = (back_conv(cot_three, layer_three, 2, back_spec) * silu_slope(pre_two)).astype(jnp.bfloat16)
    cot_one = (back_conv(cot_two, layer_two, 2, back_spec) * silu_slope(pre_one)).astype(jnp.bfloat16)
    return back_conv(cot_one, layer_one, 2, ('NHWC', 'HWOI', 'NHCW')).astype(jnp.bfloat16)

def reference(features, target, conv_weight, disc_first, disc_second, disc_third, disc_fourth, disc_head):
    pixels = CLIPS * FRAMES * HEIGHT * WIDTH

    def first_pass(clip_index):
        clip_features = lax.dynamic_index_in_dim(features, clip_index, 0, keepdims=False)
        wanted = lax.dynamic_index_in_dim(target, clip_index, 0, keepdims=False)
        padded = jnp.pad(clip_features, ((0, 0), (1, 1), (1, 1), (0, 0)))
        rebuilt = forward_conv(padded, conv_weight)
        rec_grad = loss_scale * (rebuilt - wanted.astype(jnp.float32))
        rec_part = weight_terms(padded, rec_grad.astype(jnp.bfloat16))
        gan_grad = disc_gradient(rebuilt.astype(jnp.bfloat16), disc_first, disc_second, disc_third, disc_fourth, disc_head)
        gan_part = weight_terms(padded, gan_grad)
        return (rec_part, gan_part, rec_grad, gan_grad)
    rec_parts, gan_parts, rec_grads, gan_grads = lax.map(first_pass, jnp.arange(CLIPS, dtype=jnp.int32))
    rec_weight = lax.optimization_barrier(jnp.sum(rec_parts, axis=0))
    gan_weight = lax.optimization_barrier(jnp.sum(gan_parts, axis=0))
    adaptive = jnp.sqrt(jnp.sum(rec_weight * rec_weight)) / (jnp.sqrt(jnp.sum(gan_weight * gan_weight)) + epsilon)
    weight_grad = (rec_weight + adaptive * gan_weight) / pixels
    combined = (rec_grads + adaptive * gan_grads.astype(jnp.float32)).astype(jnp.bfloat16)

    def second_pass(clip_grads):
        grad_rows = jnp.pad(clip_grads, ((0, 0), (1, 1), (0, 0), (0, 0)))
        return input_grad(grad_rows, conv_weight)
    feature_grad = lax.map(second_pass, combined)
    return (feature_grad, gan_grads, weight_grad, adaptive)
```

```python
import functools

import jax
import jax.numpy as jnp
from jax import lax
from jax.experimental import pallas as pl
from jax.experimental.pallas import tpu as pltpu
from jax.sharding import PartitionSpec as P

MESH = pl.DeviceIdType.MESH
F32 = jnp.float32
BF16 = jnp.bfloat16
SCALE = 64.0
EPS = 0.0001
FR = 16
W = 48
NT = (((1,), (1,)), ((), ()))
TN = (((0,), (0,)), ((), ()))
VM = pltpu.VMEM


def vspec():
    return pl.BlockSpec(memory_space=pltpu.VMEM)


def dot(a, b, dims=(((1,), (0,)), ((), ()))):
    return lax.dot_general(a, b, dims, preferred_element_type=F32)


def iota(shape, dim):
    return lax.broadcasted_iota(jnp.int32, shape, dim)


def rnd(v):
    return v.astype(BF16).astype(F32)


def down1(v):
    return jnp.where(iota(v.shape, 0) >= 1, pltpu.roll(v, 1, 0), 0.0)


def up1(v):
    n = v.shape[0]
    return jnp.where(iota(v.shape, 0) < n - 1, pltpu.roll(v, n - 1, 0), 0.0)


def lroll(v, s):
    s = s % v.shape[1]
    return v if s == 0 else pltpu.roll(v, s, 1)


def forward_body(w_ref, f_ref, r_ref, e_ref, wm, frames):
    i = pl.program_id(0)

    @pl.when(i == 0)
    def _():
        wm[...] = jnp.zeros_like(wm)
        for ab in range(9):
            wm[ab * 8 : ab * 8 + 3, :] = w_ref[ab // 3, ab % 3].astype(F32)

    wmb = wm[...].astype(BF16)
    col = iota((8, 768), 1) % W
    pad = jnp.zeros((8, 128), F32)
    for k in range(frames):
        feats = f_ref[k].reshape(768, 128)
        part = dot(wmb, feats, NT)
        total = None
        for ab in range(9):
            a, b = ab // 3, ab % 3
            g = part[ab * 8 : ab * 8 + 8, :]
            if b == 0:
                g = jnp.where(col <= W - 2, g, 0.0)
            elif b == 2:
                g = jnp.where(col >= 1, g, 0.0)
            g = lroll(jnp.concatenate([g, pad], 1), (2 - a) * W + 1 - b)
            total = g if total is None else total + g
        f = i * frames + k
        for t in range(7):
            tile = total[0:3, t * 128 : t * 128 + 128]
            r_ref[k, 3 * t : 3 * t + 3, :] = tile
            if t in (0, 6):
                for o in range(3):
                    e_ref[0 if t == 0 else 1, o, pl.ds(f, 1), :] = tile[o : o + 1, :]
        r_ref[k, 21:24, :] = jnp.zeros((3, 128), F32)


def forward_partials(conv_weight, features):
    frames = 4
    return pl.pallas_call(
        functools.partial(forward_body, frames=frames),
        grid=(FR // frames,),
        out_shape=(
            jax.ShapeDtypeStruct((FR, 24, 128), F32),
            jax.ShapeDtypeStruct((2, 3, FR, 128), F32),
        ),
        in_specs=[
            pl.BlockSpec((3, 3, 3, 128), lambda i: (0, 0, 0, 0)),
            pl.BlockSpec((frames, 16, W, 128), lambda i: (i, 0, 0, 0)),
        ],
        out_specs=(
            pl.BlockSpec((frames, 24, 128), lambda i: (i, 0, 0)),
            pl.BlockSpec((2, 3, FR, 128), lambda i: (0, 0, 0, 0)),
        ),
        scratch_shapes=[VM((80, 128), F32)],
        name="forward_partials",
    )(conv_weight, features)


def exchange_body(m_ref, e_ref, recv, nb, send, got, esend, egot, own):
    r = lax.axis_index("row")
    barrier = pltpu.get_barrier_semaphore()
    for d in range(1, FR):
        pl.semaphore_signal(
            barrier, inc=1, device_id={"row": lax.rem(r + d, FR)}, device_id_type=MESH
        )
    local = pltpu.make_async_copy(m_ref.at[r], recv.at[r], own)
    local.start()
    pl.semaphore_wait(barrier, FR - 1)
    copies = []
    for d in range(1, FR):
        peer = lax.rem(r + d, FR)
        copies.append(
            pltpu.make_async_remote_copy(
                src_ref=m_ref.at[peer],
                dst_ref=recv.at[r],
                send_sem=send.at[d],
                recv_sem=got.at[d],
                device_id={"row": peer},
                device_id_type=MESH,
            )
        )
    for d, k in ((FR - 1, 0), (1, 1)):
        copies.append(
            pltpu.make_async_remote_copy(
                src_ref=e_ref.at[k],
                dst_ref=nb.at[1 - k],
                send_sem=esend.at[k],
                recv_sem=egot.at[k],
                device_id={"row": lax.rem(r + d, FR)},
                device_id_type=MESH,
            )
        )
    for c in copies:
        c.start()
    local.wait()
    for c in copies:
        c.wait()


def exchange(messages, edges, collective_id):
    return pl.pallas_call(
        exchange_body,
        out_shape=(
            jax.ShapeDtypeStruct((FR, 24, 128), F32),
            jax.ShapeDtypeStruct((2, 3, FR, 128), F32),
        ),
        in_specs=[vspec(), vspec()],
        out_specs=(vspec(), vspec()),
        scratch_shapes=[
            pltpu.SemaphoreType.DMA((FR,)),
            pltpu.SemaphoreType.DMA((FR,)),
            pltpu.SemaphoreType.DMA((2,)),
            pltpu.SemaphoreType.DMA((2,)),
            pltpu.SemaphoreType.DMA,
        ],
        compiler_params=pltpu.CompilerParams(collective_id=collective_id, has_side_effects=True),
        name=f"exchange_{collective_id}",
    )(messages, edges)


def place(tiles, lane, src, dst):
    t, off = src // 128, src % 128
    v = lroll(tiles[t], dst - off)
    if off + W > 128:
        v = jnp.where(lane - dst < 128 - off, v, lroll(tiles[t + 1], dst - off))
    return jnp.where((lane >= dst) & (lane < dst + W), v, 0.0)


def spread(tiles, lane, v, src, dst):
    t, off = dst // 128, dst % 128
    v = lroll(jnp.where((lane >= src) & (lane < src + W), v, 0.0), off - src)
    if off + W > 128:
        tiles[t] = tiles[t] + jnp.where(lane >= off, v, 0.0)
        tiles[t + 1] = tiles[t + 1] + jnp.where(lane < off + W - 128, v, 0.0)
    else:
        tiles[t] = tiles[t] + v


def build_band(w1_ref, t1):
    t1[...] = jnp.zeros_like(t1)
    row = iota((16, 128), 0)
    lane = iota((16, 128), 1)
    for ao in range(12):
        w = w1_ref[ao // 3, ao % 3].astype(F32)
        left = jnp.concatenate([w, jnp.zeros((12, 64), F32)], 0)
        patch = jnp.concatenate([left, pltpu.roll(left, 2, 0)], 1)
        for s in (13, 1, 5, 9):
            rolled = pltpu.roll(patch, s, 0)
            parts = [(0, rolled)]
            if s == 13:
                parts = [(0, jnp.where(row >= 13, rolled, 0.0)), (1, jnp.where(row < 13, rolled, 0.0))]
            for v in range(13):
                start = 4 * v - 3
                if start % 16 != s:
                    continue
                for over, tile in parts:
                    g = start // 16 + over
                    if g < 0 or g > 2:
                        continue
                    if v == 0:
                        tile = jnp.where(lane >= 64, tile, 0.0)
                    if v == 12:
                        tile = jnp.where(lane < 64, tile, 0.0)
                    r0 = ao * 64 + g * 16
                    t1[r0 : r0 + 16, v * 128 : v * 128 + 128] = tile.astype(BF16)


def silu_pair(v):
    s = jax.nn.sigmoid(v)
    return v * s, s * (1.0 + v * (1.0 - s))


def rows16(v, k):
    return v[k * 16 : k * 16 + 16]


def disc_body(
    recv_ref, w1_ref, w2_ref, w3_ref, w4_ref, head_ref, out_ref,
    t1, pp, a1, s1, a2, s2, a3, s3, c4, c3, c2, c1,
):
    lane = iota((16, 128), 1)
    build_band(w1_ref, t1)
    x = []
    for o in range(3):
        tiles = [recv_ref[pl.ds(3 * t + o, 16, stride=24), :] for t in range(7)]
        first, last = tiles[0], tiles[6]
        tiles[0] = first + jnp.where((lane >= W) & (lane < 2 * W), down1(last), 0.0)
        tiles[6] = last + jnp.where(lane < W, up1(first), 0.0)
        x.append([rnd(v) for v in tiles])
    halves = {}
    for m in range(16):
        s = 1 - m % 2
        for o in range(3):
            q = s * 3 + o
            halves[m, q] = place(x[o], lane, W * (m + 1), (q % 2) * 64)
    for i in range(9):
        piece = {}
        for q in range(6):
            m = 2 * i - 1 if q < 3 else 2 * i
            if m == -1:
                piece[q] = down1(halves[15, q])
            elif m == 16:
                piece[q] = up1(halves[0, q])
            else:
                piece[q] = halves[m, q]
        for j in range(3):
            pp[i, :, j * 128 : j * 128 + 128] = (piece[2 * j] + piece[2 * j + 1]).astype(BF16)
    lhs = jnp.concatenate([pp[0:8].reshape(128, 384), pp[1:9].reshape(128, 384)], 1)
    for v in range(13):
        pre = dot(lhs, t1[:, v * 128 : v * 128 + 128])
        act, slope = silu_pair(pre)
        s1[:, v] = slope.reshape(8, 16, 128)
        a1[1:9, v] = act.astype(BF16).reshape(8, 16, 128)
        a1[0, v] = down1(rows16(act, 7)).astype(BF16)
        a1[9, v] = up1(rows16(act, 0)).astype(BF16)
    zero = jnp.zeros((16, 128), BF16)
    for m in range(6):
        a2[m, 0, 0] = zero
        a2[m, 1, 6] = zero
        c2[m, 0] = zero
        c2[m, 13] = zero
    for m in range(4):
        lhs = jnp.concatenate(
            [a1[2 * m + a, k : k + 12].reshape(192, 128) for a in range(4) for k in range(2)], 1
        )
        pre = dot(lhs, w2_ref[...].reshape(1024, 128))
        act, slope = silu_pair(pre)
        s2[m] = slope.reshape(12, 16, 128)
        for c in range(12):
            v = rows16(act, c)
            e, p = (c + 1) % 2, (c + 1) // 2
            a2[m + 1, e, p] = v.astype(BF16)
            if m == 3:
                a2[0, e, p] = down1(v).astype(BF16)
            if m == 0:
                a2[5, e, p] = up1(v).astype(BF16)
    zero = jnp.zeros((16, 256), BF16)
    for k in range(5):
        a3[k, 0] = zero
        a3[k, 7] = zero
    for k in range(4):
        c3[k, 0] = zero
        c3[k, 7] = zero
    acc = None
    for a in range(4):
        lhs = jnp.concatenate(
            [
                jnp.concatenate(
                    [a2[2 * m + a, b % 2, b // 2 : b // 2 + 6].reshape(96, 128) for m in range(2)], 0
                )
                for b in range(4)
            ],
            1,
        )
        term = dot(lhs, w3_ref[a * 4 : a * 4 + 4].reshape(512, 256))
        acc = term if acc is None else acc + term
    act, slope = silu_pair(acc)
    s3[...] = slope.reshape(2, 6, 16, 256)
    for c in range(6):
        v0, v1 = rows16(act, c), rows16(act, 6 + c)
        a3[0, c + 1] = down1(v1).astype(BF16)
        a3[1, c + 1] = v0.astype(BF16)
        a3[2, c + 1] = v1.astype(BF16)
        a3[3, c + 1] = up1(v0).astype(BF16)
        a3[4, c + 1] = up1(v1).astype(BF16)
    acc = None
    for a in range(4):
        lhs = jnp.concatenate(
            [
                jnp.concatenate([a3[m + a, b : b + 5].reshape(80, 256) for m in range(2)], 0)
                for b in range(4)
            ],
            1,
        )
        term = dot(lhs, w4_ref[a * 4 : a * 4 + 4].reshape(1024, 512))
        acc = term if acc is None else acc + term
    _, slope = silu_pair(acc)
    rr = iota((160, 16), 0)
    tap = iota((160, 16), 1)
    y4 = 2 * (rr % 16) + rr // 80
    x4 = (rr % 80) // 16
    py = y4 + 1 - tap // 4
    px = x4 + 1 - tap % 4
    ok = (py >= 0) & (py <= 29) & (px >= 0) & (px <= 3) & (y4 <= 30)
    mask = jnp.where(ok, -SCALE, 0.0).astype(BF16)
    head = jnp.concatenate([head_ref[a].astype(F32) for a in range(4)], 0).astype(BF16)
    cot = dot(mask, head) * slope
    zero = jnp.zeros((16, 512), BF16)
    for k in range(5):
        for c in (0, 1, 7, 8):
            c4[k, c] = zero
    for c in range(5):
        v0, v1 = rows16(cot, c), rows16(cot, 5 + c)
        c4[0, c + 2] = down1(v0).astype(BF16)
        c4[1, c + 2] = down1(v1).astype(BF16)
        c4[2, c + 2] = v0.astype(BF16)
        c4[3, c + 2] = v1.astype(BF16)
        c4[4, c + 2] = up1(v0).astype(BF16)
    acc = None
    for a in range(4):
        for b in range(4):
            lhs = jnp.concatenate(
                [c4[m + 3 - a, 3 - b : 9 - b].reshape(96, 512) for m in range(2)], 0
            )
            term = dot(lhs, w4_ref[a * 4 + b], NT)
            acc = term if acc is None else acc + term
    cot = acc * s3[...].reshape(192, 256)
    for c in range(6):
        v0, v1 = rows16(cot, c), rows16(cot, 6 + c)
        c3[0, c + 1] = down1(v1).astype(BF16)
        c3[1, c + 1] = v0.astype(BF16)
        c3[2, c + 1] = v1.astype(BF16)
        c3[3, c + 1] = up1(v0).astype(BF16)
    for first in (0, 1):
        rows = (1, 3) if first == 0 else (0, 2)
        for e in range(2):
            p0 = 1 - e
            acc = None
            for a in (first, first + 2):
                for b in (e, e + 2):
                    lo = p0 + 1 - b // 2
                    lhs = jnp.concatenate(
                        [c3[(m + 1 - a) // 2 + 1, lo : lo + 6].reshape(96, 256) for m in rows], 0
                    )
                    term = dot(lhs, w3_ref[a * 4 + b], NT)
                    acc = term if acc is None else acc + term
            for n, m in enumerate(rows):
                for p in range(6):
                    c = 2 * (p0 + p) + e - 1
                    v = rows16(acc, n * 6 + p) * s2[m, c]
                    c2[m + 1, c + 1] = v.astype(BF16)
                    if m == 3:
                        c2[0, c + 1] = down1(v).astype(BF16)
                    if m == 0:
                        c2[5, c + 1] = up1(v).astype(BF16)
    for first in (0, 1):
        rhs = jnp.concatenate(
            [w2_ref[a, h * 128 : h * 128 + 128] for a in (first, first + 2) for h in range(2)], 1
        )
        for i in range(4):
            m = 2 * i + 1 - first
            lhs = jnp.concatenate(
                [
                    c2[(m + 1 - a) // 2 + 1, 1 - h : 14 - h].reshape(208, 128)
                    for a in (first, first + 2)
                    for h in range(2)
                ],
                1,
            )
            cot = dot(lhs, rhs, NT) * s1[m].reshape(208, 128)
            for v in range(13):
                c1[m * 16 : m * 16 + 16, v * 128 : v * 128 + 128] = rows16(cot, v).astype(BF16)
    grad = dot(c1[...], t1[...], NT)
    halves = {}
    for j in range(3):
        ps = []
        for i in range(9):
            v = None
            if i <= 7:
                v = grad[i * 16 : i * 16 + 16, j * 128 : j * 128 + 128]
            if i >= 1:
                u = grad[(i - 1) * 16 : i * 16, 384 + j * 128 : 512 + j * 128]
                v = u if v is None else v + u
            ps.append(v)
        for h in range(2):
            q = 2 * j + h
            for i in range(9):
                m = 2 * i - 1 if q < 3 else 2 * i
                if 0 <= m <= 15:
                    v = ps[i]
                    if m == 15:
                        v = v + up1(ps[0])
                    if m == 0:
                        v = v + down1(ps[8])
                    halves[m, q] = rnd(v)
    for o in range(3):
        tiles = [jnp.zeros((16, 128), F32) for _ in range(7)]
        for m in range(16):
            q = (1 - m % 2) * 3 + o
            spread(tiles, lane, halves[m, q], (q % 2) * 64, W * (m + 1))
        first, last = tiles[0], tiles[6]
        tiles[0] = first + jnp.where(lane < W, down1(last), 0.0)
        tiles[6] = last + jnp.where((lane >= W) & (lane < 2 * W), up1(first), 0.0)
        for t in range(7):
            out_ref[pl.ds(3 * t + o, 16, stride=24), :] = tiles[t]
    for k in range(21, 24):
        out_ref[pl.ds(k, 16, stride=24), :] = jnp.zeros((16, 128), F32)


def disc(recv, w1, w2, w3, w4, head):
    return pl.pallas_call(
        disc_body,
        out_shape=jax.ShapeDtypeStruct((FR * 24, 128), F32),
        in_specs=[vspec()] * 6,
        out_specs=vspec(),
        scratch_shapes=[
            VM((768, 1664), BF16),
            VM((9, 16, 384), BF16),
            VM((10, 13, 16, 128), BF16),
            VM((8, 13, 16, 128), F32),
            VM((6, 2, 7, 16, 128), BF16),
            VM((4, 12, 16, 128), F32),
            VM((5, 8, 16, 256), BF16),
            VM((2, 6, 16, 256), F32),
            VM((5, 9, 16, 512), BF16),
            VM((4, 8, 16, 256), BF16),
            VM((6, 14, 16, 128), BF16),
            VM((128, 1664), BF16),
        ],
        name="disc",
    )(recv, w1, w2, w3, w4, head)


def rec_body(r_ref, nb_ref, t_ref, out_ref, e_ref, wide):
    r = lax.axis_index("row")
    lane = iota((16, 128), 1)
    wide[:, 0:W] = t_ref[...].astype(F32)
    for o in range(3):
        want = [jnp.zeros((16, 128), F32) for _ in range(7)]
        for y in range(16):
            v = wide[pl.ds(o * 16 + y, 16, stride=48), :]
            spread(want, lane, v, 0, W * (y + 1))
        for t in range(7):
            v = r_ref[pl.ds(3 * t + o, 16, stride=24), :]
            if t == 0:
                v = v + jnp.where((lane >= W) & (lane < 2 * W) & (r > 0), nb_ref[0, o], 0.0)
            if t == 6:
                v = v + jnp.where((lane < W) & (r < FR - 1), nb_ref[1, o], 0.0)
            v = SCALE * (v - want[t])
            if t == 0:
                v = jnp.where(lane >= W, v, 0.0)
            if t == 6:
                v = jnp.where(lane < W, v, 0.0)
            out_ref[t, o] = v
            if t in (0, 6):
                e_ref[t // 6, o] = v


def rec_gradient(r, nb, target):
    return pl.pallas_call(
        rec_body,
        out_shape=(
            jax.ShapeDtypeStruct((7, 3, FR, 128), F32),
            jax.ShapeDtypeStruct((2, 3, FR, 128), F32),
        ),
        in_specs=[vspec()] * 3,
        out_specs=(vspec(), vspec()),
        scratch_shapes=[VM((768, 128), F32)],
        name="rec_gradient",
    )(r, nb, target)


def weights_body(rec_ref, ne_ref, gan_ref, f_ref, acc_ref, g_ref, back_ref, gg, wide, frames):
    i = pl.program_id(0)
    lane = iota((16, 128), 1)

    @pl.when(i == 0)
    def _():
        r = lax.axis_index("row")
        acc_ref[...] = jnp.zeros_like(acc_ref)
        zero = jnp.zeros((16, 128), F32)
        for o in range(3):
            tiles = []
            for t in range(7):
                v = rec_ref[t, o]
                if t == 0:
                    v = v + jnp.where((lane < W) & (r > 0), ne_ref[0, o], 0.0)
                if t == 6:
                    v = v + jnp.where((lane >= W) & (lane < 2 * W) & (r < FR - 1), ne_ref[1, o], 0.0)
                gg[pl.ds(t * 8 + o, 16, stride=56), :] = v
                v = gan_ref[pl.ds(3 * t + o, 16, stride=24), :]
                gg[pl.ds(t * 8 + 4 + o, 16, stride=56), :] = v
                tiles.append(v)
            for y in range(16):
                wide[pl.ds(o * 16 + y, 16, stride=48), :] = place(tiles, lane, W * (y + 1), 0)
        for t in range(7):
            gg[pl.ds(t * 8 + 3, 16, stride=56), :] = zero
            gg[pl.ds(t * 8 + 7, 16, stride=56), :] = zero
        back_ref[...] = wide[:, 0:W].astype(BF16)

    col = iota((8, 768), 1) % W
    for k in range(frames):
        f = i * frames + k
        g = jnp.concatenate([gg[pl.ds(f * 56 + t * 8, 8), :] for t in range(7)], 1)
        rows = []
        for ab in range(9):
            a, b = ab // 3, ab % 3
            v = lroll(g, -((2 - a) * W + 1 - b))[:, 0:768]
            if b == 0:
                v = jnp.where(col <= W - 2, v, 0.0)
            elif b == 2:
                v = jnp.where(col >= 1, v, 0.0)
            rows.append(v)
        rows.append(jnp.zeros((8, 768), F32))
        gt = jnp.concatenate(rows, 0).astype(BF16)
        g_ref[k] = gt
        acc_ref[...] += dot(gt, f_ref[k].reshape(768, 128))


def weight_gradients(rec, ne, gan, features):
    frames = 4
    full = lambda shape: pl.BlockSpec(shape, lambda i: (0,) * len(shape))
    return pl.pallas_call(
        functools.partial(weights_body, frames=frames),
        grid=(FR // frames,),
        out_shape=(
            jax.ShapeDtypeStruct((80, 128), F32),
            jax.ShapeDtypeStruct((FR, 80, 768), BF16),
            jax.ShapeDtypeStruct((768, W), BF16),
        ),
        in_specs=[
            full((7, 3, FR, 128)),
            full((2, 3, FR, 128)),
            full((FR * 24, 128)),
            pl.BlockSpec((frames, 16, W, 128), lambda i: (i, 0, 0, 0)),
        ],
        out_specs=(
            full((80, 128)),
            pl.BlockSpec((frames, 80, 768), lambda i: (i, 0, 0)),
            full((768, W)),
        ),
        scratch_shapes=[VM((FR * 56, 128), F32), VM((768, 128), F32)],
        name="weight_gradients",
    )(rec, ne, gan, features)


def total_body(x_ref, out_ref, pair, bx, by, bz, psend, pgot, send, got, fsend, fgot):
    clip = lax.axis_index("clip")
    row = lax.axis_index("row")
    core, x = lax.rem(clip, 2), clip // 2
    y, z = row // 4, lax.rem(row, 4)

    def at(xx, yy, zz, cc):
        return (xx * 2 + cc, yy * 4 + zz)

    partner = at(x, y, z, 1 - core)
    peers = []
    for d in range(1, 4):
        peers.append(at(lax.rem(x + d, 4), y, z, core))
    for d in range(1, 4):
        peers.append(at(x, lax.rem(y + d, 4), z, core))
    for d in range(1, 4):
        peers.append(at(x, y, lax.rem(z + d, 4), core))
    barrier = pltpu.get_barrier_semaphore()
    for p in [partner] + peers:
        pl.semaphore_signal(barrier, inc=1, device_id=p, device_id_type=MESH)
    pl.semaphore_wait(barrier, 10)

    mine = pl.ds(pl.multiple_of(core * 40, 8), 40)
    other = pl.ds(pl.multiple_of((1 - core) * 40, 8), 40)
    copy = pltpu.make_async_remote_copy(
        src_ref=x_ref.at[other], dst_ref=pair, send_sem=psend, recv_sem=pgot,
        device_id=partner, device_id_type=MESH,
    )
    copy.start()
    copy.wait()
    value = x_ref[mine, :] + pair[...]
    for axis, (buf, me) in enumerate(((bx, x), (by, y), (bz, z))):
        buf[me] = value
        copies = []
        for d in range(3):
            k = axis * 3 + d
            copies.append(
                pltpu.make_async_remote_copy(
                    src_ref=buf.at[me], dst_ref=buf.at[me], send_sem=send.at[k],
                    recv_sem=got.at[k], device_id=peers[k], device_id_type=MESH,
                )
            )
        for c in copies:
            c.start()
        for c in copies:
            c.wait()
        value = (buf[0] + buf[1]) + (buf[2] + buf[3])
    out_ref[mine, :] = value
    copy = pltpu.make_async_remote_copy(
        src_ref=out_ref.at[mine], dst_ref=out_ref.at[mine], send_sem=fsend, recv_sem=fgot,
        device_id=partner, device_id_type=MESH,
    )
    copy.start()
    copy.wait()


def total(acc):
    half = (40, 128)
    return pl.pallas_call(
        total_body,
        out_shape=jax.ShapeDtypeStruct((80, 128), F32),
        in_specs=[vspec()],
        out_specs=vspec(),
        scratch_shapes=[
            VM(half, F32),
            VM((4,) + half, F32),
            VM((4,) + half, F32),
            VM((4,) + half, F32),
            pltpu.SemaphoreType.DMA,
            pltpu.SemaphoreType.DMA,
            pltpu.SemaphoreType.DMA((9,)),
            pltpu.SemaphoreType.DMA((9,)),
            pltpu.SemaphoreType.DMA,
            pltpu.SemaphoreType.DMA,
        ],
        compiler_params=pltpu.CompilerParams(collective_id=2, has_side_effects=True),
        name="total",
    )(acc)


def final_body(s_ref, w_ref, g_ref, out_ref, wg_ref, ad_ref, wf, frames, pixels):
    i = pl.program_id(0)

    @pl.when(i == 0)
    def _():
        s = s_ref[...]
        kind = iota((80, 128), 0) % 8
        sq = s * s
        rec = jnp.sum(jnp.where(kind < 3, sq, 0.0), keepdims=True)
        gan = jnp.sum(jnp.where((kind >= 4) & (kind < 7), sq, 0.0), keepdims=True)
        adaptive = jnp.sqrt(rec) / (jnp.sqrt(gan) + EPS)
        ad_ref[...] = jnp.broadcast_to(adaptive, (8, 128))
        wf[...] = jnp.zeros_like(wf)
        for ab in range(9):
            k = ab * 8
            wf[k : k + 3, :] = w_ref[ab // 3, ab % 3].astype(F32)
            wf[k + 4 : k + 7, :] = adaptive * w_ref[ab // 3, ab % 3].astype(F32)
            wg_ref[ab // 3, ab % 3] = (s[k : k + 3] + adaptive * s[k + 4 : k + 7]) / pixels

    wfb = wf[...].astype(BF16)
    for k in range(frames):
        out_ref[k] = dot(g_ref[k], wfb, TN).astype(BF16).reshape(16, W, 128)


def final(sums, conv_weight, g, pixels):
    frames = 4
    full = lambda shape: pl.BlockSpec(shape, lambda i: (0,) * len(shape))
    return pl.pallas_call(
        functools.partial(final_body, frames=frames, pixels=pixels),
        grid=(FR // frames,),
        out_shape=(
            jax.ShapeDtypeStruct((FR, 16, W, 128), BF16),
            jax.ShapeDtypeStruct((3, 3, 3, 128), F32),
            jax.ShapeDtypeStruct((8, 128), F32),
        ),
        in_specs=[
            full((80, 128)),
            full((3, 3, 3, 128)),
            pl.BlockSpec((frames, 80, 768), lambda i: (i, 0, 0)),
        ],
        out_specs=(
            pl.BlockSpec((frames, 16, W, 128), lambda i: (i, 0, 0, 0)),
            full((3, 3, 3, 128)),
            full((8, 128)),
        ),
        scratch_shapes=[VM((80, 128), F32)],
        name="final",
    )(sums, conv_weight, g)


def per_device(
    features, target, conv_weight, disc_first, disc_second, disc_third, disc_fourth, disc_head
):
    feats = features[0]
    wanted = jnp.transpose(target[0], (0, 2, 1, 3)).reshape(768, W)
    w1 = jnp.transpose(disc_first, (0, 2, 1, 3))
    w2 = disc_second.reshape(4, 256, 128)
    w3 = disc_third.reshape(16, 128, 256)
    w4 = disc_fourth.reshape(16, 256, 512)
    head = disc_head.reshape(4, 4, 512)
    pixels = float(8 * FR * 256 * W)
    parts, edges = forward_partials(conv_weight, feats)
    recv, nb = exchange(parts, edges, 0)
    rec, rec_edges = rec_gradient(parts.reshape(FR * 24, 128), nb, wanted)
    messages = disc(recv.reshape(FR * 24, 128), w1, w2, w3, w4, head)
    gan, ne = exchange(messages.reshape(FR, 24, 128), rec_edges, 1)
    acc, g, back = weight_gradients(rec, ne, gan.reshape(FR * 24, 128), feats)
    sums = total(acc)
    feature_grad, weight_grad, adaptive = final(sums, conv_weight, g, pixels)
    image_back = jnp.transpose(back.reshape(FR, 3, 16, W), (0, 2, 1, 3))
    return (feature_grad[None], image_back[None], weight_grad, adaptive[0, 0])


def solution(mesh):
    return jax.shard_map(
        per_device,
        mesh=mesh,
        in_specs=(
            P("clip", None, "row", None, None),
            P("clip", None, "row", None, None),
            P(),
            P(),
            P(),
            P(),
            P(),
            P(),
        ),
        out_specs=(
            P("clip", None, "row", None, None),
            P("clip", None, "row", None, None),
            P(),
            P(),
        ),
        check_vma=False,
    )
```

```python
import functools

import jax
import jax.numpy as jnp
from jax import lax
from jax.experimental import pallas as pl
from jax.experimental.pallas import tpu as pltpu
from jax.sharding import PartitionSpec as P

MESH = pl.DeviceIdType.MESH
F32 = jnp.float32
BF16 = jnp.bfloat16
SCALE = 64.0
EPS = 0.0001
FR = 16
W = 48
NT = (((1,), (1,)), ((), ()))
TN = (((0,), (0,)), ((), ()))
VM = pltpu.VMEM


def vspec():
    return pl.BlockSpec(memory_space=pltpu.VMEM)


def dot(a, b, dims=(((1,), (0,)), ((), ()))):
    return lax.dot_general(a, b, dims, preferred_element_type=F32)


def iota(shape, dim):
    return lax.broadcasted_iota(jnp.int32, shape, dim)


def rnd(v):
    return v.astype(BF16).astype(F32)


def down1(v):
    return jnp.where(iota(v.shape, 0) >= 1, pltpu.roll(v, 1, 0), 0.0)


def up1(v):
    n = v.shape[0]
    return jnp.where(iota(v.shape, 0) < n - 1, pltpu.roll(v, n - 1, 0), 0.0)


def lroll(v, s):
    s = s % v.shape[1]
    return v if s == 0 else pltpu.roll(v, s, 1)


def place(tiles, lane, src, dst):
    t, off = src // 128, src % 128
    v = lroll(tiles[t], dst - off)
    if off + W > 128:
        v = jnp.where(lane - dst < 128 - off, v, lroll(tiles[t + 1], dst - off))
    return jnp.where((lane >= dst) & (lane < dst + W), v, 0.0)


def spread(tiles, lane, v, src, dst):
    t, off = dst // 128, dst % 128
    v = lroll(jnp.where((lane >= src) & (lane < src + W), v, 0.0), off - src)
    if off + W > 128:
        tiles[t] = tiles[t] + jnp.where(lane >= off, v, 0.0)
        tiles[t + 1] = tiles[t + 1] + jnp.where(lane < off + W - 128, v, 0.0)
    else:
        tiles[t] = tiles[t] + v


def build_band(w1_ref, t1):
    t1[...] = jnp.zeros_like(t1)
    row = iota((16, 128), 0)
    lane = iota((16, 128), 1)
    for ao in range(12):
        w = w1_ref[ao // 3, ao % 3].astype(F32)
        left = jnp.concatenate([w, jnp.zeros((12, 64), F32)], 0)
        patch = jnp.concatenate([left, pltpu.roll(left, 2, 0)], 1)
        for s in (13, 1, 5, 9):
            rolled = pltpu.roll(patch, s, 0)
            parts = [(0, rolled)]
            if s == 13:
                parts = [(0, jnp.where(row >= 13, rolled, 0.0)), (1, jnp.where(row < 13, rolled, 0.0))]
            for v in range(13):
                start = 4 * v - 3
                if start % 16 != s:
                    continue
                for over, tile in parts:
                    g = start // 16 + over
                    if g < 0 or g > 2:
                        continue
                    if v == 0:
                        tile = jnp.where(lane >= 64, tile, 0.0)
                    if v == 12:
                        tile = jnp.where(lane < 64, tile, 0.0)
                    r0 = ao * 64 + g * 16
                    t1[r0 : r0 + 16, v * 128 : v * 128 + 128] = tile.astype(BF16)


def silu_pair(v):
    s = jax.nn.sigmoid(v)
    return v * s, s * (1.0 + v * (1.0 - s))


def rows16(v, k):
    return v[k * 16 : k * 16 + 16]


def disc_stage(
    recv_ref, w2_ref, w3_ref, w4_ref, head_ref, out_ref, wait2, wait3, wait4,
    t1, pp, a1, s1, a2, s2, a3, s3, c4, c3, c2, c1,
):
    lane = iota((16, 128), 1)
    x = []
    for o in range(3):
        tiles = [recv_ref[pl.ds(3 * t + o, 16, stride=24), :] for t in range(7)]
        first, last = tiles[0], tiles[6]
        tiles[0] = first + jnp.where((lane >= W) & (lane < 2 * W), down1(last), 0.0)
        tiles[6] = last + jnp.where(lane < W, up1(first), 0.0)
        x.append([rnd(v) for v in tiles])
    halves = {}
    for m in range(16):
        s = 1 - m % 2
        for o in range(3):
            q = s * 3 + o
            halves[m, q] = place(x[o], lane, W * (m + 1), (q % 2) * 64)
    for i in range(9):
        piece = {}
        for q in range(6):
            m = 2 * i - 1 if q < 3 else 2 * i
            if m == -1:
                piece[q] = down1(halves[15, q])
            elif m == 16:
                piece[q] = up1(halves[0, q])
            else:
                piece[q] = halves[m, q]
        for j in range(3):
            pp[i, :, j * 128 : j * 128 + 128] = (piece[2 * j] + piece[2 * j + 1]).astype(BF16)
    lhs = jnp.concatenate([pp[0:8].reshape(128, 384), pp[1:9].reshape(128, 384)], 1)
    for v in range(13):
        pre = dot(lhs, t1[:, v * 128 : v * 128 + 128])
        act, slope = silu_pair(pre)
        s1[:, v] = slope.reshape(8, 16, 128)
        a1[1:9, v] = act.astype(BF16).reshape(8, 16, 128)
        a1[0, v] = down1(rows16(act, 7)).astype(BF16)
        a1[9, v] = up1(rows16(act, 0)).astype(BF16)
    wait2()
    zero = jnp.zeros((16, 128), BF16)
    for m in range(6):
        a2[m, 0, 0] = zero
        a2[m, 1, 6] = zero
        c2[m, 0] = zero
        c2[m, 13] = zero
    for m in range(4):
        lhs = jnp.concatenate(
            [a1[2 * m + a, k : k + 12].reshape(192, 128) for a in range(4) for k in range(2)], 1
        )
        pre = dot(lhs, w2_ref[...].reshape(1024, 128))
        act, slope = silu_pair(pre)
        s2[m] = slope.reshape(12, 16, 128)
        for c in range(12):
            v = rows16(act, c)
            e, p = (c + 1) % 2, (c + 1) // 2
            a2[m + 1, e, p] = v.astype(BF16)
            if m == 3:
                a2[0, e, p] = down1(v).astype(BF16)
            if m == 0:
                a2[5, e, p] = up1(v).astype(BF16)
    wait3()
    zero = jnp.zeros((16, 256), BF16)
    for k in range(5):
        a3[k, 0] = zero
        a3[k, 7] = zero
    for k in range(4):
        c3[k, 0] = zero
        c3[k, 7] = zero
    acc = None
    for a in range(4):
        lhs = jnp.concatenate(
            [
                jnp.concatenate(
                    [a2[2 * m + a, b % 2, b // 2 : b // 2 + 6].reshape(96, 128) for m in range(2)], 0
                )
                for b in range(4)
            ],
            1,
        )
        term = dot(lhs, w3_ref[a * 4 : a * 4 + 4].reshape(512, 256))
        acc = term if acc is None else acc + term
    act, slope = silu_pair(acc)
    s3[...] = slope.reshape(2, 6, 16, 256)
    for c in range(6):
        v0, v1 = rows16(act, c), rows16(act, 6 + c)
        a3[0, c + 1] = down1(v1).astype(BF16)
        a3[1, c + 1] = v0.astype(BF16)
        a3[2, c + 1] = v1.astype(BF16)
        a3[3, c + 1] = up1(v0).astype(BF16)
        a3[4, c + 1] = up1(v1).astype(BF16)
    wait4()
    acc = None
    for a in range(4):
        lhs = jnp.concatenate(
            [
                jnp.concatenate([a3[m + a, b : b + 5].reshape(80, 256) for m in range(2)], 0)
                for b in range(4)
            ],
            1,
        )
        term = dot(lhs, w4_ref[a * 4 : a * 4 + 4].reshape(1024, 512))
        acc = term if acc is None else acc + term
    _, slope = silu_pair(acc)
    rr = iota((160, 16), 0)
    tap = iota((160, 16), 1)
    y4 = 2 * (rr % 16) + rr // 80
    x4 = (rr % 80) // 16
    py = y4 + 1 - tap // 4
    px = x4 + 1 - tap % 4
    ok = (py >= 0) & (py <= 29) & (px >= 0) & (px <= 3) & (y4 <= 30)
    mask = jnp.where(ok, -SCALE, 0.0).astype(BF16)
    head = jnp.concatenate([head_ref[a].astype(F32) for a in range(4)], 0).astype(BF16)
    cot = dot(mask, head) * slope
    zero = jnp.zeros((16, 512), BF16)
    for k in range(5):
        for c in (0, 1, 7, 8):
            c4[k, c] = zero
    for c in range(5):
        v0, v1 = rows16(cot, c), rows16(cot, 5 + c)
        c4[0, c + 2] = down1(v0).astype(BF16)
        c4[1, c + 2] = down1(v1).astype(BF16)
        c4[2, c + 2] = v0.astype(BF16)
        c4[3, c + 2] = v1.astype(BF16)
        c4[4, c + 2] = up1(v0).astype(BF16)
    acc = None
    for a in range(4):
        for b in range(4):
            lhs = jnp.concatenate(
                [c4[m + 3 - a, 3 - b : 9 - b].reshape(96, 512) for m in range(2)], 0
            )
            term = dot(lhs, w4_ref[a * 4 + b], NT)
            acc = term if acc is None else acc + term
    cot = acc * s3[...].reshape(192, 256)
    for c in range(6):
        v0, v1 = rows16(cot, c), rows16(cot, 6 + c)
        c3[0, c + 1] = down1(v1).astype(BF16)
        c3[1, c + 1] = v0.astype(BF16)
        c3[2, c + 1] = v1.astype(BF16)
        c3[3, c + 1] = up1(v0).astype(BF16)
    for first in (0, 1):
        rows = (1, 3) if first == 0 else (0, 2)
        for e in range(2):
            p0 = 1 - e
            acc = None
            for a in (first, first + 2):
                for b in (e, e + 2):
                    lo = p0 + 1 - b // 2
                    lhs = jnp.concatenate(
                        [c3[(m + 1 - a) // 2 + 1, lo : lo + 6].reshape(96, 256) for m in rows], 0
                    )
                    term = dot(lhs, w3_ref[a * 4 + b], NT)
                    acc = term if acc is None else acc + term
            for n, m in enumerate(rows):
                for p in range(6):
                    c = 2 * (p0 + p) + e - 1
                    v = rows16(acc, n * 6 + p) * s2[m, c]
                    c2[m + 1, c + 1] = v.astype(BF16)
                    if m == 3:
                        c2[0, c + 1] = down1(v).astype(BF16)
                    if m == 0:
                        c2[5, c + 1] = up1(v).astype(BF16)
    for first in (0, 1):
        rhs = jnp.concatenate(
            [w2_ref[a, h * 128 : h * 128 + 128] for a in (first, first + 2) for h in range(2)], 1
        )
        for i in range(4):
            m = 2 * i + 1 - first
            lhs = jnp.concatenate(
                [
                    c2[(m + 1 - a) // 2 + 1, 1 - h : 14 - h].reshape(208, 128)
                    for a in (first, first + 2)
                    for h in range(2)
                ],
                1,
            )
            cot = dot(lhs, rhs, NT) * s1[m].reshape(208, 128)
            for v in range(13):
                c1[m * 16 : m * 16 + 16, v * 128 : v * 128 + 128] = rows16(cot, v).astype(BF16)
    grad = dot(c1[...], t1[...], NT)
    halves = {}
    for j in range(3):
        ps = []
        for i in range(9):
            v = None
            if i <= 7:
                v = grad[i * 16 : i * 16 + 16, j * 128 : j * 128 + 128]
            if i >= 1:
                u = grad[(i - 1) * 16 : i * 16, 384 + j * 128 : 512 + j * 128]
                v = u if v is None else v + u
            ps.append(v)
        for h in range(2):
            q = 2 * j + h
            for i in range(9):
                m = 2 * i - 1 if q < 3 else 2 * i
                if 0 <= m <= 15:
                    v = ps[i]
                    if m == 15:
                        v = v + up1(ps[0])
                    if m == 0:
                        v = v + down1(ps[8])
                    halves[m, q] = rnd(v)
    for o in range(3):
        tiles = [jnp.zeros((16, 128), F32) for _ in range(7)]
        for m in range(16):
            q = (1 - m % 2) * 3 + o
            spread(tiles, lane, halves[m, q], (q % 2) * 64, W * (m + 1))
        first, last = tiles[0], tiles[6]
        tiles[0] = first + jnp.where(lane < W, down1(last), 0.0)
        tiles[6] = last + jnp.where((lane >= W) & (lane < 2 * W), up1(first), 0.0)
        for t in range(7):
            out_ref[pl.ds(3 * t + o, 16, stride=24), :] = tiles[t]
    for k in range(21, 24):
        out_ref[pl.ds(k, 16, stride=24), :] = jnp.zeros((16, 128), F32)

def edge_mask(v, b, col):
    if b == 0:
        return jnp.where(col <= W - 2, v, 0.0)
    if b == 2:
        return jnp.where(col >= 1, v, 0.0)
    return v


def shifted(g, col):
    rows = []
    for ab in range(9):
        a, b = ab // 3, ab % 3
        rows.append(edge_mask(lroll(g, -((2 - a) * W + 1 - b))[:, 0:768], b, col))
    rows.append(jnp.zeros((56, 768), F32))
    return jnp.concatenate(rows, 0).astype(BF16)


def compact(dst, acc):
    dst[...] = jnp.zeros_like(dst)
    for ab in range(9):
        k = ab * 8
        dst[ab * 3 : ab * 3 + 3, :] = acc[k : k + 3, 0:128] + acc[k + 4 : k + 7, 128:256]


class Gather:
    def __init__(self, axis, count, buf, send, got):
        me = lax.axis_index(axis)
        self.buf, self.me, self.count = buf, me, count
        self.copies = [
            pltpu.make_async_remote_copy(
                src_ref=buf.at[me],
                dst_ref=buf.at[me],
                send_sem=send.at[d],
                recv_sem=got.at[d],
                device_id={axis: lax.rem(me + d, count)},
                device_id_type=MESH,
            )
            for d in range(1, count)
        ]

    def start(self, value):
        self.buf[self.me] = value
        for c in self.copies:
            c.start()

    def finish(self):
        for c in self.copies:
            c.wait()
        parts = [self.buf[k] for k in range(self.count)]
        while len(parts) > 1:
            parts = [a + b for a, b in zip(parts[::2], parts[1::2])]
        return parts[0]


def row_exchange(src, dst, send, got, own):
    r = lax.axis_index("row")
    local = pltpu.make_async_copy(src.at[r], dst.at[r], own)
    copies = [local]
    for d in range(1, FR):
        peer = lax.rem(r + d, FR)
        copies.append(
            pltpu.make_async_remote_copy(
                src_ref=src.at[peer],
                dst_ref=dst.at[r],
                send_sem=send.at[d],
                recv_sem=got.at[d],
                device_id={"row": peer},
                device_id_type=MESH,
            )
        )
    return copies


def edge_exchange(src, dst, send, got):
    r = lax.axis_index("row")
    return [
        pltpu.make_async_remote_copy(
            src_ref=src.at[k],
            dst_ref=dst.at[1 - k],
            send_sem=send.at[k],
            recv_sem=got.at[k],
            device_id={"row": lax.rem(r + d, FR)},
            device_id_type=MESH,
        )
        for d, k in ((FR - 1, 0), (1, 1))
    ]


def start_all(copies):
    for c in copies:
        c.start()


def wait_all(copies):
    for c in copies:
        c.wait()


def core_body(
    clips,
    w_ref, f_hbm, t_ref, w1_ref, w2_hbm, w3_hbm, w4_hbm, head_ref,
    sums_ref, gt_hbm, back_ref,
    fs, w2s, w3s, w4s, wm, parts, edges, recv, nb, wide, want, rec, redges, ne, msg, gan,
    gg, gts, xsum, clip_buf, row_buf,
    t1, pp, a1, s1, a2, s2, a3, s3, c4, c3, c2, c1,
    fsem, wsem, gsem, own, send0, got0, send1, got1, esend0, egot0, esend1, egot1,
    csend, cgot, rsend, rgot,
):
    r = lax.axis_index("row")
    clip = lax.axis_index("clip")
    barrier = pltpu.get_barrier_semaphore()
    for d in range(1, FR):
        pl.semaphore_signal(
            barrier, inc=1, device_id={"row": lax.rem(r + d, FR)}, device_id_type=MESH
        )
    for d in range(1, clips):
        pl.semaphore_signal(
            barrier, inc=1, device_id={"clip": lax.rem(clip + d, clips)}, device_id_type=MESH
        )
    loads = [pltpu.make_async_copy(f_hbm.at[f], fs.at[f], fsem.at[f]) for f in range(FR)]
    for p in range(8):
        loads[p].start()
        loads[p + 8].start()
    weights = [
        pltpu.make_async_copy(a, b, wsem.at[k])
        for k, (a, b) in enumerate(((w2_hbm, w2s), (w3_hbm, w3s), (w4_hbm, w4s)))
    ]
    start_all(weights)

    wm[...] = jnp.zeros_like(wm)
    for ab in range(9):
        v = w_ref[ab // 3, ab % 3].astype(F32)
        wm[ab * 8 : ab * 8 + 3, 0:128] = v
        wm[ab * 8 + 4 : ab * 8 + 7, 128:256] = v
    wmb = wm[...].astype(BF16)
    col = iota((8, 768), 1) % W
    lane = iota((16, 128), 1)
    pad = jnp.zeros((8, 128), F32)
    for k in range(21, 24):
        parts[:, k, :] = jnp.zeros((FR, 128), F32)

    def pair_features(p):
        return jnp.concatenate([fs[p].reshape(768, 128), fs[p + 8].reshape(768, 128)], 1)

    for p in range(8):
        loads[p].wait()
        loads[p + 8].wait()
        out = dot(wmb, pair_features(p), NT)
        total = None
        for ab in range(9):
            a, b = ab // 3, ab % 3
            g = edge_mask(out[ab * 8 : ab * 8 + 8, :], b, col)
            g = lroll(jnp.concatenate([g, pad], 1), (2 - a) * W + 1 - b)
            total = g if total is None else total + g
        for h in range(2):
            f = p + 8 * h
            for t in range(7):
                tile = total[4 * h : 4 * h + 3, t * 128 : t * 128 + 128]
                parts[f, 3 * t : 3 * t + 3, :] = tile
                if t in (0, 6):
                    for o in range(3):
                        edges[t // 6, o, f : f + 1, :] = tile[o : o + 1, :]
    pl.semaphore_wait(barrier, FR + clips - 2)
    first = row_exchange(parts, recv, send0, got0, own.at[0])
    ends = edge_exchange(edges, nb, esend0, egot0)
    start_all(ends)
    start_all(first)

    build_band(w1_ref, t1)
    wide[:, 0:W] = t_ref[...].astype(F32)
    for o in range(3):
        tiles = [jnp.zeros((16, 128), F32) for _ in range(7)]
        for y in range(16):
            spread(tiles, lane, wide[pl.ds(o * 16 + y, 16, stride=48), :], 0, W * (y + 1))
        for t in range(7):
            want[t, o] = tiles[t]
    flat = parts.reshape(FR * 24, 128)
    wait_all(ends)
    for o in range(3):
        for t in range(7):
            v = flat[pl.ds(3 * t + o, 16, stride=24), :]
            if t == 0:
                v = v + jnp.where((lane >= W) & (lane < 2 * W) & (r > 0), nb[0, o], 0.0)
            if t == 6:
                v = v + jnp.where((lane < W) & (r < FR - 1), nb[1, o], 0.0)
            v = SCALE * (v - want[t, o])
            if t == 0:
                v = jnp.where(lane >= W, v, 0.0)
            if t == 6:
                v = jnp.where(lane < W, v, 0.0)
            rec[t, o] = v
            if t in (0, 6):
                redges[t // 6, o] = v
    rends = edge_exchange(redges, ne, esend1, egot1)
    start_all(rends)
    wait_all(first)

    disc_stage(
        recv.reshape(FR * 24, 128), w2s, w3s, w4s, head_ref, msg.reshape(FR * 24, 128),
        weights[0].wait, weights[1].wait, weights[2].wait,
        t1, pp, a1, s1, a2, s2, a3, s3, c4, c3, c2, c1,
    )
    second = row_exchange(msg, gan, send1, got1, own.at[1])
    start_all(second)

    gg[...] = jnp.zeros_like(gg)
    wait_all(rends)

    def put(k, t, o, v):
        gg[k, pl.ds(t * 8 + o, 8, stride=56), :] = v[0:8]
        gg[k, pl.ds(t * 8 + 4 + o, 8, stride=56), :] = v[8:16]

    for o in range(3):
        for t in range(7):
            v = rec[t, o]
            if t == 0:
                v = v + jnp.where((lane < W) & (r > 0), ne[0, o], 0.0)
            if t == 6:
                v = v + jnp.where((lane >= W) & (lane < 2 * W) & (r < FR - 1), ne[1, o], 0.0)
            put(0, t, o, v)

    def weight_part(k, p, acc):
        g = jnp.concatenate([gg[k, p * 56 + t * 8 : p * 56 + t * 8 + 8, :] for t in range(7)], 1)
        gt = shifted(g, col)
        gts[p, :, k * 128 : k * 128 + 128] = gt.T
        term = dot(gt[0:80], pair_features(p))
        return term if acc is None else acc + term

    acc = None
    for p in range(8):
        acc = weight_part(0, p, acc)
    compact(xsum, acc)
    rec_clip = Gather("clip", clips, clip_buf.at[0], csend.at[0], cgot.at[0])
    rec_row = Gather("row", FR, row_buf.at[0], rsend.at[0], rgot.at[0])
    gan_clip = Gather("clip", clips, clip_buf.at[1], csend.at[1], cgot.at[1])
    gan_row = Gather("row", FR, row_buf.at[1], rsend.at[1], rgot.at[1])
    rec_clip.start(xsum[...])

    wait_all(second)
    flat = gan.reshape(FR * 24, 128)
    for o in range(3):
        for t in range(7):
            put(1, t, o, flat[pl.ds(3 * t + o, 16, stride=24), :])
    acc = None
    for p in range(8):
        acc = weight_part(1, p, acc)
    compact(xsum, acc)
    gan_clip.start(xsum[...])
    stores = [pltpu.make_async_copy(gts.at[p], gt_hbm.at[p], gsem.at[p]) for p in range(8)]
    start_all(stores)
    rec_row.start(rec_clip.finish())
    for o in range(3):
        tiles = [flat[pl.ds(3 * t + o, 16, stride=24), :] for t in range(7)]
        for y in range(16):
            wide[pl.ds(o * 16 + y, 16, stride=48), :] = place(tiles, lane, W * (y + 1), 0)
    back_ref[...] = wide[:, 0:W].astype(BF16)
    gan_row.start(gan_clip.finish())
    sums_ref[0:32] = rec_row.finish()
    sums_ref[32:64] = gan_row.finish()
    wait_all(stores)


def core(clips, conv_weight, features, target, w1, w2, w3, w4, head):
    anyspec = lambda: pl.BlockSpec(memory_space=pl.ANY)
    dma = pltpu.SemaphoreType.DMA
    return pl.pallas_call(
        functools.partial(core_body, clips),
        out_shape=(
            jax.ShapeDtypeStruct((64, 128), F32),
            jax.ShapeDtypeStruct((8, 768, 256), BF16),
            jax.ShapeDtypeStruct((768, W), BF16),
        ),
        in_specs=[vspec(), anyspec(), vspec(), vspec(), anyspec(), anyspec(), anyspec(), vspec()],
        out_specs=(vspec(), anyspec(), vspec()),
        scratch_shapes=[
            VM((FR, 16, W, 128), BF16),
            VM((4, 256, 128), BF16),
            VM((16, 128, 256), BF16),
            VM((16, 256, 512), BF16),
            VM((80, 256), F32),
            VM((FR, 24, 128), F32),
            VM((2, 3, FR, 128), F32),
            VM((FR, 24, 128), F32),
            VM((2, 3, FR, 128), F32),
            VM((768, 128), F32),
            VM((7, 3, FR, 128), F32),
            VM((7, 3, FR, 128), F32),
            VM((2, 3, FR, 128), F32),
            VM((2, 3, FR, 128), F32),
            VM((FR, 24, 128), F32),
            VM((FR, 24, 128), F32),
            VM((2, 448, 128), F32),
            VM((8, 768, 256), BF16),
            VM((32, 128), F32),
            VM((2, clips, 32, 128), F32),
            VM((2, FR, 32, 128), F32),
            VM((768, 1664), BF16),
            VM((9, 16, 384), BF16),
            VM((10, 13, 16, 128), BF16),
            VM((8, 13, 16, 128), F32),
            VM((6, 2, 7, 16, 128), BF16),
            VM((4, 12, 16, 128), F32),
            VM((5, 8, 16, 256), BF16),
            VM((2, 6, 16, 256), F32),
            VM((5, 9, 16, 512), BF16),
            VM((4, 8, 16, 256), BF16),
            VM((6, 14, 16, 128), BF16),
            VM((128, 1664), BF16),
            dma((FR,)),
            dma((3,)),
            dma((8,)),
            dma((2,)),
            dma((FR,)),
            dma((FR,)),
            dma((FR,)),
            dma((FR,)),
            dma((2,)),
            dma((2,)),
            dma((2,)),
            dma((2,)),
            dma((2, clips)),
            dma((2, clips)),
            dma((2, FR)),
            dma((2, FR)),
        ],
        compiler_params=pltpu.CompilerParams(collective_id=0, has_side_effects=True),
        name="core",
    )(conv_weight, features, target, w1, w2, w3, w4, head)


def final_body(s_ref, w_ref, g_ref, b_ref, out_ref, wg_ref, ad_ref, back_ref, wf, step, pixels):
    i = pl.program_id(0)

    @pl.when(i == 0)
    def _():
        rec, gan = s_ref[0:32], s_ref[32:64]
        adaptive = jnp.sqrt(jnp.sum(rec * rec, keepdims=True)) / (
            jnp.sqrt(jnp.sum(gan * gan, keepdims=True)) + EPS
        )
        ad_ref[...] = adaptive
        wf[...] = jnp.zeros_like(wf)
        for ab in range(9):
            w = w_ref[ab // 3, ab % 3].astype(F32)
            k = ab * 8
            wf[k : k + 3, 0:128] = w
            wf[k + 4 : k + 7, 128:256] = w
            wf[128 + k : 131 + k, 0:128] = adaptive * w
            wf[132 + k : 135 + k, 128:256] = adaptive * w
        mixed = (rec + adaptive * gan) / pixels
        for ab in range(9):
            wg_ref[ab // 3, ab % 3] = mixed[ab * 3 : ab * 3 + 3]
        back_ref[...] = b_ref[...]

    wfb = wf[...].astype(BF16)
    for k in range(step):
        out = dot(g_ref[k], wfb).astype(BF16)
        out_ref[0, k] = out[:, 0:128].reshape(16, W, 128)
        out_ref[1, k] = out[:, 128:256].reshape(16, W, 128)


def final(sums, conv_weight, g, back, pixels):
    step = 2
    full = lambda shape: pl.BlockSpec(shape, lambda i: (0,) * len(shape))
    return pl.pallas_call(
        functools.partial(final_body, step=step, pixels=pixels),
        grid=(8 // step,),
        out_shape=(
            jax.ShapeDtypeStruct((2, 8, 16, W, 128), BF16),
            jax.ShapeDtypeStruct((3, 3, 3, 128), F32),
            jax.ShapeDtypeStruct((1, 1), F32),
            jax.ShapeDtypeStruct((768, W), BF16),
        ),
        in_specs=[
            full((64, 128)),
            full((3, 3, 3, 128)),
            pl.BlockSpec((step, 768, 256), lambda i: (i, 0, 0)),
            full((768, W)),
        ],
        out_specs=(
            pl.BlockSpec((2, step, 16, W, 128), lambda i: (0, i, 0, 0, 0)),
            full((3, 3, 3, 128)),
            full((1, 1)),
            full((768, W)),
        ),
        scratch_shapes=[VM((256, 256), F32)],
        name="final",
    )(sums, conv_weight, g, back)


def per_device(
    features, target, conv_weight, disc_first, disc_second, disc_third, disc_fourth, disc_head
):
    clips = lax.axis_size("clip")
    wanted = jnp.transpose(target[0], (0, 2, 1, 3)).reshape(768, W)
    w1 = jnp.transpose(disc_first, (0, 2, 1, 3))
    w2 = disc_second.reshape(4, 256, 128)
    w3 = disc_third.reshape(16, 128, 256)
    w4 = disc_fourth.reshape(16, 256, 512)
    head = disc_head.reshape(4, 4, 512)
    pixels = float(clips * FR * 256 * W)
    sums, g, back = core(clips, conv_weight, features[0], wanted, w1, w2, w3, w4, head)
    feature_grad, weight_grad, adaptive, back = final(sums, conv_weight, g, back, pixels)
    feature_grad = feature_grad.reshape(1, FR, 16, W, 128)
    image_back = jnp.transpose(back.reshape(1, FR, 3, 16, W), (0, 1, 3, 2, 4))
    return (feature_grad, image_back, weight_grad, adaptive[0, 0])


def solution(mesh):
    return jax.shard_map(
        per_device,
        mesh=mesh,
        in_specs=(
            P("clip", None, "row", None, None),
            P("clip", None, "row", None, None),
            P(),
            P(),
            P(),
            P(),
            P(),
            P(),
        ),
        out_specs=(
            P("clip", None, "row", None, None),
            P("clip", None, "row", None, None),
            P(),
            P(),
        ),
        check_vma=False,
    )
```

```python
import functools

import jax
import jax.numpy as jnp
from jax import lax
from jax.experimental import pallas as pl
from jax.experimental.pallas import tpu as pltpu
from jax.sharding import PartitionSpec as P

MESH = pl.DeviceIdType.MESH
F32 = jnp.float32
BF16 = jnp.bfloat16
SCALE = 64.0
EPS = 0.0001
FR = 16
W = 48
NT = (((1,), (1,)), ((), ()))
TN = (((0,), (0,)), ((), ()))
VM = pltpu.VMEM


def vspec():
    return pl.BlockSpec(memory_space=pltpu.VMEM)


def dot(a, b, dims=(((1,), (0,)), ((), ()))):
    return lax.dot_general(a, b, dims, preferred_element_type=F32)


def iota(shape, dim):
    return lax.broadcasted_iota(jnp.int32, shape, dim)


def rnd(v):
    return v.astype(BF16).astype(F32)


def down1(v):
    return jnp.where(iota(v.shape, 0) >= 1, pltpu.roll(v, 1, 0), 0.0)


def up1(v):
    n = v.shape[0]
    return jnp.where(iota(v.shape, 0) < n - 1, pltpu.roll(v, n - 1, 0), 0.0)


def lroll(v, s):
    s = s % v.shape[1]
    return v if s == 0 else pltpu.roll(v, s, 1)


def place(tiles, lane, src, dst):
    t, off = src // 128, src % 128
    v = lroll(tiles[t], dst - off)
    if off + W > 128:
        v = jnp.where(lane - dst < 128 - off, v, lroll(tiles[t + 1], dst - off))
    return jnp.where((lane >= dst) & (lane < dst + W), v, 0.0)


def spread(tiles, lane, v, src, dst):
    t, off = dst // 128, dst % 128
    v = lroll(jnp.where((lane >= src) & (lane < src + W), v, 0.0), off - src)
    if off + W > 128:
        tiles[t] = tiles[t] + jnp.where(lane >= off, v, 0.0)
        tiles[t + 1] = tiles[t + 1] + jnp.where(lane < off + W - 128, v, 0.0)
    else:
        tiles[t] = tiles[t] + v


def build_band(w1_ref, t1):
    t1[...] = jnp.zeros_like(t1)
    row = iota((16, 128), 0)
    lane = iota((16, 128), 1)
    for ao in range(12):
        w = w1_ref[ao // 3, ao % 3].astype(F32)
        left = jnp.concatenate([w, jnp.zeros((12, 64), F32)], 0)
        patch = jnp.concatenate([left, pltpu.roll(left, 2, 0)], 1)
        for s in (13, 1, 5, 9):
            rolled = pltpu.roll(patch, s, 0)
            parts = [(0, rolled)]
            if s == 13:
                parts = [(0, jnp.where(row >= 13, rolled, 0.0)), (1, jnp.where(row < 13, rolled, 0.0))]
            for v in range(13):
                start = 4 * v - 3
                if start % 16 != s:
                    continue
                for over, tile in parts:
                    g = start // 16 + over
                    if g < 0 or g > 2:
                        continue
                    if v == 0:
                        tile = jnp.where(lane >= 64, tile, 0.0)
                    if v == 12:
                        tile = jnp.where(lane < 64, tile, 0.0)
                    r0 = ao * 64 + g * 16
                    t1[r0 : r0 + 16, v * 128 : v * 128 + 128] = tile.astype(BF16)


def silu_pair(v):
    s = jax.nn.sigmoid(v)
    return v * s, s * (1.0 + v * (1.0 - s))


def rows16(v, k):
    return v[k * 16 : k * 16 + 16]


def disc_stage(
    recv_ref, w2_ref, w3_ref, w4_ref, head_ref, out_ref, wait2, wait3, wait4,
    t1, pp, a1, s1, a2, s2, a3, s3, c4, c3, c2, c1,
):
    lane = iota((16, 128), 1)
    x = []
    for o in range(3):
        tiles = [recv_ref[pl.ds(3 * t + o, 16, stride=24), :] for t in range(7)]
        first, last = tiles[0], tiles[6]
        tiles[0] = first + jnp.where((lane >= W) & (lane < 2 * W), down1(last), 0.0)
        tiles[6] = last + jnp.where(lane < W, up1(first), 0.0)
        x.append([rnd(v) for v in tiles])
    halves = {}
    for m in range(16):
        s = 1 - m % 2
        for o in range(3):
            q = s * 3 + o
            halves[m, q] = place(x[o], lane, W * (m + 1), (q % 2) * 64)
    for i in range(9):
        piece = {}
        for q in range(6):
            m = 2 * i - 1 if q < 3 else 2 * i
            if m == -1:
                piece[q] = down1(halves[15, q])
            elif m == 16:
                piece[q] = up1(halves[0, q])
            else:
                piece[q] = halves[m, q]
        for j in range(3):
            pp[i, :, j * 128 : j * 128 + 128] = (piece[2 * j] + piece[2 * j + 1]).astype(BF16)
    lhs = jnp.concatenate([pp[0:8].reshape(128, 384), pp[1:9].reshape(128, 384)], 1)
    for v in range(13):
        pre = dot(lhs, t1[:, v * 128 : v * 128 + 128])
        act, slope = silu_pair(pre)
        s1[:, v] = slope.reshape(8, 16, 128)
        a1[1:9, v] = act.astype(BF16).reshape(8, 16, 128)
        a1[0, v] = down1(rows16(act, 7)).astype(BF16)
        a1[9, v] = up1(rows16(act, 0)).astype(BF16)
    wait2()
    zero = jnp.zeros((16, 128), BF16)
    for m in range(6):
        a2[m, 0, 0] = zero
        a2[m, 1, 6] = zero
        c2[m, 0] = zero
        c2[m, 13] = zero
    for m in range(4):
        lhs = jnp.concatenate(
            [a1[2 * m + a, k : k + 12].reshape(192, 128) for a in range(4) for k in range(2)], 1
        )
        pre = dot(lhs, w2_ref[...].reshape(1024, 128))
        act, slope = silu_pair(pre)
        s2[m] = slope.reshape(12, 16, 128)
        for c in range(12):
            v = rows16(act, c)
            e, p = (c + 1) % 2, (c + 1) // 2
            a2[m + 1, e, p] = v.astype(BF16)
            if m == 3:
                a2[0, e, p] = down1(v).astype(BF16)
            if m == 0:
                a2[5, e, p] = up1(v).astype(BF16)
    wait3()
    zero = jnp.zeros((16, 256), BF16)
    for k in range(5):
        a3[k, 0] = zero
        a3[k, 7] = zero
    for k in range(4):
        c3[k, 0] = zero
        c3[k, 7] = zero
    acc = None
    for a in range(4):
        lhs = jnp.concatenate(
            [
                jnp.concatenate(
                    [a2[2 * m + a, b % 2, b // 2 : b // 2 + 6].reshape(96, 128) for m in range(2)], 0
                )
                for b in range(4)
            ],
            1,
        )
        term = dot(lhs, w3_ref[a * 4 : a * 4 + 4].reshape(512, 256))
        acc = term if acc is None else acc + term
    act, slope = silu_pair(acc)
    s3[...] = slope.reshape(2, 6, 16, 256)
    for c in range(6):
        v0, v1 = rows16(act, c), rows16(act, 6 + c)
        a3[0, c + 1] = down1(v1).astype(BF16)
        a3[1, c + 1] = v0.astype(BF16)
        a3[2, c + 1] = v1.astype(BF16)
        a3[3, c + 1] = up1(v0).astype(BF16)
        a3[4, c + 1] = up1(v1).astype(BF16)
    wait4()
    acc = None
    for a in range(4):
        lhs = jnp.concatenate(
            [
                jnp.concatenate([a3[m + a, b : b + 5].reshape(80, 256) for m in range(2)], 0)
                for b in range(4)
            ],
            1,
        )
        term = dot(lhs, w4_ref[a * 4 : a * 4 + 4].reshape(1024, 512))
        acc = term if acc is None else acc + term
    _, slope = silu_pair(acc)
    rr = iota((160, 16), 0)
    tap = iota((160, 16), 1)
    y4 = 2 * (rr % 16) + rr // 80
    x4 = (rr % 80) // 16
    py = y4 + 1 - tap // 4
    px = x4 + 1 - tap % 4
    ok = (py >= 0) & (py <= 29) & (px >= 0) & (px <= 3) & (y4 <= 30)
    mask = jnp.where(ok, -SCALE, 0.0).astype(BF16)
    head = jnp.concatenate([head_ref[a].astype(F32) for a in range(4)], 0).astype(BF16)
    cot = dot(mask, head) * slope
    zero = jnp.zeros((16, 512), BF16)
    for k in range(5):
        for c in (0, 1, 7, 8):
            c4[k, c] = zero
    for c in range(5):
        v0, v1 = rows16(cot, c), rows16(cot, 5 + c)
        c4[0, c + 2] = down1(v0).astype(BF16)
        c4[1, c + 2] = down1(v1).astype(BF16)
        c4[2, c + 2] = v0.astype(BF16)
        c4[3, c + 2] = v1.astype(BF16)
        c4[4, c + 2] = up1(v0).astype(BF16)
    acc = None
    for a in range(4):
        lhs = jnp.concatenate(
            [
                jnp.concatenate(
                    [c4[m + 3 - a, 3 - b : 9 - b].reshape(96, 512) for m in range(2)], 0
                )
                for b in range(4)
            ],
            1,
        )
        rhs = jnp.concatenate([w4_ref[a * 4 + b] for b in range(4)], 1)
        term = dot(lhs, rhs, NT)
        acc = term if acc is None else acc + term
    cot = acc * s3[...].reshape(192, 256)
    for c in range(6):
        v0, v1 = rows16(cot, c), rows16(cot, 6 + c)
        c3[0, c + 1] = down1(v1).astype(BF16)
        c3[1, c + 1] = v0.astype(BF16)
        c3[2, c + 1] = v1.astype(BF16)
        c3[3, c + 1] = up1(v0).astype(BF16)
    for first in (0, 1):
        rows = (1, 3) if first == 0 else (0, 2)
        for e in range(2):
            p0 = 1 - e
            taps = [(a, b) for a in (first, first + 2) for b in (e, e + 2)]
            lhs = jnp.concatenate(
                [
                    jnp.concatenate(
                        [
                            c3[(m + 1 - a) // 2 + 1, p0 + 1 - b // 2 : p0 + 7 - b // 2].reshape(96, 256)
                            for m in rows
                        ],
                        0,
                    )
                    for a, b in taps
                ],
                1,
            )
            acc = dot(lhs, jnp.concatenate([w3_ref[a * 4 + b] for a, b in taps], 1), NT)
            for n, m in enumerate(rows):
                for p in range(6):
                    c = 2 * (p0 + p) + e - 1
                    v = rows16(acc, n * 6 + p) * s2[m, c]
                    c2[m + 1, c + 1] = v.astype(BF16)
                    if m == 3:
                        c2[0, c + 1] = down1(v).astype(BF16)
                    if m == 0:
                        c2[5, c + 1] = up1(v).astype(BF16)
    for first in (0, 1):
        rhs = jnp.concatenate(
            [w2_ref[a, h * 128 : h * 128 + 128] for a in (first, first + 2) for h in range(2)], 1
        )
        for i in range(4):
            m = 2 * i + 1 - first
            lhs = jnp.concatenate(
                [
                    c2[(m + 1 - a) // 2 + 1, 1 - h : 14 - h].reshape(208, 128)
                    for a in (first, first + 2)
                    for h in range(2)
                ],
                1,
            )
            cot = dot(lhs, rhs, NT) * s1[m].reshape(208, 128)
            for v in range(13):
                c1[m * 16 : m * 16 + 16, v * 128 : v * 128 + 128] = rows16(cot, v).astype(BF16)
    grad = dot(c1[...], t1[...], NT)
    halves = {}
    for j in range(3):
        ps = []
        for i in range(9):
            v = None
            if i <= 7:
                v = grad[i * 16 : i * 16 + 16, j * 128 : j * 128 + 128]
            if i >= 1:
                u = grad[(i - 1) * 16 : i * 16, 384 + j * 128 : 512 + j * 128]
                v = u if v is None else v + u
            ps.append(v)
        for h in range(2):
            q = 2 * j + h
            for i in range(9):
                m = 2 * i - 1 if q < 3 else 2 * i
                if 0 <= m <= 15:
                    v = ps[i]
                    if m == 15:
                        v = v + up1(ps[0])
                    if m == 0:
                        v = v + down1(ps[8])
                    halves[m, q] = rnd(v)
    for o in range(3):
        tiles = [jnp.zeros((16, 128), F32) for _ in range(7)]
        for m in range(16):
            q = (1 - m % 2) * 3 + o
            spread(tiles, lane, halves[m, q], (q % 2) * 64, W * (m + 1))
        first, last = tiles[0], tiles[6]
        tiles[0] = first + jnp.where(lane < W, down1(last), 0.0)
        tiles[6] = last + jnp.where((lane >= W) & (lane < 2 * W), up1(first), 0.0)
        for t in range(7):
            out_ref[pl.ds(3 * t + o, 16, stride=24), :] = tiles[t]
    for k in range(21, 24):
        out_ref[pl.ds(k, 16, stride=24), :] = jnp.zeros((16, 128), F32)

def edge_mask(v, b, col):
    if b == 0:
        return jnp.where(col <= W - 2, v, 0.0)
    if b == 2:
        return jnp.where(col >= 1, v, 0.0)
    return v


def shifted(g, col):
    rows = []
    for ab in range(9):
        a, b = ab // 3, ab % 3
        rows.append(edge_mask(lroll(g, -((2 - a) * W + 1 - b))[:, 0:768], b, col))
    rows.append(jnp.zeros((8, 768), F32))
    return jnp.concatenate(rows, 0).astype(BF16)


def compact(dst, acc):
    dst[...] = jnp.zeros_like(dst)
    for ab in range(9):
        k = ab * 8
        dst[ab * 3 : ab * 3 + 3, :] = acc[k : k + 3, 0:128] + acc[k + 4 : k + 7, 128:256]


class Gather:
    def __init__(self, axis, count, buf, send, got):
        me = lax.axis_index(axis)
        self.buf, self.me, self.count = buf, me, count
        self.copies = [
            pltpu.make_async_remote_copy(
                src_ref=buf.at[me],
                dst_ref=buf.at[me],
                send_sem=send.at[d],
                recv_sem=got.at[d],
                device_id={axis: lax.rem(me + d, count)},
                device_id_type=MESH,
            )
            for d in range(1, count)
        ]

    def start(self, value):
        self.buf[self.me] = value
        for c in self.copies:
            c.start()

    def finish(self):
        for c in self.copies:
            c.wait()
        parts = [self.buf[k] for k in range(self.count)]
        while len(parts) > 1:
            parts = [a + b for a, b in zip(parts[::2], parts[1::2])]
        return parts[0]


def row_exchange(src, dst, send, got, own):
    r = lax.axis_index("row")
    local = pltpu.make_async_copy(src.at[r], dst.at[r], own)
    copies = [local]
    for d in range(1, FR):
        peer = lax.rem(r + d, FR)
        copies.append(
            pltpu.make_async_remote_copy(
                src_ref=src.at[peer],
                dst_ref=dst.at[r],
                send_sem=send.at[d],
                recv_sem=got.at[d],
                device_id={"row": peer},
                device_id_type=MESH,
            )
        )
    return copies


def edge_exchange(src, dst, send, got):
    r = lax.axis_index("row")
    return [
        pltpu.make_async_remote_copy(
            src_ref=src.at[k],
            dst_ref=dst.at[1 - k],
            send_sem=send.at[k],
            recv_sem=got.at[k],
            device_id={"row": lax.rem(r + d, FR)},
            device_id_type=MESH,
        )
        for d, k in ((FR - 1, 0), (1, 1))
    ]


def start_all(copies):
    for c in copies:
        c.start()


def wait_all(copies):
    for c in copies:
        c.wait()


def core_body(
    clips,
    w_hbm, f_hbm, t_hbm, w1_hbm, w2_hbm, w3_hbm, w4_hbm, head_hbm,
    sums_ref, a_ref, b_ref, back_ref,
    fs, w_ref, t_ref, w1_ref, w2s, w3s, w4s, head_ref, wm, parts, edges, recv, nb, wide, want, rec, redges, ne, msg, gan,
    gg, xsum, clip_buf, row_buf,
    t1, pp, a1, s1, a2, s2, a3, s3, c4, c3, c2, c1,
    fsem, wsem, own, send0, got0, send1, got1, esend0, egot0, esend1, egot1,
    csend, cgot, rsend, rgot,
):
    r = lax.axis_index("row")
    clip = lax.axis_index("clip")
    barrier = pltpu.get_barrier_semaphore()
    for d in range(1, FR):
        pl.semaphore_signal(
            barrier, inc=1, device_id={"row": lax.rem(r + d, FR)}, device_id_type=MESH
        )
    for d in range(1, clips):
        pl.semaphore_signal(
            barrier, inc=1, device_id={"clip": lax.rem(clip + d, clips)}, device_id_type=MESH
        )
    loads = [pltpu.make_async_copy(f_hbm.at[f], fs.at[f], fsem.at[f]) for f in range(FR)]
    weights = [
        pltpu.make_async_copy(a, b, wsem.at[k])
        for k, (a, b) in enumerate(
            (
                (w2_hbm, w2s), (w3_hbm, w3s), (w4_hbm, w4s), (head_hbm, head_ref),
                (w1_hbm, w1_ref), (t_hbm, t_ref), (w_hbm, w_ref),
            )
        )
    ]
    weights[6].start()
    for p in range(8):
        loads[p].start()
        loads[p + 8].start()
    start_all(weights[3:6])
    weights[6].wait()

    wm[...] = jnp.zeros_like(wm)
    for ab in range(9):
        v = w_ref[ab // 3, ab % 3].astype(F32)
        wm[ab * 8 : ab * 8 + 3, 0:128] = v
        wm[ab * 8 + 4 : ab * 8 + 7, 128:256] = v
    wmb = wm[...].astype(BF16)
    col = iota((8, 768), 1) % W
    lane = iota((16, 128), 1)
    pad = jnp.zeros((8, 128), F32)
    for k in range(21, 24):
        parts[:, k, :] = jnp.zeros((FR, 128), F32)

    def pair_features(p):
        return jnp.concatenate([fs[p].reshape(768, 128), fs[p + 8].reshape(768, 128)], 1)

    for p in range(8):
        loads[p].wait()
        loads[p + 8].wait()
        if p == 5:
            start_all(weights[0:3])
        out = dot(wmb, pair_features(p), NT)
        total = None
        for ab in range(9):
            a, b = ab // 3, ab % 3
            g = edge_mask(out[ab * 8 : ab * 8 + 8, :], b, col)
            g = lroll(jnp.concatenate([g, pad], 1), (2 - a) * W + 1 - b)
            total = g if total is None else total + g
        for h in range(2):
            f = p + 8 * h
            for t in range(7):
                tile = total[4 * h : 4 * h + 3, t * 128 : t * 128 + 128]
                parts[f, 3 * t : 3 * t + 3, :] = tile
                if t in (0, 6):
                    for o in range(3):
                        edges[t // 6, o, f : f + 1, :] = tile[o : o + 1, :]
    pl.semaphore_wait(barrier, FR + clips - 2)
    first = row_exchange(parts, recv, send0, got0, own.at[0])
    ends = edge_exchange(edges, nb, esend0, egot0)
    start_all(ends)
    start_all(first)

    weights[4].wait()
    build_band(w1_ref, t1)
    weights[5].wait()
    wide[:, 0:W] = t_ref[...].astype(F32)
    for o in range(3):
        tiles = [jnp.zeros((16, 128), F32) for _ in range(7)]
        for y in range(16):
            spread(tiles, lane, wide[pl.ds(o * 16 + y, 16, stride=48), :], 0, W * (y + 1))
        for t in range(7):
            want[t, o] = tiles[t]
    flat = parts.reshape(FR * 24, 128)
    wait_all(ends)
    for o in range(3):
        for t in range(7):
            v = flat[pl.ds(3 * t + o, 16, stride=24), :]
            if t == 0:
                v = v + jnp.where((lane >= W) & (lane < 2 * W) & (r > 0), nb[0, o], 0.0)
            if t == 6:
                v = v + jnp.where((lane < W) & (r < FR - 1), nb[1, o], 0.0)
            v = SCALE * (v - want[t, o])
            if t == 0:
                v = jnp.where(lane >= W, v, 0.0)
            if t == 6:
                v = jnp.where(lane < W, v, 0.0)
            rec[t, o] = v
            if t in (0, 6):
                redges[t // 6, o] = v
    rends = edge_exchange(redges, ne, esend1, egot1)
    start_all(rends)
    wait_all(first)
    weights[3].wait()

    disc_stage(
        recv.reshape(FR * 24, 128), w2s, w3s, w4s, head_ref, msg.reshape(FR * 24, 128),
        weights[0].wait, weights[1].wait, weights[2].wait,
        t1, pp, a1, s1, a2, s2, a3, s3, c4, c3, c2, c1,
    )
    second = row_exchange(msg, gan, send1, got1, own.at[1])
    start_all(second)

    gg[...] = jnp.zeros_like(gg)
    wait_all(rends)

    def put(k, t, o, v):
        gg[k, pl.ds(t * 8 + o, 8, stride=56), :] = v[0:8]
        gg[k, pl.ds(t * 8 + 4 + o, 8, stride=56), :] = v[8:16]

    for o in range(3):
        for t in range(7):
            v = rec[t, o]
            if t == 0:
                v = v + jnp.where((lane < W) & (r > 0), ne[0, o], 0.0)
            if t == 6:
                v = v + jnp.where((lane >= W) & (lane < 2 * W) & (r < FR - 1), ne[1, o], 0.0)
            put(0, t, o, v)

    def weight_part(k, p, acc, part_ref):
        g = jnp.concatenate([gg[k, p * 56 + t * 8 : p * 56 + t * 8 + 8, :] for t in range(7)], 1)
        gt = shifted(g, col)
        out = dot(gt, wmb, TN)
        part_ref[p] = out[:, 0:128]
        part_ref[p + 8] = out[:, 128:256]
        term = dot(gt, pair_features(p))
        return term if acc is None else acc + term

    acc = None
    for p in range(8):
        acc = weight_part(0, p, acc, a_ref)
    compact(xsum, acc)
    rec_clip = Gather("clip", clips, clip_buf.at[0], csend.at[0], cgot.at[0])
    rec_row = Gather("row", FR, row_buf.at[0], rsend.at[0], rgot.at[0])
    gan_clip = Gather("clip", clips, clip_buf.at[1], csend.at[1], cgot.at[1])
    gan_row = Gather("row", FR, row_buf.at[1], rsend.at[1], rgot.at[1])
    rec_clip.start(xsum[...])

    wait_all(second)
    flat = gan.reshape(FR * 24, 128)
    for o in range(3):
        for t in range(7):
            put(1, t, o, flat[pl.ds(3 * t + o, 16, stride=24), :])
    acc = None
    for p in range(8):
        acc = weight_part(1, p, acc, b_ref)
    compact(xsum, acc)
    gan_clip.start(xsum[...])
    rec_row.start(rec_clip.finish())
    for o in range(3):
        tiles = [flat[pl.ds(3 * t + o, 16, stride=24), :] for t in range(7)]
        for y in range(16):
            wide[pl.ds(o * 16 + y, 16, stride=48), :] = place(tiles, lane, W * (y + 1), 0)
    back_ref[...] = wide[:, 0:W].astype(BF16)
    gan_row.start(gan_clip.finish())
    sums_ref[0:32] = rec_row.finish()
    sums_ref[32:64] = gan_row.finish()


def core(clips, conv_weight, features, target, w1, w2, w3, w4, head):
    hbm = lambda: pl.BlockSpec(memory_space=pltpu.HBM)
    dma = pltpu.SemaphoreType.DMA
    return pl.pallas_call(
        functools.partial(core_body, clips),
        out_shape=(
            VM((64, 128), F32),
            VM((FR, 768, 128), F32),
            VM((FR, 768, 128), F32),
            VM((768, W), BF16),
        ),
        in_specs=[hbm()] * 8,
        out_specs=(vspec(), vspec(), vspec(), vspec()),
        scratch_shapes=[
            VM((FR, 16, W, 128), BF16),
            VM((3, 3, 3, 128), BF16),
            VM((768, W), BF16),
            VM((4, 3, 4, 64), BF16),
            VM((4, 256, 128), BF16),
            VM((16, 128, 256), BF16),
            VM((16, 256, 512), BF16),
            VM((4, 4, 512), BF16),
            VM((80, 256), F32),
            VM((FR, 24, 128), F32),
            VM((2, 3, FR, 128), F32),
            VM((FR, 24, 128), F32),
            VM((2, 3, FR, 128), F32),
            VM((768, 128), F32),
            VM((7, 3, FR, 128), F32),
            VM((7, 3, FR, 128), F32),
            VM((2, 3, FR, 128), F32),
            VM((2, 3, FR, 128), F32),
            VM((FR, 24, 128), F32),
            VM((FR, 24, 128), F32),
            VM((2, 448, 128), F32),
            VM((32, 128), F32),
            VM((2, clips, 32, 128), F32),
            VM((2, FR, 32, 128), F32),
            VM((768, 1664), BF16),
            VM((9, 16, 384), BF16),
            VM((10, 13, 16, 128), BF16),
            VM((8, 13, 16, 128), F32),
            VM((6, 2, 7, 16, 128), BF16),
            VM((4, 12, 16, 128), F32),
            VM((5, 8, 16, 256), BF16),
            VM((2, 6, 16, 256), F32),
            VM((5, 9, 16, 512), BF16),
            VM((4, 8, 16, 256), BF16),
            VM((6, 14, 16, 128), BF16),
            VM((128, 1664), BF16),
            dma((FR,)),
            dma((7,)),
            dma((2,)),
            dma((FR,)),
            dma((FR,)),
            dma((FR,)),
            dma((FR,)),
            dma((2,)),
            dma((2,)),
            dma((2,)),
            dma((2,)),
            dma((2, clips)),
            dma((2, clips)),
            dma((2, FR)),
            dma((2, FR)),
        ],
        compiler_params=pltpu.CompilerParams(
            collective_id=0, has_side_effects=True, vmem_limit_bytes=36 << 20
        ),
        name="core",
    )(
        *(
            pltpu.with_memory_space_constraint(v, pltpu.HBM)
            for v in (conv_weight, features, target, w1, w2, w3, w4, head)
        )
    )


def final_body(pixels, s_ref, a_ref, b_ref, g_ref, out_hbm, wg_ref, ad_ref, back_ref, buf, sem):
    rec, gan = s_ref[0:32], s_ref[32:64]
    adaptive = jnp.sqrt(jnp.sum(rec * rec, keepdims=True)) / (
        jnp.sqrt(jnp.sum(gan * gan, keepdims=True)) + EPS
    )
    scale = jnp.broadcast_to(adaptive, (8, 128))[None]
    stores = []
    for f in range(FR):
        v = a_ref[f].reshape(96, 8, 128) + scale * b_ref[f].reshape(96, 8, 128)
        buf[f] = v.reshape(16, W, 128).astype(BF16)
        copy = pltpu.make_async_copy(buf.at[f], out_hbm.at[f], sem.at[f])
        copy.start()
        stores.append(copy)
    ad_ref[...] = adaptive
    mixed = (rec + adaptive * gan) / pixels
    for ab in range(9):
        wg_ref[ab // 3, ab % 3] = mixed[ab * 3 : ab * 3 + 3]
    back_ref[...] = g_ref[...]
    wait_all(stores)


def final(sums, a, b, back, pixels):
    return pl.pallas_call(
        functools.partial(final_body, pixels),
        out_shape=(
            jax.ShapeDtypeStruct((FR, 16, W, 128), BF16),
            jax.ShapeDtypeStruct((3, 3, 3, 128), F32),
            jax.ShapeDtypeStruct((1, 1), F32),
            jax.ShapeDtypeStruct((768, W), BF16),
        ),
        in_specs=[vspec()] * 4,
        out_specs=(pl.BlockSpec(memory_space=pltpu.HBM), vspec(), vspec(), vspec()),
        scratch_shapes=[VM((FR, 16, W, 128), BF16), pltpu.SemaphoreType.DMA((FR,))],
        compiler_params=pltpu.CompilerParams(vmem_limit_bytes=24 << 20),
        name="final",
    )(sums, a, b, back)


def per_device(
    features, target, conv_weight, disc_first, disc_second, disc_third, disc_fourth, disc_head
):
    clips = lax.axis_size("clip")
    wanted = jnp.transpose(target[0], (0, 2, 1, 3)).reshape(768, W)
    w1 = jnp.transpose(disc_first, (0, 2, 1, 3))
    w2 = disc_second.reshape(4, 256, 128)
    w3 = disc_third.reshape(16, 128, 256)
    w4 = disc_fourth.reshape(16, 256, 512)
    head = disc_head.reshape(4, 4, 512)
    pixels = float(clips * FR * 256 * W)
    sums, a, b, back = core(clips, conv_weight, features[0], wanted, w1, w2, w3, w4, head)
    feature_grad, weight_grad, adaptive, back = final(sums, a, b, back, pixels)
    image_back = jnp.transpose(back.reshape(1, FR, 3, 16, W), (0, 1, 3, 2, 4))
    return (feature_grad[None], image_back, weight_grad, adaptive[0, 0])


def solution(mesh):
    return jax.shard_map(
        per_device,
        mesh=mesh,
        in_specs=(
            P("clip", None, "row", None, None),
            P("clip", None, "row", None, None),
            P(),
            P(),
            P(),
            P(),
            P(),
            P(),
        ),
        out_specs=(
            P("clip", None, "row", None, None),
            P("clip", None, "row", None, None),
            P(),
            P(),
        ),
        check_vma=False,
    )
```

```python
import functools

import jax
import jax.numpy as jnp
from jax import lax
from jax.experimental import pallas as pl
from jax.experimental.pallas import tpu as pltpu
from jax.sharding import PartitionSpec as P

MESH = pl.DeviceIdType.MESH
F32 = jnp.float32
BF16 = jnp.bfloat16
SCALE = 64.0
EPS = 0.0001
FR = 16
W = 48
NT = (((1,), (1,)), ((), ()))
TN = (((0,), (0,)), ((), ()))
VM = pltpu.VMEM


def vspec():
    return pl.BlockSpec(memory_space=pltpu.VMEM)


def dot(a, b, dims=(((1,), (0,)), ((), ()))):
    return lax.dot_general(a, b, dims, preferred_element_type=F32)


def iota(shape, dim):
    return lax.broadcasted_iota(jnp.int32, shape, dim)


def rnd(v):
    return v.astype(BF16).astype(F32)


def down1(v):
    return jnp.where(iota(v.shape, 0) >= 1, pltpu.roll(v, 1, 0), 0.0)


def up1(v):
    n = v.shape[0]
    return jnp.where(iota(v.shape, 0) < n - 1, pltpu.roll(v, n - 1, 0), 0.0)


def lroll(v, s):
    s = s % v.shape[1]
    return v if s == 0 else pltpu.roll(v, s, 1)


def place(tiles, lane, src, dst):
    t, off = src // 128, src % 128
    v = lroll(tiles[t], dst - off)
    if off + W > 128:
        v = jnp.where(lane - dst < 128 - off, v, lroll(tiles[t + 1], dst - off))
    return jnp.where((lane >= dst) & (lane < dst + W), v, 0.0)


def spread(tiles, lane, v, src, dst):
    t, off = dst // 128, dst % 128
    v = lroll(jnp.where((lane >= src) & (lane < src + W), v, 0.0), off - src)
    if off + W > 128:
        tiles[t] = tiles[t] + jnp.where(lane >= off, v, 0.0)
        tiles[t + 1] = tiles[t + 1] + jnp.where(lane < off + W - 128, v, 0.0)
    else:
        tiles[t] = tiles[t] + v


def build_band(w1_ref, t1):
    t1[...] = jnp.zeros_like(t1)
    row = iota((16, 128), 0)
    lane = iota((16, 128), 1)
    for ao in range(12):
        w = w1_ref[ao // 3, ao % 3].astype(F32)
        left = jnp.concatenate([w, jnp.zeros((12, 64), F32)], 0)
        patch = jnp.concatenate([left, pltpu.roll(left, 2, 0)], 1)
        for s in (13, 1, 5, 9):
            rolled = pltpu.roll(patch, s, 0)
            parts = [(0, rolled)]
            if s == 13:
                parts = [(0, jnp.where(row >= 13, rolled, 0.0)), (1, jnp.where(row < 13, rolled, 0.0))]
            for v in range(13):
                start = 4 * v - 3
                if start % 16 != s:
                    continue
                for over, tile in parts:
                    g = start // 16 + over
                    if g < 0 or g > 2:
                        continue
                    if v == 0:
                        tile = jnp.where(lane >= 64, tile, 0.0)
                    if v == 12:
                        tile = jnp.where(lane < 64, tile, 0.0)
                    r0 = ao * 64 + g * 16
                    t1[r0 : r0 + 16, v * 128 : v * 128 + 128] = tile.astype(BF16)


def silu_pair(v):
    s = jax.nn.sigmoid(v)
    return v * s, s * (1.0 + v * (1.0 - s))


def rows16(v, k):
    return v[k * 16 : k * 16 + 16]


def head_term(head_ref, hg):
    rr = iota((160, 16), 0)
    tap = iota((160, 16), 1)
    y4 = 2 * (rr % 16) + rr // 80
    x4 = (rr % 80) // 16
    py = y4 + 1 - tap // 4
    px = x4 + 1 - tap % 4
    ok = (py >= 0) & (py <= 29) & (px >= 0) & (px <= 3) & (y4 <= 30)
    mask = jnp.where(ok, -SCALE, 0.0).astype(BF16)
    head = jnp.concatenate([head_ref[a].astype(F32) for a in range(4)], 0).astype(BF16)
    hg[...] = dot(mask, head)


def disc_stage(
    recv_ref, w2_ref, w3_ref, w4_ref, w4t, t1t, hg, out_ref,
    t1, pp, a1, s1, a2, s2, a3, s3, c4, c3, c2, c1,
):
    lane = iota((16, 128), 1)
    x = []
    for o in range(3):
        tiles = [recv_ref[pl.ds(3 * t + o, 16, stride=24), :] for t in range(7)]
        first, last = tiles[0], tiles[6]
        tiles[0] = first + jnp.where((lane >= W) & (lane < 2 * W), down1(last), 0.0)
        tiles[6] = last + jnp.where(lane < W, up1(first), 0.0)
        x.append([rnd(v) for v in tiles])
    halves = {}
    for m in range(16):
        s = 1 - m % 2
        for o in range(3):
            q = s * 3 + o
            halves[m, q] = place(x[o], lane, W * (m + 1), (q % 2) * 64)
    for i in range(9):
        piece = {}
        for q in range(6):
            m = 2 * i - 1 if q < 3 else 2 * i
            if m == -1:
                piece[q] = down1(halves[15, q])
            elif m == 16:
                piece[q] = up1(halves[0, q])
            else:
                piece[q] = halves[m, q]
        for j in range(3):
            pp[i, :, j * 128 : j * 128 + 128] = (piece[2 * j] + piece[2 * j + 1]).astype(BF16)
    lhs = jnp.concatenate([pp[0:8].reshape(128, 384), pp[1:9].reshape(128, 384)], 1)
    for v0 in range(0, 13, 2):
        n = min(2, 13 - v0)
        pre = dot(lhs, t1[:, v0 * 128 : (v0 + n) * 128])
        for v in range(v0, v0 + n):
            act, slope = silu_pair(pre[:, (v - v0) * 128 : (v - v0 + 1) * 128])
            s1[:, v] = slope.reshape(8, 16, 128)
            a1[1:9, v] = act.astype(BF16).reshape(8, 16, 128)
            a1[0, v] = down1(rows16(act, 7)).astype(BF16)
            a1[9, v] = up1(rows16(act, 0)).astype(BF16)
    zero = jnp.zeros((16, 128), BF16)
    for m in range(6):
        a2[m, 0, 0] = zero
        a2[m, 1, 6] = zero
        c2[m, 0] = zero
        c2[m, 13] = zero
    for m in range(4):
        lhs = jnp.concatenate(
            [a1[2 * m + a, k : k + 12].reshape(192, 128) for a in range(4) for k in range(2)], 1
        )
        pre = dot(lhs, w2_ref[...].reshape(1024, 128))
        act, slope = silu_pair(pre)
        s2[m] = slope.reshape(12, 16, 128)
        for c in range(12):
            v = rows16(act, c)
            e, p = (c + 1) % 2, (c + 1) // 2
            a2[m + 1, e, p] = v.astype(BF16)
            if m == 3:
                a2[0, e, p] = down1(v).astype(BF16)
            if m == 0:
                a2[5, e, p] = up1(v).astype(BF16)
    zero = jnp.zeros((16, 256), BF16)
    for k in range(5):
        a3[k, 0] = zero
        a3[k, 7] = zero
    for k in range(4):
        c3[k, 0] = zero
        c3[k, 7] = zero
    acc = None
    for a in range(4):
        lhs = jnp.concatenate(
            [
                jnp.concatenate(
                    [a2[2 * m + a, b % 2, b // 2 : b // 2 + 6].reshape(96, 128) for m in range(2)], 0
                )
                for b in range(4)
            ],
            1,
        )
        term = dot(lhs, w3_ref[a * 4 : a * 4 + 4].reshape(512, 256))
        acc = term if acc is None else acc + term
    act, slope = silu_pair(acc)
    s3[...] = slope.reshape(2, 6, 16, 256)
    for c in range(6):
        v0, v1 = rows16(act, c), rows16(act, 6 + c)
        a3[0, c + 1] = down1(v1).astype(BF16)
        a3[1, c + 1] = v0.astype(BF16)
        a3[2, c + 1] = v1.astype(BF16)
        a3[3, c + 1] = up1(v0).astype(BF16)
        a3[4, c + 1] = up1(v1).astype(BF16)
    acc = None
    for a in range(4):
        lhs = jnp.concatenate(
            [
                jnp.concatenate([a3[m + a, b : b + 5].reshape(80, 256) for m in range(2)], 0)
                for b in range(4)
            ],
            1,
        )
        term = dot(lhs, w4_ref[a * 4 : a * 4 + 4].reshape(1024, 512))
        acc = term if acc is None else acc + term
    _, slope = silu_pair(acc)
    cot = hg[...] * slope
    zero = jnp.zeros((16, 512), BF16)
    for k in range(5):
        for c in (0, 1, 7, 8):
            c4[k, c] = zero
    for c in range(5):
        v0, v1 = rows16(cot, c), rows16(cot, 5 + c)
        c4[0, c + 2] = down1(v0).astype(BF16)
        c4[1, c + 2] = down1(v1).astype(BF16)
        c4[2, c + 2] = v0.astype(BF16)
        c4[3, c + 2] = v1.astype(BF16)
        c4[4, c + 2] = up1(v0).astype(BF16)
    acc = None
    for a in range(4):
        lhs = jnp.concatenate(
            [
                jnp.concatenate(
                    [c4[m + 3 - a, 3 - b : 9 - b].reshape(96, 512) for m in range(2)], 0
                )
                for b in range(4)
            ],
            1,
        )
        term = dot(lhs, w4t[a * 4 : a * 4 + 4].reshape(2048, 256))
        acc = term if acc is None else acc + term
    cot = acc * s3[...].reshape(192, 256)
    for c in range(6):
        v0, v1 = rows16(cot, c), rows16(cot, 6 + c)
        c3[0, c + 1] = down1(v1).astype(BF16)
        c3[1, c + 1] = v0.astype(BF16)
        c3[2, c + 1] = v1.astype(BF16)
        c3[3, c + 1] = up1(v0).astype(BF16)
    for first in (0, 1):
        rows = (1, 3) if first == 0 else (0, 2)
        for e in range(2):
            p0 = 1 - e
            taps = [(a, b) for a in (first, first + 2) for b in (e, e + 2)]
            lhs = jnp.concatenate(
                [
                    jnp.concatenate(
                        [
                            c3[(m + 1 - a) // 2 + 1, p0 + 1 - b // 2 : p0 + 7 - b // 2].reshape(96, 256)
                            for m in rows
                        ],
                        0,
                    )
                    for a, b in taps
                ],
                1,
            )
            acc = dot(lhs, jnp.concatenate([w3_ref[a * 4 + b] for a, b in taps], 1), NT)
            for n, m in enumerate(rows):
                for p in range(6):
                    c = 2 * (p0 + p) + e - 1
                    v = rows16(acc, n * 6 + p) * s2[m, c]
                    c2[m + 1, c + 1] = v.astype(BF16)
                    if m == 3:
                        c2[0, c + 1] = down1(v).astype(BF16)
                    if m == 0:
                        c2[5, c + 1] = up1(v).astype(BF16)
    for first in (0, 1):
        rhs = jnp.concatenate(
            [w2_ref[a, h * 128 : h * 128 + 128] for a in (first, first + 2) for h in range(2)], 1
        )
        for i in range(4):
            m = 2 * i + 1 - first
            lhs = jnp.concatenate(
                [
                    c2[(m + 1 - a) // 2 + 1, 1 - h : 14 - h].reshape(208, 128)
                    for a in (first, first + 2)
                    for h in range(2)
                ],
                1,
            )
            cot = dot(lhs, rhs, NT) * s1[m].reshape(208, 128)
            for v in range(13):
                c1[m * 16 : m * 16 + 16, v * 128 : v * 128 + 128] = rows16(cot, v).astype(BF16)
    grad = dot(c1[...], t1t[...])
    halves = {}
    for j in range(3):
        ps = []
        for i in range(9):
            v = None
            if i <= 7:
                v = grad[i * 16 : i * 16 + 16, j * 128 : j * 128 + 128]
            if i >= 1:
                u = grad[(i - 1) * 16 : i * 16, 384 + j * 128 : 512 + j * 128]
                v = u if v is None else v + u
            ps.append(v)
        for h in range(2):
            q = 2 * j + h
            for i in range(9):
                m = 2 * i - 1 if q < 3 else 2 * i
                if 0 <= m <= 15:
                    v = ps[i]
                    if m == 15:
                        v = v + up1(ps[0])
                    if m == 0:
                        v = v + down1(ps[8])
                    halves[m, q] = rnd(v)
    for o in range(3):
        tiles = [jnp.zeros((16, 128), F32) for _ in range(7)]
        for m in range(16):
            q = (1 - m % 2) * 3 + o
            spread(tiles, lane, halves[m, q], (q % 2) * 64, W * (m + 1))
        first, last = tiles[0], tiles[6]
        tiles[0] = first + jnp.where(lane < W, down1(last), 0.0)
        tiles[6] = last + jnp.where((lane >= W) & (lane < 2 * W), up1(first), 0.0)
        for t in range(7):
            out_ref[pl.ds(3 * t + o, 16, stride=24), :] = tiles[t]
    for k in range(21, 24):
        out_ref[pl.ds(k, 16, stride=24), :] = jnp.zeros((16, 128), F32)

def edge_mask(v, b, col):
    if b == 0:
        return jnp.where(col <= W - 2, v, 0.0)
    if b == 2:
        return jnp.where(col >= 1, v, 0.0)
    return v


def shifted(g, col):
    rows = []
    for ab in range(9):
        a, b = ab // 3, ab % 3
        rows.append(edge_mask(lroll(g, -((2 - a) * W + 1 - b))[:, 0:768], b, col))
    rows.append(jnp.zeros((8, 768), F32))
    return jnp.concatenate(rows, 0).astype(BF16)


def compact(dst, acc):
    dst[...] = jnp.zeros_like(dst)
    for ab in range(9):
        k = ab * 8
        dst[ab * 3 : ab * 3 + 3, :] = acc[k : k + 3, 0:128] + acc[k + 4 : k + 7, 128:256]


def drain(ref, sem):
    pltpu.make_async_copy(ref, ref, sem).wait()


class Gather:
    def __init__(self, axis, count, buf, send, got):
        me = lax.axis_index(axis)
        self.buf, self.me, self.count, self.sems = buf, me, count, (send, got)
        self.copies = [
            pltpu.make_async_remote_copy(
                src_ref=buf.at[me],
                dst_ref=buf.at[me],
                send_sem=send,
                recv_sem=got,
                device_id={axis: lax.rem(me + d, count)},
                device_id_type=MESH,
            )
            for d in range(1, count)
        ]

    def start(self, value):
        self.buf[self.me] = value
        for c in self.copies:
            c.start()

    def finish(self):
        for sem in self.sems:
            drain(self.buf.at[pl.ds(0, self.count - 1)], sem)
        parts = [self.buf[k] for k in range(self.count)]
        while len(parts) > 1:
            parts = [a + b for a, b in zip(parts[::2], parts[1::2])]
        return parts[0]


class RowExchange:
    def __init__(self, src, dst, send, got):
        r = lax.axis_index("row")
        self.src, self.dst, self.send, self.got = src, dst, send, got
        self.copies = [pltpu.make_async_copy(src.at[r], dst.at[r], got)]
        for d in range(1, FR):
            peer = lax.rem(r + d, FR)
            self.copies.append(
                pltpu.make_async_remote_copy(
                    src_ref=src.at[peer],
                    dst_ref=dst.at[r],
                    send_sem=send,
                    recv_sem=got,
                    device_id={"row": peer},
                    device_id_type=MESH,
                )
            )

    def start(self):
        for c in self.copies:
            c.start()

    def wait(self):
        drain(self.dst, self.got)
        drain(self.src.at[pl.ds(0, FR - 1)], self.send)


class EdgeExchange:
    def __init__(self, src, dst, send, got):
        r = lax.axis_index("row")
        self.src, self.dst, self.send, self.got = src, dst, send, got
        self.copies = [
            pltpu.make_async_remote_copy(
                src_ref=src.at[k],
                dst_ref=dst.at[1 - k],
                send_sem=send,
                recv_sem=got,
                device_id={"row": lax.rem(r + d, FR)},
                device_id_type=MESH,
            )
            for d, k in ((FR - 1, 0), (1, 1))
        ]

    def start(self):
        for c in self.copies:
            c.start()

    def wait(self):
        drain(self.dst, self.got)
        drain(self.src, self.send)


def start_all(copies):
    for c in copies:
        c.start()


def wait_all(copies):
    for c in copies:
        c.wait()


def core_body(
    clips,
    w_hbm, f_hbm, t_hbm, w1_hbm, w2_hbm, w3_hbm, w4_hbm, head_hbm,
    sums_ref, a_ref, b_ref, back_ref,
    fs, w_ref, t_ref, w1_ref, w2s, w3s, w4s, head_ref, wm, parts, edges, recv, nb, wide, want, rec, redges, ne, msg, gan,
    gg, gts, xsum, clip_buf, row_buf, w4t, t1t, hg,
    t1, pp, a1, s1, a2, s2, a3, s3, c4, c3, c2, c1,
    fsem, wsem, xsem,
):
    r = lax.axis_index("row")
    clip = lax.axis_index("clip")
    barrier = pltpu.get_barrier_semaphore()
    for d in range(1, FR):
        pl.semaphore_signal(
            barrier, inc=1, device_id={"row": lax.rem(r + d, FR)}, device_id_type=MESH
        )
    for d in range(1, clips):
        pl.semaphore_signal(
            barrier, inc=1, device_id={"clip": lax.rem(clip + d, clips)}, device_id_type=MESH
        )
    loads = [
        pltpu.make_async_copy(f_hbm.at[pl.ds(4 * k, 4)], fs.at[pl.ds(4 * k, 4)], fsem)
        for k in range(4)
    ]
    weights = [
        pltpu.make_async_copy(a, b, wsem.at[k])
        for k, (a, b) in enumerate(
            (
                (w2_hbm, w2s), (w3_hbm, w3s), (w4_hbm, w4s), (head_hbm, head_ref),
                (w1_hbm, w1_ref), (t_hbm, t_ref), (w_hbm, w_ref),
            )
        )
    ]
    weights[6].start()
    start_all(loads)
    weights[6].wait()

    wm[...] = jnp.zeros_like(wm)
    for ab in range(9):
        v = w_ref[ab // 3, ab % 3].astype(F32)
        wm[ab * 8 : ab * 8 + 3, 0:128] = v
        wm[ab * 8 + 4 : ab * 8 + 7, 128:256] = v
    wmb = wm[...].astype(BF16)
    col = iota((8, 768), 1) % W
    lane = iota((16, 128), 1)
    pad = jnp.zeros((8, 128), F32)
    for k in range(21, 24):
        parts[:, k, :] = jnp.zeros((FR, 128), F32)

    def pair_features(p):
        return jnp.concatenate([fs[p].reshape(768, 128), fs[p + 8].reshape(768, 128)], 1)

    drain(fs, fsem)
    start_all(weights[0:6])
    for p in range(8):
        out = dot(pair_features(p), wmb, NT).T
        total = None
        for ab in range(9):
            a, b = ab // 3, ab % 3
            g = edge_mask(out[ab * 8 : ab * 8 + 8, :], b, col)
            g = lroll(jnp.concatenate([g, pad], 1), (2 - a) * W + 1 - b)
            total = g if total is None else total + g
        for h in range(2):
            f = p + 8 * h
            for t in range(7):
                tile = total[4 * h : 4 * h + 3, t * 128 : t * 128 + 128]
                parts[f, 3 * t : 3 * t + 3, :] = tile
                if t in (0, 6):
                    for o in range(3):
                        edges[t // 6, o, f : f + 1, :] = tile[o : o + 1, :]
    pl.semaphore_wait(barrier, FR + clips - 2)
    first = RowExchange(parts, recv, xsem.at[0], xsem.at[1])
    ends = EdgeExchange(edges, nb, xsem.at[2], xsem.at[3])
    ends.start()
    first.start()

    weights[4].wait()
    build_band(w1_ref, t1)
    weights[5].wait()
    wide[:, 0:W] = t_ref[...].astype(F32)
    for o in range(3):
        tiles = [jnp.zeros((16, 128), F32) for _ in range(7)]
        for y in range(16):
            spread(tiles, lane, wide[pl.ds(o * 16 + y, 16, stride=48), :], 0, W * (y + 1))
        for t in range(7):
            want[t, o] = tiles[t]
    flat = parts.reshape(FR * 24, 128)
    ends.wait()
    for o in range(3):
        for t in range(7):
            v = flat[pl.ds(3 * t + o, 16, stride=24), :]
            if t == 0:
                v = v + jnp.where((lane >= W) & (lane < 2 * W) & (r > 0), nb[0, o], 0.0)
            if t == 6:
                v = v + jnp.where((lane < W) & (r < FR - 1), nb[1, o], 0.0)
            v = SCALE * (v - want[t, o])
            if t == 0:
                v = jnp.where(lane >= W, v, 0.0)
            if t == 6:
                v = jnp.where(lane < W, v, 0.0)
            rec[t, o] = v
            if t in (0, 6):
                redges[t // 6, o] = v
    rends = EdgeExchange(redges, ne, xsem.at[4], xsem.at[5])
    rends.start()
    wait_all(weights[0:4])
    head_term(head_ref, hg)
    for k in range(16):
        w4t[k] = w4s[k].T
    for k in range(6):
        t1t[:, k * 128 : k * 128 + 128] = t1[k * 128 : k * 128 + 128, :].T
    first.wait()

    disc_stage(
        recv.reshape(FR * 24, 128), w2s, w3s, w4s, w4t, t1t, hg, msg.reshape(FR * 24, 128),
        t1, pp, a1, s1, a2, s2, a3, s3, c4, c3, c2, c1,
    )
    second = RowExchange(msg, gan, xsem.at[6], xsem.at[7])
    second.start()

    gg[...] = jnp.zeros_like(gg)
    rends.wait()

    def put(k, t, o, v):
        gg[k, pl.ds(t * 8 + o, 8, stride=56), :] = v[0:8]
        gg[k, pl.ds(t * 8 + 4 + o, 8, stride=56), :] = v[8:16]

    for o in range(3):
        for t in range(7):
            v = rec[t, o]
            if t == 0:
                v = v + jnp.where((lane < W) & (r > 0), ne[0, o], 0.0)
            if t == 6:
                v = v + jnp.where((lane >= W) & (lane < 2 * W) & (r < FR - 1), ne[1, o], 0.0)
            put(0, t, o, v)

    def weight_part(k, p, acc):
        g = jnp.concatenate([gg[k, p * 56 + t * 8 : p * 56 + t * 8 + 8, :] for t in range(7)], 1)
        gt = shifted(g, col)
        gts[p] = gt
        term = dot(gt, pair_features(p))
        return term if acc is None else acc + term

    def feature_part(part_ref):
        for p in range(8):
            out = dot(gts[p], wmb, TN)
            part_ref[p] = out[:, 0:128]
            part_ref[p + 8] = out[:, 128:256]

    acc = None
    for p in range(8):
        acc = weight_part(0, p, acc)
    compact(xsum, acc)
    rec_clip = Gather("clip", clips, clip_buf.at[0], xsem.at[8], xsem.at[9])
    rec_row = Gather("row", FR, row_buf.at[0], xsem.at[10], xsem.at[11])
    gan_clip = Gather("clip", clips, clip_buf.at[1], xsem.at[12], xsem.at[13])
    gan_row = Gather("row", FR, row_buf.at[1], xsem.at[14], xsem.at[15])
    rec_clip.start(xsum[...])
    feature_part(a_ref)

    second.wait()
    flat = gan.reshape(FR * 24, 128)
    for o in range(3):
        for t in range(7):
            put(1, t, o, flat[pl.ds(3 * t + o, 16, stride=24), :])
    acc = None
    for p in range(8):
        acc = weight_part(1, p, acc)
    compact(xsum, acc)
    gan_clip.start(xsum[...])
    rec_row.start(rec_clip.finish())
    feature_part(b_ref)
    for o in range(3):
        tiles = [flat[pl.ds(3 * t + o, 16, stride=24), :] for t in range(7)]
        for y in range(16):
            wide[pl.ds(o * 16 + y, 16, stride=48), :] = place(tiles, lane, W * (y + 1), 0)
    back_ref[...] = wide[:, 0:W].astype(BF16)
    gan_row.start(gan_clip.finish())
    sums_ref[0:32] = rec_row.finish()
    sums_ref[32:64] = gan_row.finish()


def core(clips, conv_weight, features, target, w1, w2, w3, w4, head):
    hbm = lambda: pl.BlockSpec(memory_space=pltpu.HBM)
    dma = pltpu.SemaphoreType.DMA
    return pl.pallas_call(
        functools.partial(core_body, clips),
        out_shape=(
            VM((64, 128), F32),
            VM((FR, 768, 128), F32),
            VM((FR, 768, 128), F32),
            VM((768, W), BF16),
        ),
        in_specs=[hbm()] * 8,
        out_specs=(vspec(), vspec(), vspec(), vspec()),
        scratch_shapes=[
            VM((FR, 16, W, 128), BF16),
            VM((3, 3, 3, 128), BF16),
            VM((768, W), BF16),
            VM((4, 3, 4, 64), BF16),
            VM((4, 256, 128), BF16),
            VM((16, 128, 256), BF16),
            VM((16, 256, 512), BF16),
            VM((4, 4, 512), BF16),
            VM((80, 256), F32),
            VM((FR, 24, 128), F32),
            VM((2, 3, FR, 128), F32),
            VM((FR, 24, 128), F32),
            VM((2, 3, FR, 128), F32),
            VM((768, 128), F32),
            VM((7, 3, FR, 128), F32),
            VM((7, 3, FR, 128), F32),
            VM((2, 3, FR, 128), F32),
            VM((2, 3, FR, 128), F32),
            VM((FR, 24, 128), F32),
            VM((FR, 24, 128), F32),
            VM((2, 448, 128), F32),
            VM((8, 80, 768), BF16),
            VM((32, 128), F32),
            VM((2, clips, 32, 128), F32),
            VM((2, FR, 32, 128), F32),
            VM((16, 512, 256), BF16),
            VM((1664, 768), BF16),
            VM((160, 512), F32),
            VM((768, 1664), BF16),
            VM((9, 16, 384), BF16),
            VM((10, 13, 16, 128), BF16),
            VM((8, 13, 16, 128), F32),
            VM((6, 2, 7, 16, 128), BF16),
            VM((4, 12, 16, 128), F32),
            VM((5, 8, 16, 256), BF16),
            VM((2, 6, 16, 256), F32),
            VM((5, 9, 16, 512), BF16),
            VM((4, 8, 16, 256), BF16),
            VM((6, 14, 16, 128), BF16),
            VM((128, 1664), BF16),
            dma,
            dma((7,)),
            dma((16,)),
        ],
        compiler_params=pltpu.CompilerParams(
            collective_id=0, has_side_effects=True, vmem_limit_bytes=44 << 20
        ),
        name="core",
    )(
        *(
            pltpu.with_memory_space_constraint(v, pltpu.HBM)
            for v in (conv_weight, features, target, w1, w2, w3, w4, head)
        )
    )


def final_body(pixels, s_ref, a_ref, b_ref, g_ref, out_hbm, wg_ref, ad_ref, back_ref, buf, sem):
    rec, gan = s_ref[0:32], s_ref[32:64]
    adaptive = jnp.sqrt(jnp.sum(rec * rec, keepdims=True)) / (
        jnp.sqrt(jnp.sum(gan * gan, keepdims=True)) + EPS
    )
    scale = jnp.broadcast_to(adaptive, (8, 128))[None]
    stores = []
    for f in range(FR):
        v = a_ref[f].reshape(96, 8, 128) + scale * b_ref[f].reshape(96, 8, 128)
        buf[f] = v.reshape(16, W, 128).astype(BF16)
        copy = pltpu.make_async_copy(buf.at[f], out_hbm.at[f], sem.at[f])
        copy.start()
        stores.append(copy)
    ad_ref[...] = adaptive
    mixed = (rec + adaptive * gan) / pixels
    for ab in range(9):
        wg_ref[ab // 3, ab % 3] = mixed[ab * 3 : ab * 3 + 3]
    back_ref[...] = g_ref[...]
    wait_all(stores)


def final(sums, a, b, back, pixels):
    return pl.pallas_call(
        functools.partial(final_body, pixels),
        out_shape=(
            jax.ShapeDtypeStruct((FR, 16, W, 128), BF16),
            jax.ShapeDtypeStruct((3, 3, 3, 128), F32),
            jax.ShapeDtypeStruct((1, 1), F32),
            jax.ShapeDtypeStruct((768, W), BF16),
        ),
        in_specs=[vspec()] * 4,
        out_specs=(pl.BlockSpec(memory_space=pltpu.HBM), vspec(), vspec(), vspec()),
        scratch_shapes=[VM((FR, 16, W, 128), BF16), pltpu.SemaphoreType.DMA((FR,))],
        compiler_params=pltpu.CompilerParams(vmem_limit_bytes=24 << 20),
        name="final",
    )(sums, a, b, back)


def per_device(
    features, target, conv_weight, disc_first, disc_second, disc_third, disc_fourth, disc_head
):
    clips = lax.axis_size("clip")
    wanted = jnp.transpose(target[0], (0, 2, 1, 3)).reshape(768, W)
    w1 = jnp.transpose(disc_first, (0, 2, 1, 3))
    w2 = disc_second.reshape(4, 256, 128)
    w3 = disc_third.reshape(16, 128, 256)
    w4 = disc_fourth.reshape(16, 256, 512)
    head = disc_head.reshape(4, 4, 512)
    pixels = float(clips * FR * 256 * W)
    sums, a, b, back = core(clips, conv_weight, features[0], wanted, w1, w2, w3, w4, head)
    feature_grad, weight_grad, adaptive, back = final(sums, a, b, back, pixels)
    image_back = jnp.transpose(back.reshape(1, FR, 3, 16, W), (0, 1, 3, 2, 4))
    return (feature_grad[None], image_back, weight_grad, adaptive[0, 0])


def solution(mesh):
    return jax.shard_map(
        per_device,
        mesh=mesh,
        in_specs=(
            P("clip", None, "row", None, None),
            P("clip", None, "row", None, None),
            P(),
            P(),
            P(),
            P(),
            P(),
            P(),
        ),
        out_specs=(
            P("clip", None, "row", None, None),
            P("clip", None, "row", None, None),
            P(),
            P(),
        ),
        check_vma=False,
    )
```

```python
import functools

import jax
import jax.numpy as jnp
from jax import lax
from jax.experimental import pallas as pl
from jax.experimental.pallas import tpu as pltpu
from jax.sharding import PartitionSpec as P

MESH = pl.DeviceIdType.MESH
F32 = jnp.float32
BF16 = jnp.bfloat16
SCALE = 64.0
EPS = 0.0001
FR = 16
W = 48
NT = (((1,), (1,)), ((), ()))
TN = (((0,), (0,)), ((), ()))
VM = pltpu.VMEM


def vspec():
    return pl.BlockSpec(memory_space=pltpu.VMEM)


def dot(a, b, dims=(((1,), (0,)), ((), ()))):
    return lax.dot_general(a, b, dims, preferred_element_type=F32)


def iota(shape, dim):
    return lax.broadcasted_iota(jnp.int32, shape, dim)


def rnd(v):
    return v.astype(BF16).astype(F32)


def down1(v):
    return jnp.where(iota(v.shape, 0) >= 1, pltpu.roll(v, 1, 0), 0.0)


def up1(v):
    n = v.shape[0]
    return jnp.where(iota(v.shape, 0) < n - 1, pltpu.roll(v, n - 1, 0), 0.0)


def lroll(v, s):
    s = s % v.shape[1]
    return v if s == 0 else pltpu.roll(v, s, 1)


def place(tiles, lane, src, dst):
    t, off = src // 128, src % 128
    v = lroll(tiles[t], dst - off)
    if off + W > 128:
        v = jnp.where(lane - dst < 128 - off, v, lroll(tiles[t + 1], dst - off))
    return jnp.where((lane >= dst) & (lane < dst + W), v, 0.0)


def spread(tiles, lane, v, src, dst):
    t, off = dst // 128, dst % 128
    v = lroll(jnp.where((lane >= src) & (lane < src + W), v, 0.0), off - src)
    if off + W > 128:
        tiles[t] = tiles[t] + jnp.where(lane >= off, v, 0.0)
        tiles[t + 1] = tiles[t + 1] + jnp.where(lane < off + W - 128, v, 0.0)
    else:
        tiles[t] = tiles[t] + v


def build_band(w1_ref, t1):
    t1[...] = jnp.zeros_like(t1)
    row = iota((16, 128), 0)
    lane = iota((16, 128), 1)
    for ao in range(12):
        w = w1_ref[ao // 3, ao % 3].astype(F32)
        left = jnp.concatenate([w, jnp.zeros((12, 64), F32)], 0)
        patch = jnp.concatenate([left, pltpu.roll(left, 2, 0)], 1)
        for s in (13, 1, 5, 9):
            rolled = pltpu.roll(patch, s, 0)
            parts = [(0, rolled)]
            if s == 13:
                parts = [(0, jnp.where(row >= 13, rolled, 0.0)), (1, jnp.where(row < 13, rolled, 0.0))]
            for v in range(13):
                start = 4 * v - 3
                if start % 16 != s:
                    continue
                for over, tile in parts:
                    g = start // 16 + over
                    if g < 0 or g > 2:
                        continue
                    if v == 0:
                        tile = jnp.where(lane >= 64, tile, 0.0)
                    if v == 12:
                        tile = jnp.where(lane < 64, tile, 0.0)
                    r0 = ao * 64 + g * 16
                    t1[r0 : r0 + 16, v * 128 : v * 128 + 128] = tile.astype(BF16)


def silu_pair(v):
    s = jax.nn.sigmoid(v)
    return v * s, s * (1.0 + v * (1.0 - s))


def rows16(v, k):
    return v[k * 16 : k * 16 + 16]


def head_term(head_ref, hg):
    rr = iota((160, 16), 0)
    tap = iota((160, 16), 1)
    y4 = 2 * (rr % 16) + rr // 80
    x4 = (rr % 80) // 16
    py = y4 + 1 - tap // 4
    px = x4 + 1 - tap % 4
    ok = (py >= 0) & (py <= 29) & (px >= 0) & (px <= 3) & (y4 <= 30)
    mask = jnp.where(ok, -SCALE, 0.0).astype(BF16)
    head = jnp.concatenate([head_ref[a].astype(F32) for a in range(4)], 0).astype(BF16)
    hg[...] = dot(mask, head)


def disc_stage(
    recv_ref, w2_ref, w3_ref, w4_ref, w4t, t1t, hg, out_ref,
    t1, pp, a1, s1, a2, s2, a3, s3, c4, c3, c2, c1,
):
    lane = iota((16, 128), 1)
    x = []
    for o in range(3):
        tiles = [recv_ref[pl.ds(3 * t + o, 16, stride=32), :] for t in range(7)]
        first = tiles[0] + recv_ref[pl.ds(21 + o, 16, stride=32), :]
        last = tiles[6] + recv_ref[pl.ds(24 + o, 16, stride=32), :]
        tiles[0] = first + jnp.where((lane >= W) & (lane < 2 * W), down1(last), 0.0)
        tiles[6] = last + jnp.where(lane < W, up1(first), 0.0)
        x.append([rnd(v) for v in tiles])
    halves = {}
    for m in range(16):
        s = 1 - m % 2
        for o in range(3):
            q = s * 3 + o
            halves[m, q] = place(x[o], lane, W * (m + 1), (q % 2) * 64)
    for i in range(9):
        piece = {}
        for q in range(6):
            m = 2 * i - 1 if q < 3 else 2 * i
            if m == -1:
                piece[q] = down1(halves[15, q])
            elif m == 16:
                piece[q] = up1(halves[0, q])
            else:
                piece[q] = halves[m, q]
        for j in range(3):
            pp[i, :, j * 128 : j * 128 + 128] = (piece[2 * j] + piece[2 * j + 1]).astype(BF16)
    lhs = jnp.concatenate([pp[0:8].reshape(128, 384), pp[1:9].reshape(128, 384)], 1)
    for v0 in range(0, 13, 2):
        n = min(2, 13 - v0)
        pre = dot(lhs, t1[:, v0 * 128 : (v0 + n) * 128])
        for v in range(v0, v0 + n):
            act, slope = silu_pair(pre[:, (v - v0) * 128 : (v - v0 + 1) * 128])
            s1[:, v] = slope.reshape(8, 16, 128)
            a1[1:9, v] = act.astype(BF16).reshape(8, 16, 128)
            a1[0, v] = down1(rows16(act, 7)).astype(BF16)
            a1[9, v] = up1(rows16(act, 0)).astype(BF16)
    zero = jnp.zeros((16, 128), BF16)
    for m in range(6):
        a2[m, 0, 0] = zero
        a2[m, 1, 6] = zero
        c2[m, 0] = zero
        c2[m, 13] = zero
    for m in range(4):
        lhs = jnp.concatenate(
            [a1[2 * m + a, k : k + 12].reshape(192, 128) for a in range(4) for k in range(2)], 1
        )
        pre = dot(lhs, w2_ref[...].reshape(1024, 128))
        act, slope = silu_pair(pre)
        s2[m] = slope.reshape(12, 16, 128)
        for c in range(12):
            v = rows16(act, c)
            e, p = (c + 1) % 2, (c + 1) // 2
            a2[m + 1, e, p] = v.astype(BF16)
            if m == 3:
                a2[0, e, p] = down1(v).astype(BF16)
            if m == 0:
                a2[5, e, p] = up1(v).astype(BF16)
    zero = jnp.zeros((16, 256), BF16)
    for k in range(5):
        a3[k, 0] = zero
        a3[k, 7] = zero
    for k in range(4):
        c3[k, 0] = zero
        c3[k, 7] = zero
    acc = None
    for a in range(4):
        lhs = jnp.concatenate(
            [
                jnp.concatenate(
                    [a2[2 * m + a, b % 2, b // 2 : b // 2 + 6].reshape(96, 128) for m in range(2)], 0
                )
                for b in range(4)
            ],
            1,
        )
        term = dot(lhs, w3_ref[a * 4 : a * 4 + 4].reshape(512, 256))
        acc = term if acc is None else acc + term
    act, slope = silu_pair(acc)
    s3[...] = slope.reshape(2, 6, 16, 256)
    for c in range(6):
        v0, v1 = rows16(act, c), rows16(act, 6 + c)
        a3[0, c + 1] = down1(v1).astype(BF16)
        a3[1, c + 1] = v0.astype(BF16)
        a3[2, c + 1] = v1.astype(BF16)
        a3[3, c + 1] = up1(v0).astype(BF16)
        a3[4, c + 1] = up1(v1).astype(BF16)
    acc = None
    for a in range(4):
        lhs = jnp.concatenate(
            [
                jnp.concatenate([a3[m + a, b : b + 5].reshape(80, 256) for m in range(2)], 0)
                for b in range(4)
            ],
            1,
        )
        term = dot(lhs, w4_ref[a * 4 : a * 4 + 4].reshape(1024, 512))
        acc = term if acc is None else acc + term
    _, slope = silu_pair(acc)
    cot = hg[...] * slope
    zero = jnp.zeros((16, 512), BF16)
    for k in range(5):
        for c in (0, 1, 7, 8):
            c4[k, c] = zero
    for c in range(5):
        v0, v1 = rows16(cot, c), rows16(cot, 5 + c)
        c4[0, c + 2] = down1(v0).astype(BF16)
        c4[1, c + 2] = down1(v1).astype(BF16)
        c4[2, c + 2] = v0.astype(BF16)
        c4[3, c + 2] = v1.astype(BF16)
        c4[4, c + 2] = up1(v0).astype(BF16)
    acc = None
    for a in range(4):
        lhs = jnp.concatenate(
            [
                jnp.concatenate(
                    [c4[m + 3 - a, 3 - b : 9 - b].reshape(96, 512) for m in range(2)], 0
                )
                for b in range(4)
            ],
            1,
        )
        term = dot(lhs, w4t[a * 4 : a * 4 + 4].reshape(2048, 256))
        acc = term if acc is None else acc + term
    cot = acc * s3[...].reshape(192, 256)
    for c in range(6):
        v0, v1 = rows16(cot, c), rows16(cot, 6 + c)
        c3[0, c + 1] = down1(v1).astype(BF16)
        c3[1, c + 1] = v0.astype(BF16)
        c3[2, c + 1] = v1.astype(BF16)
        c3[3, c + 1] = up1(v0).astype(BF16)
    for first in (0, 1):
        rows = (1, 3) if first == 0 else (0, 2)
        for e in range(2):
            p0 = 1 - e
            taps = [(a, b) for a in (first, first + 2) for b in (e, e + 2)]
            lhs = jnp.concatenate(
                [
                    jnp.concatenate(
                        [
                            c3[(m + 1 - a) // 2 + 1, p0 + 1 - b // 2 : p0 + 7 - b // 2].reshape(96, 256)
                            for m in rows
                        ],
                        0,
                    )
                    for a, b in taps
                ],
                1,
            )
            acc = dot(lhs, jnp.concatenate([w3_ref[a * 4 + b] for a, b in taps], 1), NT)
            for n, m in enumerate(rows):
                for p in range(6):
                    c = 2 * (p0 + p) + e - 1
                    v = rows16(acc, n * 6 + p) * s2[m, c]
                    c2[m + 1, c + 1] = v.astype(BF16)
                    if m == 3:
                        c2[0, c + 1] = down1(v).astype(BF16)
                    if m == 0:
                        c2[5, c + 1] = up1(v).astype(BF16)
    for first in (0, 1):
        rhs = jnp.concatenate(
            [w2_ref[a, h * 128 : h * 128 + 128] for a in (first, first + 2) for h in range(2)], 1
        )
        for i in range(4):
            m = 2 * i + 1 - first
            lhs = jnp.concatenate(
                [
                    c2[(m + 1 - a) // 2 + 1, 1 - h : 14 - h].reshape(208, 128)
                    for a in (first, first + 2)
                    for h in range(2)
                ],
                1,
            )
            cot = dot(lhs, rhs, NT) * s1[m].reshape(208, 128)
            for v in range(13):
                c1[m * 16 : m * 16 + 16, v * 128 : v * 128 + 128] = rows16(cot, v).astype(BF16)
    grad = dot(c1[...], t1t[...])
    halves = {}
    for j in range(3):
        ps = []
        for i in range(9):
            v = None
            if i <= 7:
                v = grad[i * 16 : i * 16 + 16, j * 128 : j * 128 + 128]
            if i >= 1:
                u = grad[(i - 1) * 16 : i * 16, 384 + j * 128 : 512 + j * 128]
                v = u if v is None else v + u
            ps.append(v)
        for h in range(2):
            q = 2 * j + h
            for i in range(9):
                m = 2 * i - 1 if q < 3 else 2 * i
                if 0 <= m <= 15:
                    v = ps[i]
                    if m == 15:
                        v = v + up1(ps[0])
                    if m == 0:
                        v = v + down1(ps[8])
                    halves[m, q] = rnd(v)
    for o in range(3):
        tiles = [jnp.zeros((16, 128), F32) for _ in range(7)]
        for m in range(16):
            q = (1 - m % 2) * 3 + o
            spread(tiles, lane, halves[m, q], (q % 2) * 64, W * (m + 1))
        first, last = tiles[0], tiles[6]
        tiles[0] = first + jnp.where(lane < W, down1(last), 0.0)
        tiles[6] = last + jnp.where((lane >= W) & (lane < 2 * W), up1(first), 0.0)
        for t in range(7):
            out_ref[pl.ds(4 * t + o, 16, stride=32), :] = tiles[t]

def edge_mask(v, b, col):
    if b == 0:
        return jnp.where(col <= W - 2, v, 0.0)
    if b == 2:
        return jnp.where(col >= 1, v, 0.0)
    return v


def shifted(g, col):
    rows = []
    for ab in range(9):
        a, b = ab // 3, ab % 3
        rows.append(edge_mask(lroll(g, -((2 - a) * W + 1 - b))[:, 0:768], b, col))
    rows.append(jnp.zeros((8, 768), F32))
    return jnp.concatenate(rows, 0).astype(BF16)


def compact(dst, acc):
    dst[...] = jnp.zeros_like(dst)
    for ab in range(9):
        k = ab * 8
        dst[ab * 3 : ab * 3 + 3, :] = acc[k : k + 3, 0:128] + acc[k + 4 : k + 7, 128:256]


def drain(ref, sem):
    pltpu.make_async_copy(ref, ref, sem).wait()


def hops(d):
    return min(d, 4 - d)


ROW_OFFSETS = sorted(
    ((dy, dz) for dy in range(4) for dz in range(4) if dy or dz),
    key=lambda t: -(hops(t[0]) + hops(t[1])),
)
CLIP_OFFSETS = sorted(
    ((dx, dc) for dx in range(4) for dc in range(2) if dx or dc), key=lambda t: -(2 * hops(t[0]) + t[1])
)


def row_peers():
    r = lax.axis_index("row")
    y, z = r // 4, lax.rem(r, 4)
    return [lax.rem(y + dy, 4) * 4 + lax.rem(z + dz, 4) for dy, dz in ROW_OFFSETS]


def tree(parts):
    while len(parts) > 1:
        parts = [a + b for a, b in zip(parts[::2], parts[1::2])]
    return parts[0]


class Total:
    def __init__(self, src, clip_buf, row_buf, out, sems):
        clip, row = lax.axis_index("clip"), lax.axis_index("row")
        x, core = clip // 2, lax.rem(clip, 2)
        self.src, self.clip_buf, self.row_buf, self.out, self.sems = src, clip_buf, row_buf, out, sems
        self.clip, self.row = clip, row
        self.half = pl.ds(pl.multiple_of(core * 16, 16), 16)
        self.first = []
        for dx, dc in CLIP_OFFSETS:
            other = lax.rem(core + dc, 2)
            self.first.append(
                pltpu.make_async_remote_copy(
                    src_ref=src.at[pl.ds(pl.multiple_of(other * 16, 16), 16)],
                    dst_ref=clip_buf.at[clip],
                    send_sem=sems.at[0],
                    recv_sem=sems.at[1],
                    device_id={"clip": lax.rem(x + dx, 4) * 2 + other},
                    device_id_type=MESH,
                )
            )
        self.second = [
            pltpu.make_async_remote_copy(
                src_ref=row_buf.at[row],
                dst_ref=row_buf.at[row],
                send_sem=sems.at[2],
                recv_sem=sems.at[3],
                device_id={"row": peer},
                device_id_type=MESH,
            )
            for peer in row_peers()
        ]
        self.third = pltpu.make_async_remote_copy(
            src_ref=out.at[self.half],
            dst_ref=out.at[self.half],
            send_sem=sems.at[4],
            recv_sem=sems.at[5],
            device_id={"clip": x * 2 + 1 - core},
            device_id_type=MESH,
        )

    def start(self):
        start_all(self.first)
        self.clip_buf[self.clip] = self.src[self.half, :]

    def middle(self):
        for k in (1, 0):
            drain(self.clip_buf.at[pl.ds(0, 7)], self.sems.at[k])
        self.row_buf[self.row] = tree([self.clip_buf[k] for k in range(8)])
        start_all(self.second)

    def trade(self):
        for k in (3, 2):
            drain(self.row_buf.at[pl.ds(0, FR - 1)], self.sems.at[k])
        self.out[self.half, :] = tree([self.row_buf[k] for k in range(FR)])
        self.third.start()

    def finish(self):
        self.third.wait()


class EdgeExchange:
    def __init__(self, src, dst, send, got):
        r = lax.axis_index("row")
        self.src, self.dst, self.send, self.got = src, dst, send, got
        self.copies = [
            pltpu.make_async_remote_copy(
                src_ref=src.at[k],
                dst_ref=dst.at[1 - k],
                send_sem=send,
                recv_sem=got,
                device_id={"row": lax.rem(r + d, FR)},
                device_id_type=MESH,
            )
            for d, k in ((FR - 1, 0), (1, 1))
        ]

    def start(self):
        for c in self.copies:
            c.start()

    def wait(self):
        drain(self.dst, self.got)
        drain(self.src, self.send)


def start_all(copies):
    for c in copies:
        c.start()


def wait_all(copies):
    for c in copies:
        c.wait()


def core_body(
    w_hbm, f_hbm, t_hbm, w1_hbm, w2_hbm, w3_hbm, w4_hbm, head_hbm,
    sums_ref, a_ref, b_ref, back_ref,
    fs, w_ref, t_ref, w1_ref, w2s, w3s, w4s, head_ref, wm, parts, parts16, edges, recv, recvf, nb, wide, want, rec,
    redges, ne, msg, msgf, gan,
    gg, gts, xsum, clip_buf, row_buf, w4t, t1t, hg,
    t1, pp, a1, s1, a2, s2, a3, s3, c4, c3, c2, c1,
    fsem, wsem, xsem, gsem, tsem,
):
    r = lax.axis_index("row")
    clip = lax.axis_index("clip")
    y, z = r // 4, lax.rem(r, 4)
    barrier = pltpu.get_barrier_semaphore()
    for d in range(1, FR):
        pl.semaphore_signal(
            barrier, inc=1, device_id={"row": lax.rem(r + d, FR)}, device_id_type=MESH
        )
    clips = 8
    for d in range(1, clips):
        pl.semaphore_signal(
            barrier, inc=1, device_id={"clip": lax.rem(clip + d, clips)}, device_id_type=MESH
        )
    pairs = [
        [yy * 4 + lax.rem(z + dz, 4) for dz in dzs for yy in range(2)] for dzs in ((2,), (1, 3))
    ]
    ys = lax.rem(y, 2)
    pairs.append([(1 - ys) * 4 + z, ys * 4 + z])
    loads = [
        [
            pltpu.make_async_copy(f_hbm.at[f], fs.at[f], fsem.at[k])
            for p in group
            for f in (p, p + 8)
        ]
        for k, group in enumerate(pairs)
    ]
    weights = [
        pltpu.make_async_copy(a, b, wsem.at[k])
        for k, (a, b) in enumerate(
            (
                (w2_hbm, w2s), (w3_hbm, w3s), (w4_hbm, w4s), (head_hbm, head_ref),
                (w1_hbm, w1_ref), (t_hbm, t_ref), (w_hbm, w_ref),
            )
        )
    ]
    weights[6].start()
    for group in loads:
        start_all(group)
    weights[6].wait()

    wm[...] = jnp.zeros_like(wm)
    for ab in range(9):
        v = w_ref[ab // 3, ab % 3].astype(F32)
        wm[ab * 8 : ab * 8 + 3, 0:128] = v
        wm[ab * 8 + 4 : ab * 8 + 7, 128:256] = v
    wmb = wm[...].astype(BF16)
    col = iota((8, 768), 1) % W
    lane = iota((16, 128), 1)
    pad = jnp.zeros((8, 128), F32)
    for k in range(27, 32):
        parts[:, k, :] = jnp.zeros((FR, 128), F32)

    def pair_features(p):
        return jnp.concatenate([fs[p].reshape(768, 128), fs[p + 8].reshape(768, 128)], 1)

    def send_images(f):
        pltpu.make_async_remote_copy(
            src_ref=parts16.at[f],
            dst_ref=recv.at[r],
            send_sem=xsem.at[0],
            recv_sem=xsem.at[1],
            device_id={"row": f},
            device_id_type=MESH,
        ).start()

    for k, group in enumerate(pairs):
        drain(fs.at[pl.ds(0, 2 * len(group))], fsem.at[k])
        if k == 2:
            start_all(weights[0:6])
        for p in group:
            out = dot(pair_features(p), wmb, NT).T
            total = None
            for ab in range(9):
                a, b = ab // 3, ab % 3
                g = edge_mask(out[ab * 8 : ab * 8 + 8, :], b, col)
                g = lroll(jnp.concatenate([g, pad], 1), (2 - a) * W + 1 - b)
                total = g if total is None else total + g
            for h in range(2):
                f = p + 8 * h
                for t in range(7):
                    tile = total[4 * h : 4 * h + 3, t * 128 : t * 128 + 128]
                    parts[f, 3 * t : 3 * t + 3, :] = tile
                    if t in (0, 6):
                        parts[f, 21 + t // 2 : 24 + t // 2, :] = tile - rnd(tile)
                parts16[f] = parts[f].astype(BF16)
        if k == 0:
            pl.semaphore_wait(barrier, FR + clips - 2)
        for p in group:
            if k < 2 or p is group[0]:
                send_images(p)
                send_images(p + 8)
    send_images(lax.rem(r + 8, FR))
    own = pltpu.make_async_copy(parts16.at[r], recv.at[r], xsem.at[1])
    own.start()
    flat = parts.reshape(FR * 32, 128)
    for t in (0, 6):
        for o in range(3):
            edges[t // 6, o] = flat[pl.ds(3 * t + o, 16, stride=32), :]
    ends = EdgeExchange(edges, nb, xsem.at[2], xsem.at[3])
    ends.start()

    weights[4].wait()
    build_band(w1_ref, t1)
    weights[5].wait()
    wide[:, 0:W] = t_ref[...].astype(F32)
    for o in range(3):
        tiles = [jnp.zeros((16, 128), F32) for _ in range(7)]
        for y in range(16):
            spread(tiles, lane, wide[pl.ds(o * 16 + y, 16, stride=48), :], 0, W * (y + 1))
        for t in range(7):
            want[t, o] = tiles[t]
    msgf[...] = jnp.zeros_like(msgf)
    wait_all(weights[0:4])
    head_term(head_ref, hg)
    for k in range(16):
        w4t[k] = w4s[k].T
    for k in range(6):
        t1t[:, k * 128 : k * 128 + 128] = t1[k * 128 : k * 128 + 128, :].T
    ends.wait()
    for o in range(3):
        for t in range(7):
            v = flat[pl.ds(3 * t + o, 16, stride=32), :]
            if t == 0:
                v = v + jnp.where((lane >= W) & (lane < 2 * W) & (r > 0), nb[0, o], 0.0)
            if t == 6:
                v = v + jnp.where((lane < W) & (r < FR - 1), nb[1, o], 0.0)
            v = SCALE * (v - want[t, o])
            if t == 0:
                v = jnp.where(lane >= W, v, 0.0)
            if t == 6:
                v = jnp.where(lane < W, v, 0.0)
            rec[t, o] = v
            if t in (0, 6):
                redges[t // 6, o] = v
    rends = EdgeExchange(redges, ne, xsem.at[4], xsem.at[5])
    rends.start()
    drain(recv, xsem.at[1])
    drain(parts16.at[pl.ds(0, FR - 1)], xsem.at[0])
    recvf[...] = recv.reshape(FR * 32, 128)[...].astype(F32)

    disc_stage(
        recvf, w2s, w3s, w4s, w4t, t1t, hg, msgf,
        t1, pp, a1, s1, a2, s2, a3, s3, c4, c3, c2, c1,
    )
    msg.reshape(FR * 32, 128)[...] = msgf[...].astype(BF16)
    for peer in row_peers():
        pltpu.make_async_remote_copy(
            src_ref=msg.at[peer],
            dst_ref=gan.at[r],
            send_sem=xsem.at[6],
            recv_sem=gsem.at[r],
            device_id={"row": peer},
            device_id_type=MESH,
        ).start()
    pltpu.make_async_copy(msg.at[r], gan.at[r], gsem.at[r]).start()

    gg[...] = jnp.zeros_like(gg)
    rends.wait()

    for o in range(3):
        for t in range(7):
            v = rec[t, o]
            if t == 0:
                v = v + jnp.where((lane < W) & (r > 0), ne[0, o], 0.0)
            if t == 6:
                v = v + jnp.where((lane >= W) & (lane < 2 * W) & (r < FR - 1), ne[1, o], 0.0)
            gg[pl.ds(t * 8 + o, 8, stride=56), :] = v[0:8]
            gg[pl.ds(t * 8 + 4 + o, 8, stride=56), :] = v[8:16]

    def weight_part(g, p, acc):
        gt = shifted(g, col)
        gts[p] = gt
        term = dot(gt, pair_features(p))
        return term if acc is None else acc + term

    def feature_part(part_ref):
        for p in range(8):
            out = dot(gts[p], wmb, TN)
            part_ref[p] = out[:, 0:128]
            part_ref[p + 8] = out[:, 128:256]

    rec_total = Total(xsum.at[0], clip_buf.at[0], row_buf.at[0], sums_ref.at[pl.ds(0, 32)], tsem.at[0])
    gan_total = Total(xsum.at[1], clip_buf.at[1], row_buf.at[1], sums_ref.at[pl.ds(32, 32)], tsem.at[1])
    acc = None
    for p in range(8):
        g = jnp.concatenate([gg[p * 56 + t * 8 : p * 56 + t * 8 + 8, :] for t in range(7)], 1)
        acc = weight_part(g, p, acc)
    compact(xsum.at[0], acc)
    rec_total.start()
    feature_part(a_ref)

    low = iota((8, 128), 0) < 4
    acc = None
    for group in pairs[::-1]:
        for p in group:
            for f in (p, p + 8):
                drain(gan.at[f], gsem.at[f])
        for p in group:
            va, vb = gan[p].astype(F32), gan[p + 8].astype(F32)
            ua, ub = pltpu.roll(va, 28, 0), pltpu.roll(vb, 4, 0)
            tiles = []
            for t in range(7):
                k = t // 2 * 8
                if t % 2 == 0:
                    tiles.append(jnp.where(low, va[k : k + 8], ub[k : k + 8]))
                else:
                    tiles.append(jnp.where(low, ua[k : k + 8], vb[k : k + 8]))
            acc = weight_part(jnp.concatenate(tiles, 1), p, acc)
    compact(xsum.at[1], acc)
    gan_total.start()
    rec_total.middle()
    feature_part(b_ref)
    drain(msg.at[pl.ds(0, FR - 1)], xsem.at[6])
    msgf[...] = gan.reshape(FR * 32, 128)[...].astype(F32)
    for o in range(3):
        tiles = [msgf[pl.ds(4 * t + o, 16, stride=32), :] for t in range(7)]
        for y in range(16):
            wide[pl.ds(o * 16 + y, 16, stride=48), :] = place(tiles, lane, W * (y + 1), 0)
    back_ref[...] = wide[:, 0:W].astype(BF16)
    gan_total.middle()
    rec_total.trade()
    rec_total.finish()
    gan_total.trade()
    gan_total.finish()


def core(conv_weight, features, target, w1, w2, w3, w4, head):
    hbm = lambda: pl.BlockSpec(memory_space=pltpu.HBM)
    dma = pltpu.SemaphoreType.DMA
    return pl.pallas_call(
        core_body,
        out_shape=(
            VM((64, 128), F32),
            VM((FR, 768, 128), F32),
            VM((FR, 768, 128), F32),
            VM((768, W), BF16),
        ),
        in_specs=[hbm()] * 8,
        out_specs=(vspec(), vspec(), vspec(), vspec()),
        scratch_shapes=[
            VM((FR, 16, W, 128), BF16),
            VM((3, 3, 3, 128), BF16),
            VM((768, W), BF16),
            VM((4, 3, 4, 64), BF16),
            VM((4, 256, 128), BF16),
            VM((16, 128, 256), BF16),
            VM((16, 256, 512), BF16),
            VM((4, 4, 512), BF16),
            VM((80, 256), F32),
            VM((FR, 32, 128), F32),
            VM((FR, 32, 128), BF16),
            VM((2, 3, FR, 128), F32),
            VM((FR, 32, 128), BF16),
            VM((FR * 32, 128), F32),
            VM((2, 3, FR, 128), F32),
            VM((768, 128), F32),
            VM((7, 3, FR, 128), F32),
            VM((7, 3, FR, 128), F32),
            VM((2, 3, FR, 128), F32),
            VM((2, 3, FR, 128), F32),
            VM((FR, 32, 128), BF16),
            VM((FR * 32, 128), F32),
            VM((FR, 32, 128), BF16),
            VM((448, 128), F32),
            VM((8, 80, 768), BF16),
            VM((2, 32, 128), F32),
            VM((2, 8, 16, 128), F32),
            VM((2, FR, 16, 128), F32),
            VM((16, 512, 256), BF16),
            VM((1664, 768), BF16),
            VM((160, 512), F32),
            VM((768, 1664), BF16),
            VM((9, 16, 384), BF16),
            VM((10, 13, 16, 128), BF16),
            VM((8, 13, 16, 128), F32),
            VM((6, 2, 7, 16, 128), BF16),
            VM((4, 12, 16, 128), F32),
            VM((5, 8, 16, 256), BF16),
            VM((2, 6, 16, 256), F32),
            VM((5, 9, 16, 512), BF16),
            VM((4, 8, 16, 256), BF16),
            VM((6, 14, 16, 128), BF16),
            VM((128, 1664), BF16),
            dma((3,)),
            dma((7,)),
            dma((8,)),
            dma((FR,)),
            dma((2, 6)),
        ],
        compiler_params=pltpu.CompilerParams(
            collective_id=0, has_side_effects=True, vmem_limit_bytes=44 << 20
        ),
        name="core",
    )(
        *(
            pltpu.with_memory_space_constraint(v, pltpu.HBM)
            for v in (conv_weight, features, target, w1, w2, w3, w4, head)
        )
    )


def final_body(pixels, s_ref, a_ref, b_ref, g_ref, out_hbm, wg_ref, ad_ref, back_ref, buf, sem):
    rec, gan = s_ref[0:32], s_ref[32:64]
    adaptive = jnp.sqrt(jnp.sum(rec * rec, keepdims=True)) / (
        jnp.sqrt(jnp.sum(gan * gan, keepdims=True)) + EPS
    )
    scale = jnp.broadcast_to(adaptive, (8, 128))[None]
    stores = []
    for f in range(FR):
        v = a_ref[f].reshape(96, 8, 128) + scale * b_ref[f].reshape(96, 8, 128)
        buf[f] = v.reshape(16, W, 128).astype(BF16)
        copy = pltpu.make_async_copy(buf.at[f], out_hbm.at[f], sem.at[f])
        copy.start()
        stores.append(copy)
    ad_ref[...] = adaptive
    mixed = (rec + adaptive * gan) / pixels
    for ab in range(9):
        wg_ref[ab // 3, ab % 3] = mixed[ab * 3 : ab * 3 + 3]
    back_ref[...] = g_ref[...]
    wait_all(stores)


def final(sums, a, b, back, pixels):
    return pl.pallas_call(
        functools.partial(final_body, pixels),
        out_shape=(
            jax.ShapeDtypeStruct((FR, 16, W, 128), BF16),
            jax.ShapeDtypeStruct((3, 3, 3, 128), F32),
            jax.ShapeDtypeStruct((1, 1), F32),
            jax.ShapeDtypeStruct((768, W), BF16),
        ),
        in_specs=[vspec()] * 4,
        out_specs=(pl.BlockSpec(memory_space=pltpu.HBM), vspec(), vspec(), vspec()),
        scratch_shapes=[VM((FR, 16, W, 128), BF16), pltpu.SemaphoreType.DMA((FR,))],
        compiler_params=pltpu.CompilerParams(vmem_limit_bytes=24 << 20),
        name="final",
    )(sums, a, b, back)


def per_device(
    features, target, conv_weight, disc_first, disc_second, disc_third, disc_fourth, disc_head
):
    clips = lax.axis_size("clip")
    wanted = jnp.transpose(target[0], (0, 2, 1, 3)).reshape(768, W)
    w1 = jnp.transpose(disc_first, (0, 2, 1, 3))
    w2 = disc_second.reshape(4, 256, 128)
    w3 = disc_third.reshape(16, 128, 256)
    w4 = disc_fourth.reshape(16, 256, 512)
    head = disc_head.reshape(4, 4, 512)
    pixels = float(clips * FR * 256 * W)
    sums, a, b, back = core(conv_weight, features[0], wanted, w1, w2, w3, w4, head)
    feature_grad, weight_grad, adaptive, back = final(sums, a, b, back, pixels)
    image_back = jnp.transpose(back.reshape(1, FR, 3, 16, W), (0, 1, 3, 2, 4))
    return (feature_grad[None], image_back, weight_grad, adaptive[0, 0])


def solution(mesh):
    return jax.shard_map(
        per_device,
        mesh=mesh,
        in_specs=(
            P("clip", None, "row", None, None),
            P("clip", None, "row", None, None),
            P(),
            P(),
            P(),
            P(),
            P(),
            P(),
        ),
        out_specs=(
            P("clip", None, "row", None, None),
            P("clip", None, "row", None, None),
            P(),
            P(),
        ),
        check_vma=False,
    )
```

```python
import functools

import jax
import jax.numpy as jnp
from jax import lax
from jax.experimental import pallas as pl
from jax.experimental.pallas import tpu as pltpu
from jax.sharding import PartitionSpec as P

MESH = pl.DeviceIdType.MESH
F32 = jnp.float32
BF16 = jnp.bfloat16
SCALE = 64.0
EPS = 0.0001
FR = 16
W = 48
NT = (((1,), (1,)), ((), ()))
TN = (((0,), (0,)), ((), ()))
VM = pltpu.VMEM


def vspec():
    return pl.BlockSpec(memory_space=pltpu.VMEM)


def dot(a, b, dims=(((1,), (0,)), ((), ()))):
    return lax.dot_general(a, b, dims, preferred_element_type=F32)


def iota(shape, dim):
    return lax.broadcasted_iota(jnp.int32, shape, dim)


def rnd(v):
    return v.astype(BF16).astype(F32)


def down1(v):
    return jnp.where(iota(v.shape, 0) >= 1, pltpu.roll(v, 1, 0), 0.0)


def up1(v):
    n = v.shape[0]
    return jnp.where(iota(v.shape, 0) < n - 1, pltpu.roll(v, n - 1, 0), 0.0)


def lroll(v, s):
    s = s % v.shape[1]
    return v if s == 0 else pltpu.roll(v, s, 1)


def place(tiles, lane, src, dst):
    t, off = src // 128, src % 128
    v = lroll(tiles[t], dst - off)
    if off + W > 128:
        v = jnp.where(lane - dst < 128 - off, v, lroll(tiles[t + 1], dst - off))
    return jnp.where((lane >= dst) & (lane < dst + W), v, 0.0)


def spread(tiles, lane, v, src, dst):
    t, off = dst // 128, dst % 128
    v = lroll(jnp.where((lane >= src) & (lane < src + W), v, 0.0), off - src)
    if off + W > 128:
        tiles[t] = tiles[t] + jnp.where(lane >= off, v, 0.0)
        tiles[t + 1] = tiles[t + 1] + jnp.where(lane < off + W - 128, v, 0.0)
    else:
        tiles[t] = tiles[t] + v


def build_band(w1_ref, t1):
    t1[...] = jnp.zeros_like(t1)
    row = iota((16, 128), 0)
    lane = iota((16, 128), 1)
    for ao in range(12):
        w = w1_ref[ao // 3, ao % 3].astype(F32)
        left = jnp.concatenate([w, jnp.zeros((12, 64), F32)], 0)
        patch = jnp.concatenate([left, pltpu.roll(left, 2, 0)], 1)
        for s in (13, 1, 5, 9):
            rolled = pltpu.roll(patch, s, 0)
            parts = [(0, rolled)]
            if s == 13:
                parts = [(0, jnp.where(row >= 13, rolled, 0.0)), (1, jnp.where(row < 13, rolled, 0.0))]
            for v in range(13):
                start = 4 * v - 3
                if start % 16 != s:
                    continue
                for over, tile in parts:
                    g = start // 16 + over
                    if g < 0 or g > 2:
                        continue
                    if v == 0:
                        tile = jnp.where(lane >= 64, tile, 0.0)
                    if v == 12:
                        tile = jnp.where(lane < 64, tile, 0.0)
                    r0 = ao * 64 + g * 16
                    t1[r0 : r0 + 16, v * 128 : v * 128 + 128] = tile.astype(BF16)


def silu_pair(v):
    s = jax.nn.sigmoid(v)
    return v * s, s * (1.0 + v * (1.0 - s))


def rows16(v, k):
    return v[k * 16 : k * 16 + 16]


def head_term(head_ref, hg):
    rr = iota((160, 16), 0)
    tap = iota((160, 16), 1)
    y4 = 2 * (rr % 16) + rr // 80
    x4 = (rr % 80) // 16
    py = y4 + 1 - tap // 4
    px = x4 + 1 - tap % 4
    ok = (py >= 0) & (py <= 29) & (px >= 0) & (px <= 3) & (y4 <= 30)
    mask = jnp.where(ok, -SCALE, 0.0).astype(BF16)
    head = jnp.concatenate([head_ref[a].astype(F32) for a in range(4)], 0).astype(BF16)
    hg[...] = dot(mask, head)


def disc_stage(
    recv_ref, w2x, w3_ref, w4_ref, w3t, w4t, t1t, hg, out_ref, w2_ref, between,
    t1, pp, a1, s1, a2, s2, a3, s3, c4, c3, c2, c1,
):
    lane = iota((16, 128), 1)
    x = []
    for o in range(3):
        tiles = [recv_ref[pl.ds(3 * t + o, 16, stride=32), :] for t in range(7)]
        first = tiles[0] + recv_ref[pl.ds(21 + o, 16, stride=32), :]
        last = tiles[6] + recv_ref[pl.ds(24 + o, 16, stride=32), :]
        tiles[0] = first + jnp.where((lane >= W) & (lane < 2 * W), down1(last), 0.0)
        tiles[6] = last + jnp.where(lane < W, up1(first), 0.0)
        x.append([rnd(v) for v in tiles])
    halves = {}
    for m in range(16):
        s = 1 - m % 2
        for o in range(3):
            q = s * 3 + o
            halves[m, q] = place(x[o], lane, W * (m + 1), (q % 2) * 64)
    for i in range(9):
        piece = {}
        for q in range(6):
            m = 2 * i - 1 if q < 3 else 2 * i
            if m == -1:
                piece[q] = down1(halves[15, q])
            elif m == 16:
                piece[q] = up1(halves[0, q])
            else:
                piece[q] = halves[m, q]
        for j in range(3):
            pp[i, :, j * 128 : j * 128 + 128] = (piece[2 * j] + piece[2 * j + 1]).astype(BF16)
    lhs = jnp.concatenate([pp[0:8].reshape(128, 384), pp[1:9].reshape(128, 384)], 1)
    for v0 in range(0, 13, 2):
        n = min(2, 13 - v0)
        pre = dot(lhs, t1[:, v0 * 128 : (v0 + n) * 128])
        for v in range(v0, v0 + n):
            act, slope = silu_pair(pre[:, (v - v0) * 128 : (v - v0 + 1) * 128])
            s1[:, v] = slope.reshape(8, 16, 128)
            a1[1:9, v] = act.astype(BF16).reshape(8, 16, 128)
            a1[0, v] = down1(rows16(act, 7)).astype(BF16)
            a1[9, v] = up1(rows16(act, 0)).astype(BF16)
    zero = jnp.zeros((16, 128), BF16)
    for m in range(6):
        a2[m, 0, 0] = zero
        a2[m, 1, 6] = zero
        c2[m, 0] = zero
        c2[m, 13] = zero
    lhs = jnp.concatenate(
        [
            jnp.concatenate([a1[2 * m + a, 2 * u + k] for m in range(4) for u in range(6)], 0)
            for a in range(4)
            for k in range(3)
        ],
        1,
    )
    pre = dot(lhs, w2x[...])
    for m in range(4):
        for c in range(12):
            k = (m * 6 + c // 2) * 16
            act, slope = silu_pair(pre[k : k + 16, c % 2 * 128 : c % 2 * 128 + 128])
            s2[m, c] = slope
            e, p = (c + 1) % 2, (c + 1) // 2
            a2[m + 1, e, p] = act.astype(BF16)
            if m == 3:
                a2[0, e, p] = down1(act).astype(BF16)
            if m == 0:
                a2[5, e, p] = up1(act).astype(BF16)
    zero = jnp.zeros((16, 256), BF16)
    for k in range(5):
        a3[k, 0] = zero
        a3[k, 7] = zero
    for k in range(4):
        c3[k, 0] = zero
        c3[k, 7] = zero
    acc = None
    for a in range(4):
        lhs = jnp.concatenate(
            [
                jnp.concatenate(
                    [a2[2 * m + a, b % 2, b // 2 : b // 2 + 6].reshape(96, 128) for m in range(2)], 0
                )
                for b in range(4)
            ],
            1,
        )
        term = dot(lhs, w3_ref[a * 4 : a * 4 + 4].reshape(512, 256))
        acc = term if acc is None else acc + term
    act, slope = silu_pair(acc)
    s3[...] = slope.reshape(2, 6, 16, 256)
    for c in range(6):
        v0, v1 = rows16(act, c), rows16(act, 6 + c)
        a3[0, c + 1] = down1(v1).astype(BF16)
        a3[1, c + 1] = v0.astype(BF16)
        a3[2, c + 1] = v1.astype(BF16)
        a3[3, c + 1] = up1(v0).astype(BF16)
        a3[4, c + 1] = up1(v1).astype(BF16)
    acc = None
    for a in range(4):
        lhs = jnp.concatenate(
            [
                jnp.concatenate([a3[m + a, b : b + 5].reshape(80, 256) for m in range(2)], 0)
                for b in range(4)
            ],
            1,
        )
        term = dot(lhs, w4_ref[a * 4 : a * 4 + 4].reshape(1024, 512))
        acc = term if acc is None else acc + term
    _, slope = silu_pair(acc)
    cot = hg[...] * slope
    zero = jnp.zeros((16, 512), BF16)
    for k in range(5):
        for c in (0, 1, 7, 8):
            c4[k, c] = zero
    for c in range(5):
        v0, v1 = rows16(cot, c), rows16(cot, 5 + c)
        c4[0, c + 2] = down1(v0).astype(BF16)
        c4[1, c + 2] = down1(v1).astype(BF16)
        c4[2, c + 2] = v0.astype(BF16)
        c4[3, c + 2] = v1.astype(BF16)
        c4[4, c + 2] = up1(v0).astype(BF16)
    between()
    acc = None
    for a in range(4):
        lhs = jnp.concatenate(
            [
                jnp.concatenate(
                    [c4[m + 3 - a, 3 - b : 9 - b].reshape(96, 512) for m in range(2)], 0
                )
                for b in range(4)
            ],
            1,
        )
        term = dot(lhs, w4t[a * 4 : a * 4 + 4].reshape(2048, 256))
        acc = term if acc is None else acc + term
    cot = acc * s3[...].reshape(192, 256)
    for c in range(6):
        v0, v1 = rows16(cot, c), rows16(cot, 6 + c)
        c3[0, c + 1] = down1(v1).astype(BF16)
        c3[1, c + 1] = v0.astype(BF16)
        c3[2, c + 1] = v1.astype(BF16)
        c3[3, c + 1] = up1(v0).astype(BF16)
    for first in (0, 1):
        rows = (1, 3) if first == 0 else (0, 2)
        lhs = jnp.concatenate(
            [
                jnp.concatenate(
                    [c3[(m + 1 - a) // 2 + 1, off : off + 6].reshape(96, 256) for m in rows], 0
                )
                for a in (first, first + 2)
                for off in range(3)
            ],
            1,
        )
        rhs = jnp.concatenate([w3t[a].reshape(768, 256) for a in (first, first + 2)], 0)
        acc = dot(lhs, rhs)
        for n, m in enumerate(rows):
            for p in range(6):
                for e in range(2):
                    c = 2 * p + 1 - e
                    v = rows16(acc, n * 6 + p)[:, e * 128 : e * 128 + 128] * s2[m, c]
                    c2[m + 1, c + 1] = v.astype(BF16)
                    if m == 3:
                        c2[0, c + 1] = down1(v).astype(BF16)
                    if m == 0:
                        c2[5, c + 1] = up1(v).astype(BF16)
    for first in (0, 1):
        rhs = jnp.concatenate(
            [w2_ref[a, h * 128 : h * 128 + 128] for a in (first, first + 2) for h in range(2)], 1
        )
        for i in range(4):
            m = 2 * i + 1 - first
            lhs = jnp.concatenate(
                [
                    c2[(m + 1 - a) // 2 + 1, 1 - h : 14 - h].reshape(208, 128)
                    for a in (first, first + 2)
                    for h in range(2)
                ],
                1,
            )
            cot = dot(lhs, rhs, NT) * s1[m].reshape(208, 128)
            for v in range(13):
                c1[m * 16 : m * 16 + 16, v * 128 : v * 128 + 128] = rows16(cot, v).astype(BF16)
    grad = dot(c1[...], t1t[...])
    halves = {}
    for j in range(3):
        ps = []
        for i in range(9):
            v = None
            if i <= 7:
                v = grad[i * 16 : i * 16 + 16, j * 128 : j * 128 + 128]
            if i >= 1:
                u = grad[(i - 1) * 16 : i * 16, 384 + j * 128 : 512 + j * 128]
                v = u if v is None else v + u
            ps.append(v)
        for h in range(2):
            q = 2 * j + h
            for i in range(9):
                m = 2 * i - 1 if q < 3 else 2 * i
                if 0 <= m <= 15:
                    v = ps[i]
                    if m == 15:
                        v = v + up1(ps[0])
                    if m == 0:
                        v = v + down1(ps[8])
                    halves[m, q] = rnd(v)
    for o in range(3):
        tiles = [jnp.zeros((16, 128), F32) for _ in range(7)]
        for m in range(16):
            q = (1 - m % 2) * 3 + o
            spread(tiles, lane, halves[m, q], (q % 2) * 64, W * (m + 1))
        first, last = tiles[0], tiles[6]
        tiles[0] = first + jnp.where(lane < W, down1(last), 0.0)
        tiles[6] = last + jnp.where((lane >= W) & (lane < 2 * W), up1(first), 0.0)
        for t in range(7):
            out_ref[pl.ds(4 * t + o, 16, stride=32), :] = tiles[t]

def edge_mask(v, b, col):
    if b == 0:
        return jnp.where(col <= W - 2, v, 0.0)
    if b == 2:
        return jnp.where(col >= 1, v, 0.0)
    return v


def shifted(g, col):
    rows = []
    for ab in range(9):
        a, b = ab // 3, ab % 3
        rows.append(edge_mask(lroll(g, -((2 - a) * W + 1 - b))[:, 0:768], b, col))
    rows.append(jnp.zeros((8, 768), F32))
    return jnp.concatenate(rows, 0).astype(BF16)


def compact(dst, acc):
    dst[...] = jnp.zeros_like(dst)
    for ab in range(9):
        k = ab * 8
        dst[ab * 3 : ab * 3 + 3, :] = acc[k : k + 3, 0:128] + acc[k + 4 : k + 7, 128:256]


def drain(ref, sem):
    pltpu.make_async_copy(ref, ref, sem).wait()


def hops(d):
    return min(d, 4 - d)


ROW_OFFSETS = sorted(
    ((dy, dz) for dy in range(4) for dz in range(4) if dy or dz),
    key=lambda t: -(hops(t[0]) + hops(t[1])),
)
CLIP_OFFSETS = sorted(
    ((dx, dc) for dx in range(4) for dc in range(2) if dx or dc), key=lambda t: -(2 * hops(t[0]) + t[1])
)


def row_peers():
    r = lax.axis_index("row")
    y, z = r // 4, lax.rem(r, 4)
    return [lax.rem(y + dy, 4) * 4 + lax.rem(z + dz, 4) for dy, dz in ROW_OFFSETS]


def tree(parts):
    while len(parts) > 1:
        parts = [a + b for a, b in zip(parts[::2], parts[1::2])]
    return parts[0]


class Total:
    def __init__(self, src, clip_buf, row_buf, out, sems):
        clip, row = lax.axis_index("clip"), lax.axis_index("row")
        x, core = clip // 2, lax.rem(clip, 2)
        self.src, self.clip_buf, self.row_buf, self.out, self.sems = src, clip_buf, row_buf, out, sems
        self.clip, self.row = clip, row
        self.half = pl.ds(pl.multiple_of(core * 16, 16), 16)
        self.first = []
        for dx, dc in CLIP_OFFSETS:
            other = lax.rem(core + dc, 2)
            self.first.append(
                pltpu.make_async_remote_copy(
                    src_ref=src.at[pl.ds(pl.multiple_of(other * 16, 16), 16)],
                    dst_ref=clip_buf.at[clip],
                    send_sem=sems.at[0],
                    recv_sem=sems.at[1],
                    device_id={"clip": lax.rem(x + dx, 4) * 2 + other},
                    device_id_type=MESH,
                )
            )
        self.second = [
            pltpu.make_async_remote_copy(
                src_ref=row_buf.at[row],
                dst_ref=row_buf.at[row],
                send_sem=sems.at[2],
                recv_sem=sems.at[3],
                device_id={"row": peer},
                device_id_type=MESH,
            )
            for peer in row_peers()
        ]
        self.third = pltpu.make_async_remote_copy(
            src_ref=out.at[self.half],
            dst_ref=out.at[self.half],
            send_sem=sems.at[4],
            recv_sem=sems.at[5],
            device_id={"clip": x * 2 + 1 - core},
            device_id_type=MESH,
        )

    def start(self):
        start_all(self.first)
        self.clip_buf[self.clip] = self.src[self.half, :]

    def middle(self):
        for k in (1, 0):
            drain(self.clip_buf.at[pl.ds(0, 7)], self.sems.at[k])
        self.row_buf[self.row] = tree([self.clip_buf[k] for k in range(8)])
        start_all(self.second)

    def trade(self):
        for k in (3, 2):
            drain(self.row_buf.at[pl.ds(0, FR - 1)], self.sems.at[k])
        self.out[self.half, :] = tree([self.row_buf[k] for k in range(FR)])
        self.third.start()

    def finish(self):
        self.third.wait()


class EdgeExchange:
    def __init__(self, src, dst, send, got):
        r = lax.axis_index("row")
        self.src, self.dst, self.send, self.got = src, dst, send, got
        self.copies = [
            pltpu.make_async_remote_copy(
                src_ref=src.at[k],
                dst_ref=dst.at[1 - k],
                send_sem=send,
                recv_sem=got,
                device_id={"row": lax.rem(r + d, FR)},
                device_id_type=MESH,
            )
            for d, k in ((FR - 1, 0), (1, 1))
        ]

    def start(self):
        for c in self.copies:
            c.start()

    def wait(self):
        drain(self.dst, self.got)
        drain(self.src, self.send)


def start_all(copies):
    for c in copies:
        c.start()


def wait_all(copies):
    for c in copies:
        c.wait()


def core_body(
    w_hbm, f_hbm, t_hbm, w1_hbm, w2_hbm, w3_hbm, w4_hbm, head_hbm,
    sums_ref, a_ref, b_ref, back_ref,
    fs, w_ref, t_ref, w1_ref, w2s, w3s, w4s, head_ref, wm, parts, parts16, edges, recv, recvf, nb, wide, want, rec,
    redges, ne, msg, msgf, gan,
    gg, gts, xsum, clip_buf, row_buf, w2x, w3t, w4t, t1t, hg,
    t1, pp, a1, s1, a2, s2, a3, s3, c4, c3, c2, c1,
    fsem, wsem, xsem, gsem, tsem,
):
    r = lax.axis_index("row")
    clip = lax.axis_index("clip")
    y, z = r // 4, lax.rem(r, 4)
    weights = [
        pltpu.make_async_copy(a, b, wsem.at[k])
        for k, (a, b) in enumerate(
            (
                (w2_hbm, w2s), (w3_hbm, w3s), (w4_hbm, w4s), (head_hbm, head_ref),
                (w1_hbm, w1_ref), (t_hbm, t_ref), (w_hbm, w_ref),
            )
        )
    ]
    weights[6].start()
    start_all(weights[3:6])
    barrier = pltpu.get_barrier_semaphore()
    for d in range(1, FR):
        pl.semaphore_signal(
            barrier, inc=1, device_id={"row": lax.rem(r + d, FR)}, device_id_type=MESH
        )
    clips = 8
    for d in range(1, clips):
        pl.semaphore_signal(
            barrier, inc=1, device_id={"clip": lax.rem(clip + d, clips)}, device_id_type=MESH
        )
    pairs = [
        [yy * 4 + lax.rem(z + dz, 4) for dz in dzs for yy in range(2)] for dzs in ((2,), (1, 3), (0,))
    ]
    loads = [
        [
            pltpu.make_async_copy(f_hbm.at[f], fs.at[f], fsem.at[k])
            for p in group
            for f in (p, p + 8)
        ]
        for k, group in enumerate((pairs[0] + pairs[1][0:2], pairs[1][2:4] + pairs[2]))
    ]
    for group in loads:
        start_all(group)
    weights[6].wait()

    wm[...] = jnp.zeros_like(wm)
    for ab in range(9):
        v = w_ref[ab // 3, ab % 3].astype(F32)
        wm[ab * 8 : ab * 8 + 3, 0:128] = v
        wm[ab * 8 + 4 : ab * 8 + 7, 128:256] = v
    wmb = wm[...].astype(BF16)
    col = iota((8, 768), 1) % W
    lane = iota((16, 128), 1)
    pad = jnp.zeros((8, 128), F32)
    for k in range(27, 32):
        parts[:, k, :] = jnp.zeros((FR, 128), F32)

    def pair_features(p):
        return jnp.concatenate([fs[p].reshape(768, 128), fs[p + 8].reshape(768, 128)], 1)

    halves = (pairs[0] + pairs[1][0:2], pairs[1][2:4] + pairs[2])
    for k, group in enumerate(halves):
        drain(fs.at[pl.ds(0, 8)], fsem.at[k])
        if k == 1:
            start_all(weights[0:3])
        for p in group:
            out = dot(pair_features(p), wmb, NT).T
            total = None
            for ab in range(9):
                a, b = ab // 3, ab % 3
                g = edge_mask(out[ab * 8 : ab * 8 + 8, :], b, col)
                g = lroll(jnp.concatenate([g, pad], 1), (2 - a) * W + 1 - b)
                total = g if total is None else total + g
            for h in range(2):
                f = p + 8 * h
                for t in range(7):
                    tile = total[4 * h : 4 * h + 3, t * 128 : t * 128 + 128]
                    parts[f, 3 * t : 3 * t + 3, :] = tile
                    if t in (0, 6):
                        parts[f, 21 + t // 2 : 24 + t // 2, :] = tile - rnd(tile)
                parts16[f] = parts[f].astype(BF16)
    pl.semaphore_wait(barrier, FR + clips - 2)
    for peer in row_peers():
        pltpu.make_async_remote_copy(
            src_ref=parts16.at[peer],
            dst_ref=recv.at[r],
            send_sem=xsem.at[0],
            recv_sem=xsem.at[1],
            device_id={"row": peer},
            device_id_type=MESH,
        ).start()
    pltpu.make_async_copy(parts16.at[r], recv.at[r], xsem.at[1]).start()
    flat = parts.reshape(FR * 32, 128)
    for t in (0, 6):
        for o in range(3):
            edges[t // 6, o] = flat[pl.ds(3 * t + o, 16, stride=32), :]
    ends = EdgeExchange(edges, nb, xsem.at[2], xsem.at[3])
    ends.start()

    weights[4].wait()
    build_band(w1_ref, t1)
    weights[5].wait()
    wide[:, 0:W] = t_ref[...].astype(F32)
    for o in range(3):
        tiles = [jnp.zeros((16, 128), F32) for _ in range(7)]
        for y in range(16):
            spread(tiles, lane, wide[pl.ds(o * 16 + y, 16, stride=48), :], 0, W * (y + 1))
        for t in range(7):
            want[t, o] = tiles[t]
    msgf[...] = jnp.zeros_like(msgf)
    wait_all(weights[0:4])
    head_term(head_ref, hg)
    for k in range(4):
        zero = jnp.zeros((128, 128), BF16)
        for h in range(2):
            w2x[k * 384 + h * 128 : k * 384 + h * 128 + 256, h * 128 : h * 128 + 128] = w2s[k]
        w2x[k * 384 + 256 : k * 384 + 384, 0:128] = zero
        w2x[k * 384 : k * 384 + 128, 128:256] = zero
        w3t[k, 2, :, 0:128] = w3s[k * 4].T
        w3t[k, 1, :, 0:128] = w3s[k * 4 + 2].T
        w3t[k, 1, :, 128:256] = w3s[k * 4 + 1].T
        w3t[k, 0, :, 128:256] = w3s[k * 4 + 3].T
        w3t[k, 2, :, 128:256] = jnp.zeros((256, 128), BF16)
        w3t[k, 0, :, 0:128] = jnp.zeros((256, 128), BF16)
    for k in range(16):
        w4t[k] = w4s[k].T
    for k in range(6):
        t1t[:, k * 128 : k * 128 + 128] = t1[k * 128 : k * 128 + 128, :].T
    rends = EdgeExchange(redges, ne, xsem.at[4], xsem.at[5])

    def reconstruction():
        ends.wait()
        for o in range(3):
            for t in range(7):
                v = flat[pl.ds(3 * t + o, 16, stride=32), :]
                if t == 0:
                    v = v + jnp.where((lane >= W) & (lane < 2 * W) & (r > 0), nb[0, o], 0.0)
                if t == 6:
                    v = v + jnp.where((lane < W) & (r < FR - 1), nb[1, o], 0.0)
                v = SCALE * (v - want[t, o])
                if t == 0:
                    v = jnp.where(lane >= W, v, 0.0)
                if t == 6:
                    v = jnp.where(lane < W, v, 0.0)
                rec[t, o] = v
                if t in (0, 6):
                    redges[t // 6, o] = v
        rends.start()

    drain(recv, xsem.at[1])
    drain(parts16.at[pl.ds(0, FR - 1)], xsem.at[0])
    recvf[...] = recv.reshape(FR * 32, 128)[...].astype(F32)

    disc_stage(
        recvf, w2x, w3s, w4s, w3t, w4t, t1t, hg, msgf, w2s, reconstruction,
        t1, pp, a1, s1, a2, s2, a3, s3, c4, c3, c2, c1,
    )
    msg.reshape(FR * 32, 128)[...] = msgf[...].astype(BF16)
    for peer in row_peers():
        pltpu.make_async_remote_copy(
            src_ref=msg.at[peer],
            dst_ref=gan.at[r],
            send_sem=xsem.at[6],
            recv_sem=gsem.at[r],
            device_id={"row": peer},
            device_id_type=MESH,
        ).start()
    pltpu.make_async_copy(msg.at[r], gan.at[r], gsem.at[r]).start()

    gg[...] = jnp.zeros_like(gg)
    rends.wait()

    for o in range(3):
        for t in range(7):
            v = rec[t, o]
            if t == 0:
                v = v + jnp.where((lane < W) & (r > 0), ne[0, o], 0.0)
            if t == 6:
                v = v + jnp.where((lane >= W) & (lane < 2 * W) & (r < FR - 1), ne[1, o], 0.0)
            gg[pl.ds(t * 8 + o, 8, stride=56), :] = v[0:8]
            gg[pl.ds(t * 8 + 4 + o, 8, stride=56), :] = v[8:16]

    def weight_part(g, p, acc):
        gt = shifted(g, col)
        gts[p] = gt
        term = dot(gt, pair_features(p))
        return term if acc is None else acc + term

    def feature_part(part_ref):
        for p in range(8):
            out = dot(gts[p], wmb, TN)
            part_ref[p] = out[:, 0:128]
            part_ref[p + 8] = out[:, 128:256]

    rec_total = Total(xsum.at[0], clip_buf.at[0], row_buf.at[0], sums_ref.at[pl.ds(0, 32)], tsem.at[0])
    gan_total = Total(xsum.at[1], clip_buf.at[1], row_buf.at[1], sums_ref.at[pl.ds(32, 32)], tsem.at[1])
    acc = None
    for p in range(8):
        g = jnp.concatenate([gg[p * 56 + t * 8 : p * 56 + t * 8 + 8, :] for t in range(7)], 1)
        acc = weight_part(g, p, acc)
    compact(xsum.at[0], acc)
    rec_total.start()
    feature_part(a_ref)

    low = iota((8, 128), 0) < 4
    acc = None
    for group in pairs[::-1]:
        for p in group:
            for f in (p, p + 8):
                drain(gan.at[f], gsem.at[f])
        for p in group:
            va, vb = gan[p].astype(F32), gan[p + 8].astype(F32)
            ua, ub = pltpu.roll(va, 28, 0), pltpu.roll(vb, 4, 0)
            tiles = []
            for t in range(7):
                k = t // 2 * 8
                if t % 2 == 0:
                    tiles.append(jnp.where(low, va[k : k + 8], ub[k : k + 8]))
                else:
                    tiles.append(jnp.where(low, ua[k : k + 8], vb[k : k + 8]))
            acc = weight_part(jnp.concatenate(tiles, 1), p, acc)
    compact(xsum.at[1], acc)
    gan_total.start()
    rec_total.middle()
    feature_part(b_ref)
    drain(msg.at[pl.ds(0, FR - 1)], xsem.at[6])
    msgf[...] = gan.reshape(FR * 32, 128)[...].astype(F32)
    for o in range(3):
        tiles = [msgf[pl.ds(4 * t + o, 16, stride=32), :] for t in range(7)]
        for y in range(16):
            wide[pl.ds(o * 16 + y, 16, stride=48), :] = place(tiles, lane, W * (y + 1), 0)
    back_ref[...] = wide[:, 0:W].astype(BF16)
    gan_total.middle()
    rec_total.trade()
    rec_total.finish()
    gan_total.trade()
    gan_total.finish()


def core(conv_weight, features, target, w1, w2, w3, w4, head):
    hbm = lambda: pl.BlockSpec(memory_space=pltpu.HBM)
    dma = pltpu.SemaphoreType.DMA
    return pl.pallas_call(
        core_body,
        out_shape=(
            VM((64, 128), F32),
            VM((FR, 768, 128), F32),
            VM((FR, 768, 128), F32),
            VM((768, W), BF16),
        ),
        in_specs=[hbm()] * 8,
        out_specs=(vspec(), vspec(), vspec(), vspec()),
        scratch_shapes=[
            VM((FR, 16, W, 128), BF16),
            VM((3, 3, 3, 128), BF16),
            VM((768, W), BF16),
            VM((4, 3, 4, 64), BF16),
            VM((4, 256, 128), BF16),
            VM((16, 128, 256), BF16),
            VM((16, 256, 512), BF16),
            VM((4, 4, 512), BF16),
            VM((80, 256), F32),
            VM((FR, 32, 128), F32),
            VM((FR, 32, 128), BF16),
            VM((2, 3, FR, 128), F32),
            VM((FR, 32, 128), BF16),
            VM((FR * 32, 128), F32),
            VM((2, 3, FR, 128), F32),
            VM((768, 128), F32),
            VM((7, 3, FR, 128), F32),
            VM((7, 3, FR, 128), F32),
            VM((2, 3, FR, 128), F32),
            VM((2, 3, FR, 128), F32),
            VM((FR, 32, 128), BF16),
            VM((FR * 32, 128), F32),
            VM((FR, 32, 128), BF16),
            VM((448, 128), F32),
            VM((8, 80, 768), BF16),
            VM((2, 32, 128), F32),
            VM((2, 8, 16, 128), F32),
            VM((2, FR, 16, 128), F32),
            VM((1536, 256), BF16),
            VM((4, 3, 256, 256), BF16),
            VM((16, 512, 256), BF16),
            VM((1664, 768), BF16),
            VM((160, 512), F32),
            VM((768, 1664), BF16),
            VM((9, 16, 384), BF16),
            VM((10, 13, 16, 128), BF16),
            VM((8, 13, 16, 128), F32),
            VM((6, 2, 7, 16, 128), BF16),
            VM((4, 12, 16, 128), F32),
            VM((5, 8, 16, 256), BF16),
            VM((2, 6, 16, 256), F32),
            VM((5, 9, 16, 512), BF16),
            VM((4, 8, 16, 256), BF16),
            VM((6, 14, 16, 128), BF16),
            VM((128, 1664), BF16),
            dma((2,)),
            dma((7,)),
            dma((8,)),
            dma((FR,)),
            dma((2, 6)),
        ],
        compiler_params=pltpu.CompilerParams(
            collective_id=0, has_side_effects=True, vmem_limit_bytes=44 << 20
        ),
        name="core",
    )(
        *(
            pltpu.with_memory_space_constraint(v, pltpu.HBM)
            for v in (conv_weight, features, target, w1, w2, w3, w4, head)
        )
    )


def final_body(pixels, s_ref, a_ref, b_ref, g_ref, out_hbm, wg_hbm, ad_hbm, back_hbm, buf, wg, ad, sem, side):
    sides = [
        pltpu.make_async_copy(g_ref, back_hbm, side.at[0]),
        pltpu.make_async_copy(wg, wg_hbm, side.at[1]),
        pltpu.make_async_copy(ad, ad_hbm, side.at[2]),
    ]
    sides[0].start()
    rec, gan = s_ref[0:32], s_ref[32:64]
    adaptive = jnp.sqrt(jnp.sum(rec * rec, keepdims=True)) / (
        jnp.sqrt(jnp.sum(gan * gan, keepdims=True)) + EPS
    )
    scale = jnp.broadcast_to(adaptive, (8, 128))[None]
    ad[...] = adaptive
    sides[2].start()
    for k in range(4):
        for f in range(4 * k, 4 * k + 4):
            v = a_ref[f].reshape(96, 8, 128) + scale * b_ref[f].reshape(96, 8, 128)
            buf[f] = v.reshape(16, W, 128).astype(BF16)
        pltpu.make_async_copy(buf.at[pl.ds(4 * k, 4)], out_hbm.at[pl.ds(4 * k, 4)], sem).start()
    mixed = (rec + adaptive * gan) / pixels
    for ab in range(9):
        wg[ab // 3, ab % 3] = mixed[ab * 3 : ab * 3 + 3]
    sides[1].start()
    drain(buf, sem)
    wait_all(sides)


def final(sums, a, b, back, pixels):
    hbm = lambda: pl.BlockSpec(memory_space=pltpu.HBM)
    return pl.pallas_call(
        functools.partial(final_body, pixels),
        out_shape=(
            jax.ShapeDtypeStruct((FR, 16, W, 128), BF16),
            jax.ShapeDtypeStruct((3, 3, 3, 128), F32),
            jax.ShapeDtypeStruct((1, 1), F32),
            jax.ShapeDtypeStruct((768, W), BF16),
        ),
        in_specs=[vspec()] * 4,
        out_specs=(hbm(), hbm(), hbm(), hbm()),
        scratch_shapes=[
            VM((FR, 16, W, 128), BF16),
            VM((3, 3, 3, 128), F32),
            VM((1, 1), F32),
            pltpu.SemaphoreType.DMA,
            pltpu.SemaphoreType.DMA((3,)),
        ],
        compiler_params=pltpu.CompilerParams(vmem_limit_bytes=24 << 20),
        name="final",
    )(sums, a, b, back)


def per_device(
    features, target, conv_weight, disc_first, disc_second, disc_third, disc_fourth, disc_head
):
    clips = lax.axis_size("clip")
    wanted = jnp.transpose(target[0], (0, 2, 1, 3)).reshape(768, W)
    w1 = jnp.transpose(disc_first, (0, 2, 1, 3))
    w2 = disc_second.reshape(4, 256, 128)
    w3 = disc_third.reshape(16, 128, 256)
    w4 = disc_fourth.reshape(16, 256, 512)
    head = disc_head.reshape(4, 4, 512)
    pixels = float(clips * FR * 256 * W)
    sums, a, b, back = core(conv_weight, features[0], wanted, w1, w2, w3, w4, head)
    feature_grad, weight_grad, adaptive, back = final(sums, a, b, back, pixels)
    image_back = jnp.transpose(back.reshape(1, FR, 3, 16, W), (0, 1, 3, 2, 4))
    return (feature_grad[None], image_back, weight_grad, adaptive[0, 0])


def solution(mesh):
    return jax.shard_map(
        per_device,
        mesh=mesh,
        in_specs=(
            P("clip", None, "row", None, None),
            P("clip", None, "row", None, None),
            P(),
            P(),
            P(),
            P(),
            P(),
            P(),
        ),
        out_specs=(
            P("clip", None, "row", None, None),
            P("clip", None, "row", None, None),
            P(),
            P(),
        ),
        check_vma=False,
    )
```

```python
import functools

import jax
import jax.numpy as jnp
from jax import lax
from jax.experimental import pallas as pl
from jax.experimental.pallas import tpu as pltpu
from jax.sharding import PartitionSpec as P

MESH = pl.DeviceIdType.MESH
F32 = jnp.float32
BF16 = jnp.bfloat16
SCALE = 64.0
EPS = 0.0001
FR = 16
W = 48
NT = (((1,), (1,)), ((), ()))
TN = (((0,), (0,)), ((), ()))
VM = pltpu.VMEM


def vspec():
    return pl.BlockSpec(memory_space=pltpu.VMEM)


def dot(a, b, dims=(((1,), (0,)), ((), ()))):
    return lax.dot_general(a, b, dims, preferred_element_type=F32)


def iota(shape, dim):
    return lax.broadcasted_iota(jnp.int32, shape, dim)


def rnd(v):
    return v.astype(BF16).astype(F32)


def down1(v):
    return jnp.where(iota(v.shape, 0) >= 1, pltpu.roll(v, 1, 0), 0.0)


def up1(v):
    n = v.shape[0]
    return jnp.where(iota(v.shape, 0) < n - 1, pltpu.roll(v, n - 1, 0), 0.0)


def lroll(v, s):
    s = s % v.shape[1]
    return v if s == 0 else pltpu.roll(v, s, 1)


def place(tiles, lane, src, dst):
    t, off = src // 128, src % 128
    v = lroll(tiles[t], dst - off)
    if off + W > 128:
        v = jnp.where(lane - dst < 128 - off, v, lroll(tiles[t + 1], dst - off))
    return jnp.where((lane >= dst) & (lane < dst + W), v, 0.0)


def spread(tiles, lane, v, src, dst):
    t, off = dst // 128, dst % 128
    v = lroll(jnp.where((lane >= src) & (lane < src + W), v, 0.0), off - src)
    if off + W > 128:
        tiles[t] = tiles[t] + jnp.where(lane >= off, v, 0.0)
        tiles[t + 1] = tiles[t + 1] + jnp.where(lane < off + W - 128, v, 0.0)
    else:
        tiles[t] = tiles[t] + v


def build_band(w1_ref, t1):
    t1[...] = jnp.zeros_like(t1)
    row = iota((16, 128), 0)
    lane = iota((16, 128), 1)
    for ao in range(12):
        w = w1_ref[ao // 3, ao % 3].astype(F32)
        left = jnp.concatenate([w, jnp.zeros((12, 64), F32)], 0)
        patch = jnp.concatenate([left, pltpu.roll(left, 2, 0)], 1)
        for s in (13, 1, 5, 9):
            rolled = pltpu.roll(patch, s, 0)
            parts = [(0, rolled)]
            if s == 13:
                parts = [(0, jnp.where(row >= 13, rolled, 0.0)), (1, jnp.where(row < 13, rolled, 0.0))]
            for v in range(13):
                start = 4 * v - 3
                if start % 16 != s:
                    continue
                for over, tile in parts:
                    g = start // 16 + over
                    if g < 0 or g > 2:
                        continue
                    if v == 0:
                        tile = jnp.where(lane >= 64, tile, 0.0)
                    if v == 12:
                        tile = jnp.where(lane < 64, tile, 0.0)
                    r0 = ao * 64 + g * 16
                    t1[r0 : r0 + 16, v * 128 : v * 128 + 128] = tile.astype(BF16)


def silu_pair(v):
    s = jax.nn.sigmoid(v)
    return v * s, s * (1.0 + v * (1.0 - s))


def rows16(v, k):
    return v[k * 16 : k * 16 + 16]


def head_term(head_ref, hg):
    rr = iota((160, 16), 0)
    tap = iota((160, 16), 1)
    y4 = 2 * (rr % 16) + rr // 80
    x4 = (rr % 80) // 16
    py = y4 + 1 - tap // 4
    px = x4 + 1 - tap % 4
    ok = (py >= 0) & (py <= 29) & (px >= 0) & (px <= 3) & (y4 <= 30)
    mask = jnp.where(ok, -SCALE, 0.0).astype(BF16)
    head = jnp.concatenate([head_ref[a].astype(F32) for a in range(4)], 0).astype(BF16)
    hg[...] = dot(mask, head)


def disc_stage(
    recv_ref, w2_ref, w3_ref, w4_ref, w3t, w4t, t1t, hg, out_ref, between,
    t1, pp, a1, s1, a2, s2, a3, s3, c4, c3, c2, c1,
):
    lane = iota((16, 128), 1)
    x = []
    for o in range(3):
        tiles = [recv_ref[pl.ds(3 * t + o, 16, stride=32), :] for t in range(7)]
        first = tiles[0] + recv_ref[pl.ds(21 + o, 16, stride=32), :]
        last = tiles[6] + recv_ref[pl.ds(24 + o, 16, stride=32), :]
        tiles[0] = first + jnp.where((lane >= W) & (lane < 2 * W), down1(last), 0.0)
        tiles[6] = last + jnp.where(lane < W, up1(first), 0.0)
        x.append([rnd(v) for v in tiles])
    halves = {}
    for m in range(16):
        s = 1 - m % 2
        for o in range(3):
            q = s * 3 + o
            halves[m, q] = place(x[o], lane, W * (m + 1), (q % 2) * 64)
    for i in range(9):
        piece = {}
        for q in range(6):
            m = 2 * i - 1 if q < 3 else 2 * i
            if m == -1:
                piece[q] = down1(halves[15, q])
            elif m == 16:
                piece[q] = up1(halves[0, q])
            else:
                piece[q] = halves[m, q]
        for j in range(3):
            pp[i, :, j * 128 : j * 128 + 128] = (piece[2 * j] + piece[2 * j + 1]).astype(BF16)
    lhs = jnp.concatenate([pp[0:8].reshape(128, 384), pp[1:9].reshape(128, 384)], 1)
    for v0 in range(0, 13, 2):
        n = min(2, 13 - v0)
        pre = dot(lhs, t1[:, v0 * 128 : (v0 + n) * 128])
        for v in range(v0, v0 + n):
            act, slope = silu_pair(pre[:, (v - v0) * 128 : (v - v0 + 1) * 128])
            s1[:, v] = slope.reshape(8, 16, 128)
            a1[1:9, v] = act.astype(BF16).reshape(8, 16, 128)
            a1[0, v] = down1(rows16(act, 7)).astype(BF16)
            a1[9, v] = up1(rows16(act, 0)).astype(BF16)
    zero = jnp.zeros((16, 128), BF16)
    for m in range(6):
        a2[m, 0, 0] = zero
        a2[m, 1, 6] = zero
        c2[m, 0] = zero
        c2[m, 13] = zero
    for m in range(4):
        lhs = jnp.concatenate(
            [a1[2 * m + a, k : k + 12].reshape(192, 128) for a in range(4) for k in range(2)], 1
        )
        pre = dot(lhs, w2_ref[...].reshape(1024, 128))
        act, slope = silu_pair(pre)
        s2[m] = slope.reshape(12, 16, 128)
        for c in range(12):
            v = rows16(act, c)
            e, p = (c + 1) % 2, (c + 1) // 2
            a2[m + 1, e, p] = v.astype(BF16)
            if m == 3:
                a2[0, e, p] = down1(v).astype(BF16)
            if m == 0:
                a2[5, e, p] = up1(v).astype(BF16)
    zero = jnp.zeros((16, 256), BF16)
    for k in range(5):
        a3[k, 0] = zero
        a3[k, 7] = zero
    for k in range(4):
        c3[k, 0] = zero
        c3[k, 7] = zero
    acc = None
    for a in range(4):
        lhs = jnp.concatenate(
            [
                jnp.concatenate(
                    [a2[2 * m + a, b % 2, b // 2 : b // 2 + 6].reshape(96, 128) for m in range(2)], 0
                )
                for b in range(4)
            ],
            1,
        )
        term = dot(lhs, w3_ref[a * 4 : a * 4 + 4].reshape(512, 256))
        acc = term if acc is None else acc + term
    act, slope = silu_pair(acc)
    s3[...] = slope.reshape(2, 6, 16, 256)
    for c in range(6):
        v0, v1 = rows16(act, c), rows16(act, 6 + c)
        a3[0, c + 1] = down1(v1).astype(BF16)
        a3[1, c + 1] = v0.astype(BF16)
        a3[2, c + 1] = v1.astype(BF16)
        a3[3, c + 1] = up1(v0).astype(BF16)
        a3[4, c + 1] = up1(v1).astype(BF16)
    acc = None
    for a in range(4):
        lhs = jnp.concatenate(
            [
                jnp.concatenate([a3[m + a, b : b + 5].reshape(80, 256) for m in range(2)], 0)
                for b in range(4)
            ],
            1,
        )
        term = dot(lhs, w4_ref[a * 4 : a * 4 + 4].reshape(1024, 512))
        acc = term if acc is None else acc + term
    _, slope = silu_pair(acc)
    cot = hg[...] * slope
    zero = jnp.zeros((16, 512), BF16)
    for k in range(5):
        for c in (0, 1, 7, 8):
            c4[k, c] = zero
    for c in range(5):
        v0, v1 = rows16(cot, c), rows16(cot, 5 + c)
        c4[0, c + 2] = down1(v0).astype(BF16)
        c4[1, c + 2] = down1(v1).astype(BF16)
        c4[2, c + 2] = v0.astype(BF16)
        c4[3, c + 2] = v1.astype(BF16)
        c4[4, c + 2] = up1(v0).astype(BF16)
    between()
    acc = None
    for a in range(4):
        lhs = jnp.concatenate(
            [
                jnp.concatenate(
                    [c4[m + 3 - a, 3 - b : 9 - b].reshape(96, 512) for m in range(2)], 0
                )
                for b in range(4)
            ],
            1,
        )
        term = dot(lhs, w4t[a * 4 : a * 4 + 4].reshape(2048, 256))
        acc = term if acc is None else acc + term
    cot = acc * s3[...].reshape(192, 256)
    for c in range(6):
        v0, v1 = rows16(cot, c), rows16(cot, 6 + c)
        c3[0, c + 1] = down1(v1).astype(BF16)
        c3[1, c + 1] = v0.astype(BF16)
        c3[2, c + 1] = v1.astype(BF16)
        c3[3, c + 1] = up1(v0).astype(BF16)
    for first in (0, 1):
        rows = (1, 3) if first == 0 else (0, 2)
        lhs = jnp.concatenate(
            [
                jnp.concatenate(
                    [c3[(m + 1 - a) // 2 + 1, off : off + 6].reshape(96, 256) for m in rows], 0
                )
                for a in (first, first + 2)
                for off in range(3)
            ],
            1,
        )
        rhs = jnp.concatenate([w3t[a].reshape(768, 256) for a in (first, first + 2)], 0)
        acc = dot(lhs, rhs)
        for n, m in enumerate(rows):
            for p in range(6):
                for e in range(2):
                    c = 2 * p + 1 - e
                    v = rows16(acc, n * 6 + p)[:, e * 128 : e * 128 + 128] * s2[m, c]
                    c2[m + 1, c + 1] = v.astype(BF16)
                    if m == 3:
                        c2[0, c + 1] = down1(v).astype(BF16)
                    if m == 0:
                        c2[5, c + 1] = up1(v).astype(BF16)
    for first in (0, 1):
        rhs = jnp.concatenate(
            [w2_ref[a, h * 128 : h * 128 + 128] for a in (first, first + 2) for h in range(2)], 1
        )
        for i in range(4):
            m = 2 * i + 1 - first
            lhs = jnp.concatenate(
                [
                    c2[(m + 1 - a) // 2 + 1, 1 - h : 14 - h].reshape(208, 128)
                    for a in (first, first + 2)
                    for h in range(2)
                ],
                1,
            )
            cot = dot(lhs, rhs, NT) * s1[m].reshape(208, 128)
            for v in range(13):
                c1[m * 16 : m * 16 + 16, v * 128 : v * 128 + 128] = rows16(cot, v).astype(BF16)
    grad = dot(c1[...], t1t[...])
    halves = {}
    for j in range(3):
        ps = []
        for i in range(9):
            v = None
            if i <= 7:
                v = grad[i * 16 : i * 16 + 16, j * 128 : j * 128 + 128]
            if i >= 1:
                u = grad[(i - 1) * 16 : i * 16, 384 + j * 128 : 512 + j * 128]
                v = u if v is None else v + u
            ps.append(v)
        for h in range(2):
            q = 2 * j + h
            for i in range(9):
                m = 2 * i - 1 if q < 3 else 2 * i
                if 0 <= m <= 15:
                    v = ps[i]
                    if m == 15:
                        v = v + up1(ps[0])
                    if m == 0:
                        v = v + down1(ps[8])
                    halves[m, q] = rnd(v)
    for o in range(3):
        tiles = [jnp.zeros((16, 128), F32) for _ in range(7)]
        for m in range(16):
            q = (1 - m % 2) * 3 + o
            spread(tiles, lane, halves[m, q], (q % 2) * 64, W * (m + 1))
        first, last = tiles[0], tiles[6]
        tiles[0] = first + jnp.where(lane < W, down1(last), 0.0)
        tiles[6] = last + jnp.where((lane >= W) & (lane < 2 * W), up1(first), 0.0)
        for t in range(7):
            out_ref[pl.ds(4 * t + o, 16, stride=32), :] = tiles[t]

def edge_mask(v, b, col):
    if b == 0:
        return jnp.where(col <= W - 2, v, 0.0)
    if b == 2:
        return jnp.where(col >= 1, v, 0.0)
    return v


def shifted(g, col):
    rows = []
    for ab in range(9):
        a, b = ab // 3, ab % 3
        rows.append(edge_mask(lroll(g, -((2 - a) * W + 1 - b))[:, 0:768], b, col))
    rows.append(jnp.zeros((8, 768), F32))
    return jnp.concatenate(rows, 0).astype(BF16)


def compact(dst, acc):
    dst[...] = jnp.zeros_like(dst)
    for ab in range(9):
        k = ab * 8
        dst[ab * 3 : ab * 3 + 3, :] = acc[k : k + 3, 0:128] + acc[k + 4 : k + 7, 128:256]


def drain(ref, sem):
    pltpu.make_async_copy(ref, ref, sem).wait()


def hops(d):
    return min(d, 4 - d)


ROW_OFFSETS = sorted(
    ((dy, dz) for dy in range(4) for dz in range(4) if dy or dz),
    key=lambda t: -(hops(t[0]) + hops(t[1])),
)
CLIP_OFFSETS = sorted(
    ((dx, dc) for dx in range(4) for dc in range(2) if dx or dc), key=lambda t: -(2 * hops(t[0]) + t[1])
)


def row_peers():
    r = lax.axis_index("row")
    y, z = r // 4, lax.rem(r, 4)
    return [lax.rem(y + dy, 4) * 4 + lax.rem(z + dz, 4) for dy, dz in ROW_OFFSETS]


def tree(parts):
    while len(parts) > 1:
        parts = [a + b for a, b in zip(parts[::2], parts[1::2])]
    return parts[0]


class Total:
    def __init__(self, src, clip_buf, row_buf, out, sems):
        clip, row = lax.axis_index("clip"), lax.axis_index("row")
        x, core = clip // 2, lax.rem(clip, 2)
        self.src, self.clip_buf, self.row_buf, self.out, self.sems = src, clip_buf, row_buf, out, sems
        self.clip, self.row = clip, row
        self.half = pl.ds(pl.multiple_of(core * 16, 16), 16)
        self.first = []
        for dx, dc in CLIP_OFFSETS:
            other = lax.rem(core + dc, 2)
            self.first.append(
                pltpu.make_async_remote_copy(
                    src_ref=src.at[pl.ds(pl.multiple_of(other * 16, 16), 16)],
                    dst_ref=clip_buf.at[clip],
                    send_sem=sems.at[0],
                    recv_sem=sems.at[1],
                    device_id={"clip": lax.rem(x + dx, 4) * 2 + other},
                    device_id_type=MESH,
                )
            )
        self.second = [
            pltpu.make_async_remote_copy(
                src_ref=row_buf.at[row],
                dst_ref=row_buf.at[row],
                send_sem=sems.at[2],
                recv_sem=sems.at[3],
                device_id={"row": peer},
                device_id_type=MESH,
            )
            for peer in row_peers()
        ]
        self.third = pltpu.make_async_remote_copy(
            src_ref=out.at[self.half],
            dst_ref=out.at[self.half],
            send_sem=sems.at[4],
            recv_sem=sems.at[5],
            device_id={"clip": x * 2 + 1 - core},
            device_id_type=MESH,
        )

    def start(self):
        start_all(self.first)
        self.clip_buf[self.clip] = self.src[self.half, :]

    def middle(self):
        for k in (1, 0):
            drain(self.clip_buf.at[pl.ds(0, 7)], self.sems.at[k])
        self.row_buf[self.row] = tree([self.clip_buf[k] for k in range(8)])
        start_all(self.second)

    def trade(self):
        for k in (3, 2):
            drain(self.row_buf.at[pl.ds(0, FR - 1)], self.sems.at[k])
        self.out[self.half, :] = tree([self.row_buf[k] for k in range(FR)])
        self.third.start()

    def finish(self):
        self.third.wait()


class EdgeExchange:
    def __init__(self, src, dst, send, got):
        r = lax.axis_index("row")
        self.src, self.dst, self.send, self.got = src, dst, send, got
        self.copies = [
            pltpu.make_async_remote_copy(
                src_ref=src.at[k],
                dst_ref=dst.at[1 - k],
                send_sem=send,
                recv_sem=got,
                device_id={"row": lax.rem(r + d, FR)},
                device_id_type=MESH,
            )
            for d, k in ((FR - 1, 0), (1, 1))
        ]

    def start(self):
        for c in self.copies:
            c.start()

    def wait(self):
        drain(self.dst, self.got)
        drain(self.src, self.send)


def start_all(copies):
    for c in copies:
        c.start()


def wait_all(copies):
    for c in copies:
        c.wait()


def core_body(
    w_hbm, f_hbm, t_hbm, w1_hbm, w2_hbm, w3_hbm, w4_hbm, head_hbm,
    sums_ref, a_ref, b_ref, back_ref,
    fs, w_ref, t_ref, w1_ref, w2s, w3s, w4s, head_ref, wm, parts, parts16, edges, recv, recvf, nb, wide, want, rec,
    redges, ne, msg, msgf, gan,
    gg, gts, xsum, clip_buf, row_buf, w3t, w4t, t1t, hg,
    t1, pp, a1, s1, a2, s2, a3, s3, c4, c3, c2, c1,
    fsem, wsem, xsem, gsem, tsem,
):
    r = lax.axis_index("row")
    clip = lax.axis_index("clip")
    y, z = r // 4, lax.rem(r, 4)
    weights = [
        pltpu.make_async_copy(a, b, wsem.at[k])
        for k, (a, b) in enumerate(
            (
                (w2_hbm, w2s), (w3_hbm, w3s), (w4_hbm, w4s), (head_hbm, head_ref),
                (w1_hbm, w1_ref), (t_hbm, t_ref), (w_hbm, w_ref),
            )
        )
    ]
    weights[6].start()
    start_all(weights[3:6])
    barrier = pltpu.get_barrier_semaphore()
    for d in range(1, FR):
        pl.semaphore_signal(
            barrier, inc=1, device_id={"row": lax.rem(r + d, FR)}, device_id_type=MESH
        )
    clips = 8
    for d in range(1, clips):
        pl.semaphore_signal(
            barrier, inc=1, device_id={"clip": lax.rem(clip + d, clips)}, device_id_type=MESH
        )
    pairs = [
        [yy * 4 + lax.rem(z + dz, 4) for dz in dzs for yy in range(2)] for dzs in ((2,), (1, 3), (0,))
    ]
    loads = [
        [
            pltpu.make_async_copy(f_hbm.at[f], fs.at[f], fsem.at[k])
            for p in group
            for f in (p, p + 8)
        ]
        for k, group in enumerate((pairs[0] + pairs[1][0:2], pairs[1][2:4] + pairs[2]))
    ]
    for group in loads:
        start_all(group)
    weights[6].wait()

    wm[...] = jnp.zeros_like(wm)
    for ab in range(9):
        v = w_ref[ab // 3, ab % 3].astype(F32)
        wm[ab * 8 : ab * 8 + 3, 0:128] = v
        wm[ab * 8 + 4 : ab * 8 + 7, 128:256] = v
    wmb = wm[...].astype(BF16)
    col = iota((8, 768), 1) % W
    lane = iota((16, 128), 1)
    pad = jnp.zeros((8, 128), F32)
    for k in range(27, 32):
        parts[:, k, :] = jnp.zeros((FR, 128), F32)

    def pair_features(p):
        return jnp.concatenate([fs[p].reshape(768, 128), fs[p + 8].reshape(768, 128)], 1)

    halves = (pairs[0] + pairs[1][0:2], pairs[1][2:4] + pairs[2])
    for k, group in enumerate(halves):
        drain(fs.at[pl.ds(0, 8)], fsem.at[k])
        if k == 0:
            weights[0].start()
            for n in range(8):
                part = pl.ds(2 * n, 2)
                pltpu.make_async_copy(w3_hbm.at[part], w3s.at[part], wsem.at[1]).start()
                pltpu.make_async_copy(w4_hbm.at[part], w4s.at[part], wsem.at[2]).start()
        for n, p in enumerate(group):
            if n % 2:
                out = dot(pair_features(p), wmb, NT).T
            else:
                out = dot(wmb, pair_features(p), NT)
            total = None
            for ab in range(9):
                a, b = ab // 3, ab % 3
                g = edge_mask(out[ab * 8 : ab * 8 + 8, :], b, col)
                g = lroll(jnp.concatenate([g, pad], 1), (2 - a) * W + 1 - b)
                total = g if total is None else total + g
            for h in range(2):
                f = p + 8 * h
                for t in range(7):
                    tile = total[4 * h : 4 * h + 3, t * 128 : t * 128 + 128]
                    parts[f, 3 * t : 3 * t + 3, :] = tile
                    if t in (0, 6):
                        parts[f, 21 + t // 2 : 24 + t // 2, :] = tile - rnd(tile)
                parts16[f] = parts[f].astype(BF16)
    pl.semaphore_wait(barrier, FR + clips - 2)
    for peer in row_peers():
        pltpu.make_async_remote_copy(
            src_ref=parts16.at[peer],
            dst_ref=recv.at[r],
            send_sem=xsem.at[0],
            recv_sem=xsem.at[1],
            device_id={"row": peer},
            device_id_type=MESH,
        ).start()
    pltpu.make_async_copy(parts16.at[r], recv.at[r], xsem.at[1]).start()
    flat = parts.reshape(FR * 32, 128)
    for t in (0, 6):
        for o in range(3):
            edges[t // 6, o] = flat[pl.ds(3 * t + o, 16, stride=32), :]
    ends = EdgeExchange(edges, nb, xsem.at[2], xsem.at[3])
    ends.start()

    weights[4].wait()
    build_band(w1_ref, t1)
    weights[5].wait()
    wide[:, 0:W] = t_ref[...].astype(F32)
    for o in range(3):
        tiles = [jnp.zeros((16, 128), F32) for _ in range(7)]
        for y in range(16):
            spread(tiles, lane, wide[pl.ds(o * 16 + y, 16, stride=48), :], 0, W * (y + 1))
        for t in range(7):
            want[t, o] = tiles[t]
    msgf[...] = jnp.zeros_like(msgf)
    wait_all(weights[0:4])
    head_term(head_ref, hg)
    for k in range(4):
        w3t[k, 2, :, 0:128] = w3s[k * 4].T
        w3t[k, 1, :, 0:128] = w3s[k * 4 + 2].T
        w3t[k, 1, :, 128:256] = w3s[k * 4 + 1].T
        w3t[k, 0, :, 128:256] = w3s[k * 4 + 3].T
        w3t[k, 2, :, 128:256] = jnp.zeros((256, 128), BF16)
        w3t[k, 0, :, 0:128] = jnp.zeros((256, 128), BF16)
    for k in range(16):
        w4t[k] = w4s[k].T
    for k in range(6):
        t1t[:, k * 128 : k * 128 + 128] = t1[k * 128 : k * 128 + 128, :].T
    rends = EdgeExchange(redges, ne, xsem.at[4], xsem.at[5])

    def reconstruction():
        ends.wait()
        for o in range(3):
            for t in range(7):
                v = flat[pl.ds(3 * t + o, 16, stride=32), :]
                if t == 0:
                    v = v + jnp.where((lane >= W) & (lane < 2 * W) & (r > 0), nb[0, o], 0.0)
                if t == 6:
                    v = v + jnp.where((lane < W) & (r < FR - 1), nb[1, o], 0.0)
                v = SCALE * (v - want[t, o])
                if t == 0:
                    v = jnp.where(lane >= W, v, 0.0)
                if t == 6:
                    v = jnp.where(lane < W, v, 0.0)
                rec[t, o] = v
                if t in (0, 6):
                    redges[t // 6, o] = v
        rends.start()

    drain(recv, xsem.at[1])
    drain(parts16.at[pl.ds(0, FR - 1)], xsem.at[0])
    recvf[...] = recv.reshape(FR * 32, 128)[...].astype(F32)

    disc_stage(
        recvf, w2s, w3s, w4s, w3t, w4t, t1t, hg, msgf, reconstruction,
        t1, pp, a1, s1, a2, s2, a3, s3, c4, c3, c2, c1,
    )
    msg.reshape(FR * 32, 128)[...] = msgf[...].astype(BF16)
    for peer in row_peers():
        pltpu.make_async_remote_copy(
            src_ref=msg.at[peer],
            dst_ref=gan.at[r],
            send_sem=xsem.at[6],
            recv_sem=gsem.at[r],
            device_id={"row": peer},
            device_id_type=MESH,
        ).start()
    pltpu.make_async_copy(msg.at[r], gan.at[r], gsem.at[r]).start()

    gg[...] = jnp.zeros_like(gg)
    rends.wait()

    for o in range(3):
        for t in range(7):
            v = rec[t, o]
            if t == 0:
                v = v + jnp.where((lane < W) & (r > 0), ne[0, o], 0.0)
            if t == 6:
                v = v + jnp.where((lane >= W) & (lane < 2 * W) & (r < FR - 1), ne[1, o], 0.0)
            gg[pl.ds(t * 8 + o, 8, stride=56), :] = v[0:8]
            gg[pl.ds(t * 8 + 4 + o, 8, stride=56), :] = v[8:16]

    def weight_part(g, p, acc):
        gt = shifted(g, col)
        gts[p] = gt
        term = dot(gt, pair_features(p))
        return term if acc is None else acc + term

    def feature_part(part_ref):
        for p in range(8):
            out = dot(gts[p], wmb, TN)
            part_ref[p] = out[:, 0:128]
            part_ref[p + 8] = out[:, 128:256]

    rec_total = Total(xsum.at[0], clip_buf.at[0], row_buf.at[0], sums_ref.at[pl.ds(0, 32)], tsem.at[0])
    gan_total = Total(xsum.at[1], clip_buf.at[1], row_buf.at[1], sums_ref.at[pl.ds(32, 32)], tsem.at[1])
    acc = None
    for p in range(8):
        g = jnp.concatenate([gg[p * 56 + t * 8 : p * 56 + t * 8 + 8, :] for t in range(7)], 1)
        acc = weight_part(g, p, acc)
    compact(xsum.at[0], acc)
    rec_total.start()
    feature_part(a_ref)

    low = iota((8, 128), 0) < 4
    acc = None
    for group in pairs[::-1]:
        for p in group:
            for f in (p, p + 8):
                drain(gan.at[f], gsem.at[f])
        for p in group:
            va, vb = gan[p].astype(F32), gan[p + 8].astype(F32)
            ua, ub = pltpu.roll(va, 28, 0), pltpu.roll(vb, 4, 0)
            tiles = []
            for t in range(7):
                k = t // 2 * 8
                if t % 2 == 0:
                    tiles.append(jnp.where(low, va[k : k + 8], ub[k : k + 8]))
                else:
                    tiles.append(jnp.where(low, ua[k : k + 8], vb[k : k + 8]))
            acc = weight_part(jnp.concatenate(tiles, 1), p, acc)
    compact(xsum.at[1], acc)
    gan_total.start()
    rec_total.middle()
    feature_part(b_ref)
    drain(msg.at[pl.ds(0, FR - 1)], xsem.at[6])
    msgf[...] = gan.reshape(FR * 32, 128)[...].astype(F32)
    for o in range(3):
        tiles = [msgf[pl.ds(4 * t + o, 16, stride=32), :] for t in range(7)]
        for y in range(16):
            wide[pl.ds(o * 16 + y, 16, stride=48), :] = place(tiles, lane, W * (y + 1), 0)
    back_ref[...] = wide[:, 0:W].astype(BF16)
    gan_total.middle()
    rec_total.trade()
    rec_total.finish()
    gan_total.trade()
    gan_total.finish()


def core(conv_weight, features, target, w1, w2, w3, w4, head):
    hbm = lambda: pl.BlockSpec(memory_space=pltpu.HBM)
    dma = pltpu.SemaphoreType.DMA
    return pl.pallas_call(
        core_body,
        out_shape=(
            VM((64, 128), F32),
            VM((FR, 768, 128), F32),
            VM((FR, 768, 128), F32),
            VM((768, W), BF16),
        ),
        in_specs=[hbm()] * 8,
        out_specs=(vspec(), vspec(), vspec(), vspec()),
        scratch_shapes=[
            VM((FR, 16, W, 128), BF16),
            VM((3, 3, 3, 128), BF16),
            VM((768, W), BF16),
            VM((4, 3, 4, 64), BF16),
            VM((4, 256, 128), BF16),
            VM((16, 128, 256), BF16),
            VM((16, 256, 512), BF16),
            VM((4, 4, 512), BF16),
            VM((80, 256), F32),
            VM((FR, 32, 128), F32),
            VM((FR, 32, 128), BF16),
            VM((2, 3, FR, 128), F32),
            VM((FR, 32, 128), BF16),
            VM((FR * 32, 128), F32),
            VM((2, 3, FR, 128), F32),
            VM((768, 128), F32),
            VM((7, 3, FR, 128), F32),
            VM((7, 3, FR, 128), F32),
            VM((2, 3, FR, 128), F32),
            VM((2, 3, FR, 128), F32),
            VM((FR, 32, 128), BF16),
            VM((FR * 32, 128), F32),
            VM((FR, 32, 128), BF16),
            VM((448, 128), F32),
            VM((8, 80, 768), BF16),
            VM((2, 32, 128), F32),
            VM((2, 8, 16, 128), F32),
            VM((2, FR, 16, 128), F32),
            VM((4, 3, 256, 256), BF16),
            VM((16, 512, 256), BF16),
            VM((1664, 768), BF16),
            VM((160, 512), F32),
            VM((768, 1664), BF16),
            VM((9, 16, 384), BF16),
            VM((10, 13, 16, 128), BF16),
            VM((8, 13, 16, 128), F32),
            VM((6, 2, 7, 16, 128), BF16),
            VM((4, 12, 16, 128), F32),
            VM((5, 8, 16, 256), BF16),
            VM((2, 6, 16, 256), F32),
            VM((5, 9, 16, 512), BF16),
            VM((4, 8, 16, 256), BF16),
            VM((6, 14, 16, 128), BF16),
            VM((128, 1664), BF16),
            dma((2,)),
            dma((7,)),
            dma((8,)),
            dma((FR,)),
            dma((2, 6)),
        ],
        compiler_params=pltpu.CompilerParams(
            collective_id=0, has_side_effects=True, vmem_limit_bytes=44 << 20
        ),
        name="core",
    )(
        *(
            pltpu.with_memory_space_constraint(v, pltpu.HBM)
            for v in (conv_weight, features, target, w1, w2, w3, w4, head)
        )
    )


def final_body(pixels, s_ref, a_ref, b_ref, g_ref, out_hbm, wg_hbm, ad_hbm, back_hbm, buf, wg, ad, sem, side):
    sides = [
        pltpu.make_async_copy(g_ref, back_hbm, side.at[0]),
        pltpu.make_async_copy(wg, wg_hbm, side.at[1]),
        pltpu.make_async_copy(ad, ad_hbm, side.at[2]),
    ]
    sides[0].start()
    rec, gan = s_ref[0:32], s_ref[32:64]
    adaptive = jnp.sqrt(jnp.sum(rec * rec, keepdims=True)) / (
        jnp.sqrt(jnp.sum(gan * gan, keepdims=True)) + EPS
    )
    scale = jnp.broadcast_to(adaptive, (8, 128))[None]
    ad[...] = adaptive
    sides[2].start()
    for k in range(4):
        for f in range(4 * k, 4 * k + 4):
            v = a_ref[f].reshape(96, 8, 128) + scale * b_ref[f].reshape(96, 8, 128)
            buf[f] = v.reshape(16, W, 128).astype(BF16)
        pltpu.make_async_copy(buf.at[pl.ds(4 * k, 4)], out_hbm.at[pl.ds(4 * k, 4)], sem).start()
    mixed = (rec + adaptive * gan) / pixels
    for ab in range(9):
        wg[ab // 3, ab % 3] = mixed[ab * 3 : ab * 3 + 3]
    sides[1].start()
    drain(buf, sem)
    wait_all(sides)


def final(sums, a, b, back, pixels):
    hbm = lambda: pl.BlockSpec(memory_space=pltpu.HBM)
    return pl.pallas_call(
        functools.partial(final_body, pixels),
        out_shape=(
            jax.ShapeDtypeStruct((FR, 16, W, 128), BF16),
            jax.ShapeDtypeStruct((3, 3, 3, 128), F32),
            jax.ShapeDtypeStruct((1, 1), F32),
            jax.ShapeDtypeStruct((768, W), BF16),
        ),
        in_specs=[vspec()] * 4,
        out_specs=(hbm(), hbm(), hbm(), hbm()),
        scratch_shapes=[
            VM((FR, 16, W, 128), BF16),
            VM((3, 3, 3, 128), F32),
            VM((1, 1), F32),
            pltpu.SemaphoreType.DMA,
            pltpu.SemaphoreType.DMA((3,)),
        ],
        compiler_params=pltpu.CompilerParams(vmem_limit_bytes=24 << 20),
        name="final",
    )(sums, a, b, back)


def per_device(
    features, target, conv_weight, disc_first, disc_second, disc_third, disc_fourth, disc_head
):
    clips = lax.axis_size("clip")
    wanted = jnp.transpose(target[0], (0, 2, 1, 3)).reshape(768, W)
    w1 = jnp.transpose(disc_first, (0, 2, 1, 3))
    w2 = disc_second.reshape(4, 256, 128)
    w3 = disc_third.reshape(16, 128, 256)
    w4 = disc_fourth.reshape(16, 256, 512)
    head = disc_head.reshape(4, 4, 512)
    pixels = float(clips * FR * 256 * W)
    sums, a, b, back = core(conv_weight, features[0], wanted, w1, w2, w3, w4, head)
    feature_grad, weight_grad, adaptive, back = final(sums, a, b, back, pixels)
    image_back = jnp.transpose(back.reshape(1, FR, 3, 16, W), (0, 1, 3, 2, 4))
    return (feature_grad[None], image_back, weight_grad, adaptive[0, 0])


def solution(mesh):
    return jax.shard_map(
        per_device,
        mesh=mesh,
        in_specs=(
            P("clip", None, "row", None, None),
            P("clip", None, "row", None, None),
            P(),
            P(),
            P(),
            P(),
            P(),
            P(),
        ),
        out_specs=(
            P("clip", None, "row", None, None),
            P("clip", None, "row", None, None),
            P(),
            P(),
        ),
        check_vma=False,
    )
```

```python
import functools

import jax
import jax.numpy as jnp
from jax import lax
from jax.experimental import pallas as pl
from jax.experimental.pallas import tpu as pltpu
from jax.sharding import PartitionSpec as P

MESH = pl.DeviceIdType.MESH
F32 = jnp.float32
BF16 = jnp.bfloat16
SCALE = 64.0
EPS = 0.0001
FR = 16
W = 48
NT = (((1,), (1,)), ((), ()))
TN = (((0,), (0,)), ((), ()))
VM = pltpu.VMEM


def vspec():
    return pl.BlockSpec(memory_space=pltpu.VMEM)


def dot(a, b, dims=(((1,), (0,)), ((), ()))):
    return lax.dot_general(a, b, dims, preferred_element_type=F32)


def iota(shape, dim):
    return lax.broadcasted_iota(jnp.int32, shape, dim)


def rnd(v):
    return v.astype(BF16).astype(F32)


def down1(v):
    return jnp.where(iota(v.shape, 0) >= 1, pltpu.roll(v, 1, 0), 0.0)


def up1(v):
    n = v.shape[0]
    return jnp.where(iota(v.shape, 0) < n - 1, pltpu.roll(v, n - 1, 0), 0.0)


def lroll(v, s):
    s = s % v.shape[1]
    return v if s == 0 else pltpu.roll(v, s, 1)


def place(tiles, lane, src, dst):
    t, off = src // 128, src % 128
    v = lroll(tiles[t], dst - off)
    if off + W > 128:
        v = jnp.where(lane - dst < 128 - off, v, lroll(tiles[t + 1], dst - off))
    return jnp.where((lane >= dst) & (lane < dst + W), v, 0.0)


def spread(tiles, lane, v, src, dst):
    t, off = dst // 128, dst % 128
    v = lroll(jnp.where((lane >= src) & (lane < src + W), v, 0.0), off - src)
    if off + W > 128:
        tiles[t] = tiles[t] + jnp.where(lane >= off, v, 0.0)
        tiles[t + 1] = tiles[t + 1] + jnp.where(lane < off + W - 128, v, 0.0)
    else:
        tiles[t] = tiles[t] + v


def build_band(w1_ref, t1):
    t1[...] = jnp.zeros_like(t1)
    row = iota((16, 128), 0)
    lane = iota((16, 128), 1)
    for ao in range(12):
        w = w1_ref[ao // 3, ao % 3].astype(F32)
        left = jnp.concatenate([w, jnp.zeros((12, 64), F32)], 0)
        patch = jnp.concatenate([left, pltpu.roll(left, 2, 0)], 1)
        for s in (13, 1, 5, 9):
            rolled = pltpu.roll(patch, s, 0)
            parts = [(0, rolled)]
            if s == 13:
                parts = [(0, jnp.where(row >= 13, rolled, 0.0)), (1, jnp.where(row < 13, rolled, 0.0))]
            for v in range(13):
                start = 4 * v - 3
                if start % 16 != s:
                    continue
                for over, tile in parts:
                    g = start // 16 + over
                    if g < 0 or g > 2:
                        continue
                    if v == 0:
                        tile = jnp.where(lane >= 64, tile, 0.0)
                    if v == 12:
                        tile = jnp.where(lane < 64, tile, 0.0)
                    r0 = ao * 64 + g * 16
                    t1[r0 : r0 + 16, v * 128 : v * 128 + 128] = tile.astype(BF16)


def silu_pair(v):
    s = jax.nn.sigmoid(v)
    return v * s, s * (1.0 + v * (1.0 - s))


def rows16(v, k):
    return v[k * 16 : k * 16 + 16]


def head_term(head_ref, hg):
    rr = iota((160, 16), 0)
    tap = iota((160, 16), 1)
    y4 = 2 * (rr % 16) + rr // 80
    x4 = (rr % 80) // 16
    py = y4 + 1 - tap // 4
    px = x4 + 1 - tap % 4
    ok = (py >= 0) & (py <= 29) & (px >= 0) & (px <= 3) & (y4 <= 30)
    mask = jnp.where(ok, -SCALE, 0.0).astype(BF16)
    head = jnp.concatenate([head_ref[a].astype(F32) for a in range(4)], 0).astype(BF16)
    hg[...] = dot(mask, head)


def disc_stage(
    recv_ref, w2_ref, w3_ref, w4_ref, w3t, w4t, t1t, hg, out_ref, between,
    t1, pp, a1, s1, a2, s2, a3, s3, c4, c3, c2, c1,
):
    lane = iota((16, 128), 1)
    x = []
    for o in range(3):
        tiles = [recv_ref[pl.ds(3 * t + o, 16, stride=32), :] for t in range(7)]
        first = tiles[0] + recv_ref[pl.ds(21 + o, 16, stride=32), :]
        last = tiles[6] + recv_ref[pl.ds(24 + o, 16, stride=32), :]
        tiles[0] = first + jnp.where((lane >= W) & (lane < 2 * W), down1(last), 0.0)
        tiles[6] = last + jnp.where(lane < W, up1(first), 0.0)
        x.append([rnd(v) for v in tiles])
    halves = {}
    for m in range(16):
        s = 1 - m % 2
        for o in range(3):
            q = s * 3 + o
            halves[m, q] = place(x[o], lane, W * (m + 1), (q % 2) * 64)
    for i in range(9):
        piece = {}
        for q in range(6):
            m = 2 * i - 1 if q < 3 else 2 * i
            if m == -1:
                piece[q] = down1(halves[15, q])
            elif m == 16:
                piece[q] = up1(halves[0, q])
            else:
                piece[q] = halves[m, q]
        for j in range(3):
            pp[i, :, j * 128 : j * 128 + 128] = (piece[2 * j] + piece[2 * j + 1]).astype(BF16)
    lhs = jnp.concatenate([pp[0:8].reshape(128, 384), pp[1:9].reshape(128, 384)], 1)
    for v0 in range(0, 13, 2):
        n = min(2, 13 - v0)
        pre = dot(lhs, t1[:, v0 * 128 : (v0 + n) * 128])
        for v in range(v0, v0 + n):
            act, slope = silu_pair(pre[:, (v - v0) * 128 : (v - v0 + 1) * 128])
            s1[:, v] = slope.reshape(8, 16, 128)
            a1[1:9, v] = act.astype(BF16).reshape(8, 16, 128)
            a1[0, v] = down1(rows16(act, 7)).astype(BF16)
            a1[9, v] = up1(rows16(act, 0)).astype(BF16)
    zero = jnp.zeros((16, 128), BF16)
    for m in range(6):
        a2[m, 0, 0] = zero
        a2[m, 1, 6] = zero
        c2[m, 0] = zero
        c2[m, 13] = zero
    for m in range(4):
        lhs = jnp.concatenate(
            [a1[2 * m + a, k : k + 12].reshape(192, 128) for a in range(4) for k in range(2)], 1
        )
        pre = dot(lhs, w2_ref[...].reshape(1024, 128))
        act, slope = silu_pair(pre)
        s2[m] = slope.reshape(12, 16, 128)
        for c in range(12):
            v = rows16(act, c)
            e, p = (c + 1) % 2, (c + 1) // 2
            a2[m + 1, e, p] = v.astype(BF16)
            if m == 3:
                a2[0, e, p] = down1(v).astype(BF16)
            if m == 0:
                a2[5, e, p] = up1(v).astype(BF16)
    zero = jnp.zeros((16, 256), BF16)
    for k in range(5):
        a3[k, 0] = zero
        a3[k, 7] = zero
    for k in range(4):
        c3[k, 0] = zero
        c3[k, 7] = zero
    acc = None
    for a in range(4):
        lhs = jnp.concatenate(
            [
                jnp.concatenate(
                    [a2[2 * m + a, b % 2, b // 2 : b // 2 + 6].reshape(96, 128) for m in range(2)], 0
                )
                for b in range(4)
            ],
            1,
        )
        term = dot(lhs, w3_ref[a * 4 : a * 4 + 4].reshape(512, 256))
        acc = term if acc is None else acc + term
    act, slope = silu_pair(acc)
    s3[...] = slope.reshape(2, 6, 16, 256)
    for c in range(6):
        v0, v1 = rows16(act, c), rows16(act, 6 + c)
        a3[0, c + 1] = down1(v1).astype(BF16)
        a3[1, c + 1] = v0.astype(BF16)
        a3[2, c + 1] = v1.astype(BF16)
        a3[3, c + 1] = up1(v0).astype(BF16)
        a3[4, c + 1] = up1(v1).astype(BF16)
    acc = None
    for a in range(4):
        lhs = jnp.concatenate(
            [
                jnp.concatenate([a3[m + a, b : b + 5].reshape(80, 256) for m in range(2)], 0)
                for b in range(4)
            ],
            1,
        )
        term = dot(lhs, w4_ref[a * 4 : a * 4 + 4].reshape(1024, 512))
        acc = term if acc is None else acc + term
    _, slope = silu_pair(acc)
    cot = hg[...] * slope
    zero = jnp.zeros((16, 512), BF16)
    for k in range(5):
        for c in (0, 1, 7, 8):
            c4[k, c] = zero
    for c in range(5):
        v0, v1 = rows16(cot, c), rows16(cot, 5 + c)
        c4[0, c + 2] = down1(v0).astype(BF16)
        c4[1, c + 2] = down1(v1).astype(BF16)
        c4[2, c + 2] = v0.astype(BF16)
        c4[3, c + 2] = v1.astype(BF16)
        c4[4, c + 2] = up1(v0).astype(BF16)
    between()
    acc = None
    for a in range(4):
        lhs = jnp.concatenate(
            [
                jnp.concatenate(
                    [c4[m + 3 - a, 3 - b : 9 - b].reshape(96, 512) for m in range(2)], 0
                )
                for b in range(4)
            ],
            1,
        )
        term = dot(lhs, w4t[a * 4 : a * 4 + 4].reshape(2048, 256))
        acc = term if acc is None else acc + term
    cot = acc * s3[...].reshape(192, 256)
    for c in range(6):
        v0, v1 = rows16(cot, c), rows16(cot, 6 + c)
        c3[0, c + 1] = down1(v1).astype(BF16)
        c3[1, c + 1] = v0.astype(BF16)
        c3[2, c + 1] = v1.astype(BF16)
        c3[3, c + 1] = up1(v0).astype(BF16)
    for first in (0, 1):
        rows = (1, 3) if first == 0 else (0, 2)
        lhs = jnp.concatenate(
            [
                jnp.concatenate(
                    [c3[(m + 1 - a) // 2 + 1, off : off + 6].reshape(96, 256) for m in rows], 0
                )
                for a in (first, first + 2)
                for off in range(3)
            ],
            1,
        )
        rhs = jnp.concatenate([w3t[a].reshape(768, 256) for a in (first, first + 2)], 0)
        acc = dot(lhs, rhs)
        for n, m in enumerate(rows):
            for p in range(6):
                for e in range(2):
                    c = 2 * p + 1 - e
                    v = rows16(acc, n * 6 + p)[:, e * 128 : e * 128 + 128] * s2[m, c]
                    c2[m + 1, c + 1] = v.astype(BF16)
                    if m == 3:
                        c2[0, c + 1] = down1(v).astype(BF16)
                    if m == 0:
                        c2[5, c + 1] = up1(v).astype(BF16)
    for first in (0, 1):
        rhs = jnp.concatenate(
            [w2_ref[a, h * 128 : h * 128 + 128] for a in (first, first + 2) for h in range(2)], 1
        )
        for i in range(4):
            m = 2 * i + 1 - first
            lhs = jnp.concatenate(
                [
                    c2[(m + 1 - a) // 2 + 1, 1 - h : 14 - h].reshape(208, 128)
                    for a in (first, first + 2)
                    for h in range(2)
                ],
                1,
            )
            cot = dot(lhs, rhs, NT) * s1[m].reshape(208, 128)
            for v in range(13):
                c1[m * 16 : m * 16 + 16, v * 128 : v * 128 + 128] = rows16(cot, v).astype(BF16)
    grad = dot(c1[...], t1t[...])
    halves = {}
    for j in range(3):
        ps = []
        for i in range(9):
            v = None
            if i <= 7:
                v = grad[i * 16 : i * 16 + 16, j * 128 : j * 128 + 128]
            if i >= 1:
                u = grad[(i - 1) * 16 : i * 16, 384 + j * 128 : 512 + j * 128]
                v = u if v is None else v + u
            ps.append(v)
        for h in range(2):
            q = 2 * j + h
            for i in range(9):
                m = 2 * i - 1 if q < 3 else 2 * i
                if 0 <= m <= 15:
                    v = ps[i]
                    if m == 15:
                        v = v + up1(ps[0])
                    if m == 0:
                        v = v + down1(ps[8])
                    halves[m, q] = rnd(v)
    for o in range(3):
        tiles = [jnp.zeros((16, 128), F32) for _ in range(7)]
        for m in range(16):
            q = (1 - m % 2) * 3 + o
            spread(tiles, lane, halves[m, q], (q % 2) * 64, W * (m + 1))
        first, last = tiles[0], tiles[6]
        tiles[0] = first + jnp.where(lane < W, down1(last), 0.0)
        tiles[6] = last + jnp.where((lane >= W) & (lane < 2 * W), up1(first), 0.0)
        for t in range(7):
            out_ref[pl.ds(4 * t + o, 16, stride=32), :] = tiles[t]

def edge_mask(v, b, col):
    if b == 0:
        return jnp.where(col <= W - 2, v, 0.0)
    if b == 2:
        return jnp.where(col >= 1, v, 0.0)
    return v


def shifted(g, col):
    rows = []
    for ab in range(9):
        a, b = ab // 3, ab % 3
        rows.append(edge_mask(lroll(g, -((2 - a) * W + 1 - b))[:, 0:768], b, col))
    rows.append(jnp.zeros((8, 768), F32))
    return jnp.concatenate(rows, 0).astype(BF16)


def compact(dst, acc):
    dst[...] = jnp.zeros_like(dst)
    for ab in range(9):
        k = ab * 8
        dst[ab * 3 : ab * 3 + 3, :] = acc[k : k + 3, 0:128] + acc[k + 4 : k + 7, 128:256]


def drain(ref, sem):
    pltpu.make_async_copy(ref, ref, sem).wait()


def hops(d):
    return min(d, 4 - d)


ROW_OFFSETS = sorted(
    ((dy, dz) for dy in range(4) for dz in range(4) if dy or dz),
    key=lambda t: -(hops(t[0]) + hops(t[1])),
)
CLIP_OFFSETS = sorted(
    ((dx, dc) for dx in range(4) for dc in range(2) if dx or dc), key=lambda t: -(2 * hops(t[0]) + t[1])
)


def row_peers():
    r = lax.axis_index("row")
    y, z = r // 4, lax.rem(r, 4)
    return [lax.rem(y + dy, 4) * 4 + lax.rem(z + dz, 4) for dy, dz in ROW_OFFSETS]


def tree(parts):
    while len(parts) > 1:
        parts = [a + b for a, b in zip(parts[::2], parts[1::2])]
    return parts[0]


class Total:
    def __init__(self, src, clip_buf, row_buf, out, sems):
        clip, row = lax.axis_index("clip"), lax.axis_index("row")
        x, core = clip // 2, lax.rem(clip, 2)
        self.src, self.clip_buf, self.row_buf, self.out, self.sems = src, clip_buf, row_buf, out, sems
        self.clip, self.row = clip, row
        self.half = pl.ds(pl.multiple_of(core * 16, 16), 16)
        self.first = []
        for dx, dc in CLIP_OFFSETS:
            other = lax.rem(core + dc, 2)
            self.first.append(
                pltpu.make_async_remote_copy(
                    src_ref=src.at[pl.ds(pl.multiple_of(other * 16, 16), 16)],
                    dst_ref=clip_buf.at[clip],
                    send_sem=sems.at[0],
                    recv_sem=sems.at[1],
                    device_id={"clip": lax.rem(x + dx, 4) * 2 + other},
                    device_id_type=MESH,
                )
            )
        self.second = [
            pltpu.make_async_remote_copy(
                src_ref=row_buf.at[row],
                dst_ref=row_buf.at[row],
                send_sem=sems.at[2],
                recv_sem=sems.at[3],
                device_id={"row": peer},
                device_id_type=MESH,
            )
            for peer in row_peers()
        ]
        self.third = pltpu.make_async_remote_copy(
            src_ref=out.at[self.half],
            dst_ref=out.at[self.half],
            send_sem=sems.at[4],
            recv_sem=sems.at[5],
            device_id={"clip": x * 2 + 1 - core},
            device_id_type=MESH,
        )

    def start(self):
        start_all(self.first)
        self.clip_buf[self.clip] = self.src[self.half, :]

    def middle(self):
        for k in (1, 0):
            drain(self.clip_buf.at[pl.ds(0, 7)], self.sems.at[k])
        self.row_buf[self.row] = tree([self.clip_buf[k] for k in range(8)])
        start_all(self.second)

    def trade(self):
        for k in (3, 2):
            drain(self.row_buf.at[pl.ds(0, FR - 1)], self.sems.at[k])
        self.out[self.half, :] = tree([self.row_buf[k] for k in range(FR)])
        self.third.start()

    def finish(self):
        self.third.wait()


class EdgeExchange:
    def __init__(self, src, dst, send, got):
        r = lax.axis_index("row")
        self.src, self.dst, self.send, self.got = src, dst, send, got
        self.copies = [
            pltpu.make_async_remote_copy(
                src_ref=src.at[k],
                dst_ref=dst.at[1 - k],
                send_sem=send,
                recv_sem=got,
                device_id={"row": lax.rem(r + d, FR)},
                device_id_type=MESH,
            )
            for d, k in ((FR - 1, 0), (1, 1))
        ]

    def start(self):
        for c in self.copies:
            c.start()

    def wait(self):
        drain(self.dst, self.got)
        drain(self.src, self.send)


def start_all(copies):
    for c in copies:
        c.start()


def wait_all(copies):
    for c in copies:
        c.wait()


def core_body(
    w_hbm, f_hbm, t_hbm, w1_hbm, w2_hbm, w3_hbm, w4_hbm, head_hbm,
    sums_ref, a_ref, b_ref, back_ref,
    fs, w_ref, t_ref, w1_ref, w2s, w3s, w4s, head_ref, wm, parts, parts16, edges, recv, recvf, nb, wide, want, rec,
    redges, ne, msg, msgf, gan,
    gg, gts, xsum, clip_buf, row_buf, w3t, w4t, t1t, hg,
    t1, pp, a1, s1, a2, s2, a3, s3, c4, c3, c2, c1,
    fsem, wsem, xsem, gsem, tsem,
):
    r = lax.axis_index("row")
    clip = lax.axis_index("clip")
    y, z = r // 4, lax.rem(r, 4)
    weights = [
        pltpu.make_async_copy(a, b, wsem.at[k])
        for k, (a, b) in enumerate(
            (
                (w2_hbm, w2s), (w3_hbm, w3s), (w4_hbm, w4s), (head_hbm, head_ref),
                (w1_hbm, w1_ref), (t_hbm, t_ref), (w_hbm, w_ref),
            )
        )
    ]
    weights[6].start()
    start_all(weights[3:6])
    barrier = pltpu.get_barrier_semaphore()
    for d in range(1, FR):
        pl.semaphore_signal(
            barrier, inc=1, device_id={"row": lax.rem(r + d, FR)}, device_id_type=MESH
        )
    clips = 8
    for d in range(1, clips):
        pl.semaphore_signal(
            barrier, inc=1, device_id={"clip": lax.rem(clip + d, clips)}, device_id_type=MESH
        )
    pairs = [
        [yy * 4 + lax.rem(z + dz, 4) for dz in dzs for yy in range(2)] for dzs in ((2,), (1, 3), (0,))
    ]
    loads = [
        [
            pltpu.make_async_copy(f_hbm.at[f], fs.at[f], fsem.at[k])
            for p in group
            for f in (p, p + 8)
        ]
        for k, group in enumerate((pairs[0] + pairs[1][0:2], pairs[1][2:4] + pairs[2]))
    ]
    for group in loads:
        start_all(group)
    weights[6].wait()

    wm[...] = jnp.zeros_like(wm)
    for ab in range(9):
        v = w_ref[ab // 3, ab % 3].astype(F32)
        wm[ab * 8 : ab * 8 + 3, 0:128] = v
        wm[ab * 8 + 4 : ab * 8 + 7, 128:256] = v
    wmb = wm[...].astype(BF16)
    col = iota((8, 768), 1) % W
    lane = iota((16, 128), 1)
    pad = jnp.zeros((8, 128), F32)
    for k in range(27, 32):
        parts[:, k, :] = jnp.zeros((FR, 128), F32)

    def pair_features(p):
        return jnp.concatenate([fs[p].reshape(768, 128), fs[p + 8].reshape(768, 128)], 1)

    halves = (pairs[0] + pairs[1][0:2], pairs[1][2:4] + pairs[2])
    for k, group in enumerate(halves):
        drain(fs.at[pl.ds(0, 8)], fsem.at[k])
        if k == 0:
            weights[0].start()
            for n in range(8):
                part = pl.ds(2 * n, 2)
                pltpu.make_async_copy(w3_hbm.at[part], w3s.at[part], wsem.at[1]).start()
                pltpu.make_async_copy(w4_hbm.at[part], w4s.at[part], wsem.at[2]).start()
        for n, p in enumerate(group):
            if n % 2:
                out = dot(pair_features(p), wmb, NT).T
            else:
                out = dot(wmb, pair_features(p), NT)
            total = None
            for ab in range(9):
                a, b = ab // 3, ab % 3
                g = edge_mask(out[ab * 8 : ab * 8 + 8, :], b, col)
                g = lroll(jnp.concatenate([g, pad], 1), (2 - a) * W + 1 - b)
                total = g if total is None else total + g
            for h in range(2):
                f = p + 8 * h
                for t in range(7):
                    tile = total[4 * h : 4 * h + 3, t * 128 : t * 128 + 128]
                    parts[f, 3 * t : 3 * t + 3, :] = tile
                    if t in (0, 6):
                        parts[f, 21 + t // 2 : 24 + t // 2, :] = tile - rnd(tile)
                parts16[f] = parts[f].astype(BF16)
        if k == 0:
            pl.semaphore_wait(barrier, FR + clips - 2)
        for peer, (_, dz) in zip(row_peers(), ROW_OFFSETS):
            if (dz in (1, 2)) == (k == 0):
                pltpu.make_async_remote_copy(
                    src_ref=parts16.at[peer],
                    dst_ref=recv.at[r],
                    send_sem=xsem.at[0],
                    recv_sem=xsem.at[1],
                    device_id={"row": peer},
                    device_id_type=MESH,
                ).start()
    pltpu.make_async_copy(parts16.at[r], recv.at[r], xsem.at[1]).start()
    flat = parts.reshape(FR * 32, 128)
    for t in (0, 6):
        for o in range(3):
            edges[t // 6, o] = flat[pl.ds(3 * t + o, 16, stride=32), :]
    ends = EdgeExchange(edges, nb, xsem.at[2], xsem.at[3])
    ends.start()

    weights[4].wait()
    build_band(w1_ref, t1)
    weights[5].wait()
    wide[:, 0:W] = t_ref[...].astype(F32)
    for o in range(3):
        tiles = [jnp.zeros((16, 128), F32) for _ in range(7)]
        for y in range(16):
            spread(tiles, lane, wide[pl.ds(o * 16 + y, 16, stride=48), :], 0, W * (y + 1))
        for t in range(7):
            want[t, o] = tiles[t]
    msgf[...] = jnp.zeros_like(msgf)
    wait_all(weights[0:4])
    head_term(head_ref, hg)
    for k in range(4):
        w3t[k, 2, :, 0:128] = w3s[k * 4].T
        w3t[k, 1, :, 0:128] = w3s[k * 4 + 2].T
        w3t[k, 1, :, 128:256] = w3s[k * 4 + 1].T
        w3t[k, 0, :, 128:256] = w3s[k * 4 + 3].T
        w3t[k, 2, :, 128:256] = jnp.zeros((256, 128), BF16)
        w3t[k, 0, :, 0:128] = jnp.zeros((256, 128), BF16)
    for k in range(16):
        w4t[k] = w4s[k].T
    for k in range(6):
        t1t[:, k * 128 : k * 128 + 128] = t1[k * 128 : k * 128 + 128, :].T
    rends = EdgeExchange(redges, ne, xsem.at[4], xsem.at[5])

    def reconstruction():
        ends.wait()
        for o in range(3):
            for t in range(7):
                v = flat[pl.ds(3 * t + o, 16, stride=32), :]
                if t == 0:
                    v = v + jnp.where((lane >= W) & (lane < 2 * W) & (r > 0), nb[0, o], 0.0)
                if t == 6:
                    v = v + jnp.where((lane < W) & (r < FR - 1), nb[1, o], 0.0)
                v = SCALE * (v - want[t, o])
                if t == 0:
                    v = jnp.where(lane >= W, v, 0.0)
                if t == 6:
                    v = jnp.where(lane < W, v, 0.0)
                rec[t, o] = v
                if t in (0, 6):
                    redges[t // 6, o] = v
        rends.start()

    drain(recv, xsem.at[1])
    drain(parts16.at[pl.ds(0, FR - 1)], xsem.at[0])
    recvf[...] = recv.reshape(FR * 32, 128)[...].astype(F32)

    disc_stage(
        recvf, w2s, w3s, w4s, w3t, w4t, t1t, hg, msgf, reconstruction,
        t1, pp, a1, s1, a2, s2, a3, s3, c4, c3, c2, c1,
    )
    msg.reshape(FR * 32, 128)[...] = msgf[...].astype(BF16)
    for peer, (_, dz) in zip(row_peers(), ROW_OFFSETS):
        pltpu.make_async_remote_copy(
            src_ref=msg.at[peer],
            dst_ref=gan.at[r],
            send_sem=xsem.at[6],
            recv_sem=gsem.at[hops(dz)],
            device_id={"row": peer},
            device_id_type=MESH,
        ).start()
    pltpu.make_async_copy(msg.at[r], gan.at[r], gsem.at[0]).start()

    gg[...] = jnp.zeros_like(gg)
    rends.wait()

    for o in range(3):
        for t in range(7):
            v = rec[t, o]
            if t == 0:
                v = v + jnp.where((lane < W) & (r > 0), ne[0, o], 0.0)
            if t == 6:
                v = v + jnp.where((lane >= W) & (lane < 2 * W) & (r < FR - 1), ne[1, o], 0.0)
            gg[pl.ds(t * 8 + o, 8, stride=56), :] = v[0:8]
            gg[pl.ds(t * 8 + 4 + o, 8, stride=56), :] = v[8:16]

    def weight_part(g, p, acc):
        gt = shifted(g, col)
        gts[p] = gt
        term = dot(gt, pair_features(p))
        return term if acc is None else acc + term

    def feature_part(part_ref):
        for p in range(8):
            out = dot(gts[p], wmb, TN)
            part_ref[p] = out[:, 0:128]
            part_ref[p + 8] = out[:, 128:256]

    rec_total = Total(xsum.at[0], clip_buf.at[0], row_buf.at[0], sums_ref.at[pl.ds(0, 32)], tsem.at[0])
    gan_total = Total(xsum.at[1], clip_buf.at[1], row_buf.at[1], sums_ref.at[pl.ds(32, 32)], tsem.at[1])
    acc = None
    for p in range(8):
        g = jnp.concatenate([gg[p * 56 + t * 8 : p * 56 + t * 8 + 8, :] for t in range(7)], 1)
        acc = weight_part(g, p, acc)
    compact(xsum.at[0], acc)
    rec_total.start()
    feature_part(a_ref)

    low = iota((8, 128), 0) < 4
    acc = None
    for k, group in enumerate(pairs[::-1]):
        drain(gan.at[pl.ds(0, 2 * len(group))], gsem.at[k])
        for p in group:
            va, vb = gan[p].astype(F32), gan[p + 8].astype(F32)
            ua, ub = pltpu.roll(va, 28, 0), pltpu.roll(vb, 4, 0)
            tiles = []
            for t in range(7):
                k = t // 2 * 8
                if t % 2 == 0:
                    tiles.append(jnp.where(low, va[k : k + 8], ub[k : k + 8]))
                else:
                    tiles.append(jnp.where(low, ua[k : k + 8], vb[k : k + 8]))
            acc = weight_part(jnp.concatenate(tiles, 1), p, acc)
    compact(xsum.at[1], acc)
    gan_total.start()
    rec_total.middle()
    feature_part(b_ref)
    drain(msg.at[pl.ds(0, FR - 1)], xsem.at[6])
    msgf[...] = gan.reshape(FR * 32, 128)[...].astype(F32)
    for o in range(3):
        tiles = [msgf[pl.ds(4 * t + o, 16, stride=32), :] for t in range(7)]
        for y in range(16):
            wide[pl.ds(o * 16 + y, 16, stride=48), :] = place(tiles, lane, W * (y + 1), 0)
    back_ref[...] = wide[:, 0:W].astype(BF16)
    gan_total.middle()
    rec_total.trade()
    rec_total.finish()
    gan_total.trade()
    gan_total.finish()


def core(conv_weight, features, target, w1, w2, w3, w4, head):
    hbm = lambda: pl.BlockSpec(memory_space=pltpu.HBM)
    dma = pltpu.SemaphoreType.DMA
    return pl.pallas_call(
        core_body,
        out_shape=(
            VM((64, 128), F32),
            VM((FR, 768, 128), F32),
            VM((FR, 768, 128), F32),
            VM((768, W), BF16),
        ),
        in_specs=[hbm()] * 8,
        out_specs=(vspec(), vspec(), vspec(), vspec()),
        scratch_shapes=[
            VM((FR, 16, W, 128), BF16),
            VM((3, 3, 3, 128), BF16),
            VM((768, W), BF16),
            VM((4, 3, 4, 64), BF16),
            VM((4, 256, 128), BF16),
            VM((16, 128, 256), BF16),
            VM((16, 256, 512), BF16),
            VM((4, 4, 512), BF16),
            VM((80, 256), F32),
            VM((FR, 32, 128), F32),
            VM((FR, 32, 128), BF16),
            VM((2, 3, FR, 128), F32),
            VM((FR, 32, 128), BF16),
            VM((FR * 32, 128), F32),
            VM((2, 3, FR, 128), F32),
            VM((768, 128), F32),
            VM((7, 3, FR, 128), F32),
            VM((7, 3, FR, 128), F32),
            VM((2, 3, FR, 128), F32),
            VM((2, 3, FR, 128), F32),
            VM((FR, 32, 128), BF16),
            VM((FR * 32, 128), F32),
            VM((FR, 32, 128), BF16),
            VM((448, 128), F32),
            VM((8, 80, 768), BF16),
            VM((2, 32, 128), F32),
            VM((2, 8, 16, 128), F32),
            VM((2, FR, 16, 128), F32),
            VM((4, 3, 256, 256), BF16),
            VM((16, 512, 256), BF16),
            VM((1664, 768), BF16),
            VM((160, 512), F32),
            VM((768, 1664), BF16),
            VM((9, 16, 384), BF16),
            VM((10, 13, 16, 128), BF16),
            VM((8, 13, 16, 128), F32),
            VM((6, 2, 7, 16, 128), BF16),
            VM((4, 12, 16, 128), F32),
            VM((5, 8, 16, 256), BF16),
            VM((2, 6, 16, 256), F32),
            VM((5, 9, 16, 512), BF16),
            VM((4, 8, 16, 256), BF16),
            VM((6, 14, 16, 128), BF16),
            VM((128, 1664), BF16),
            dma((2,)),
            dma((7,)),
            dma((8,)),
            dma((3,)),
            dma((2, 6)),
        ],
        compiler_params=pltpu.CompilerParams(
            collective_id=0, has_side_effects=True, vmem_limit_bytes=44 << 20
        ),
        name="core",
    )(
        *(
            pltpu.with_memory_space_constraint(v, pltpu.HBM)
            for v in (conv_weight, features, target, w1, w2, w3, w4, head)
        )
    )


def final_body(pixels, s_ref, a_ref, b_ref, g_ref, out_hbm, wg_hbm, ad_hbm, back_hbm, buf, wg, ad, sem, side):
    sides = [
        pltpu.make_async_copy(g_ref, back_hbm, side.at[0]),
        pltpu.make_async_copy(wg, wg_hbm, side.at[1]),
        pltpu.make_async_copy(ad, ad_hbm, side.at[2]),
    ]
    sides[0].start()
    rec, gan = s_ref[0:32], s_ref[32:64]
    adaptive = jnp.sqrt(jnp.sum(rec * rec, keepdims=True)) / (
        jnp.sqrt(jnp.sum(gan * gan, keepdims=True)) + EPS
    )
    scale = jnp.broadcast_to(adaptive, (8, 128))[None]
    ad[...] = adaptive
    sides[2].start()
    for f in range(FR):
        v = a_ref[f].reshape(96, 8, 128) + scale * b_ref[f].reshape(96, 8, 128)
        buf[f] = v.reshape(16, W, 128).astype(BF16)
        pltpu.make_async_copy(buf.at[f], out_hbm.at[f], sem).start()
    mixed = (rec + adaptive * gan) / pixels
    for ab in range(9):
        wg[ab // 3, ab % 3] = mixed[ab * 3 : ab * 3 + 3]
    sides[1].start()
    drain(buf, sem)
    wait_all(sides)


def final(sums, a, b, back, pixels):
    hbm = lambda: pl.BlockSpec(memory_space=pltpu.HBM)
    return pl.pallas_call(
        functools.partial(final_body, pixels),
        out_shape=(
            jax.ShapeDtypeStruct((FR, 16, W, 128), BF16),
            jax.ShapeDtypeStruct((3, 3, 3, 128), F32),
            jax.ShapeDtypeStruct((1, 1), F32),
            jax.ShapeDtypeStruct((768, W), BF16),
        ),
        in_specs=[vspec()] * 4,
        out_specs=(hbm(), hbm(), hbm(), hbm()),
        scratch_shapes=[
            VM((FR, 16, W, 128), BF16),
            VM((3, 3, 3, 128), F32),
            VM((1, 1), F32),
            pltpu.SemaphoreType.DMA,
            pltpu.SemaphoreType.DMA((3,)),
        ],
        compiler_params=pltpu.CompilerParams(vmem_limit_bytes=24 << 20),
        name="final",
    )(sums, a, b, back)


def per_device(
    features, target, conv_weight, disc_first, disc_second, disc_third, disc_fourth, disc_head
):
    clips = lax.axis_size("clip")
    wanted = jnp.transpose(target[0], (0, 2, 1, 3)).reshape(768, W)
    w1 = jnp.transpose(disc_first, (0, 2, 1, 3))
    w2 = disc_second.reshape(4, 256, 128)
    w3 = disc_third.reshape(16, 128, 256)
    w4 = disc_fourth.reshape(16, 256, 512)
    head = disc_head.reshape(4, 4, 512)
    pixels = float(clips * FR * 256 * W)
    sums, a, b, back = core(conv_weight, features[0], wanted, w1, w2, w3, w4, head)
    feature_grad, weight_grad, adaptive, back = final(sums, a, b, back, pixels)
    image_back = jnp.transpose(back.reshape(1, FR, 3, 16, W), (0, 1, 3, 2, 4))
    return (feature_grad[None], image_back, weight_grad, adaptive[0, 0])


def solution(mesh):
    return jax.shard_map(
        per_device,
        mesh=mesh,
        in_specs=(
            P("clip", None, "row", None, None),
            P("clip", None, "row", None, None),
            P(),
            P(),
            P(),
            P(),
            P(),
            P(),
        ),
        out_specs=(
            P("clip", None, "row", None, None),
            P("clip", None, "row", None, None),
            P(),
            P(),
        ),
        check_vma=False,
    )
```

```python
import functools

import jax
import jax.numpy as jnp
from jax import lax
from jax.experimental import pallas as pl
from jax.experimental.pallas import tpu as pltpu
from jax.sharding import PartitionSpec as P

MESH = pl.DeviceIdType.MESH
F32 = jnp.float32
BF16 = jnp.bfloat16
SCALE = 64.0
EPS = 0.0001
FR = 16
W = 48
NT = (((1,), (1,)), ((), ()))
TN = (((0,), (0,)), ((), ()))
VM = pltpu.VMEM


def vspec():
    return pl.BlockSpec(memory_space=pltpu.VMEM)


def dot(a, b, dims=(((1,), (0,)), ((), ()))):
    return lax.dot_general(a, b, dims, preferred_element_type=F32)


def iota(shape, dim):
    return lax.broadcasted_iota(jnp.int32, shape, dim)


def rnd(v):
    return v.astype(BF16).astype(F32)


def down1(v):
    return jnp.where(iota(v.shape, 0) >= 1, pltpu.roll(v, 1, 0), 0.0)


def up1(v):
    n = v.shape[0]
    return jnp.where(iota(v.shape, 0) < n - 1, pltpu.roll(v, n - 1, 0), 0.0)


def lroll(v, s):
    s = s % v.shape[1]
    return v if s == 0 else pltpu.roll(v, s, 1)


def place(tiles, lane, src, dst):
    t, off = src // 128, src % 128
    v = lroll(tiles[t], dst - off)
    if off + W > 128:
        v = jnp.where(lane - dst < 128 - off, v, lroll(tiles[t + 1], dst - off))
    return jnp.where((lane >= dst) & (lane < dst + W), v, 0.0)


def spread(tiles, lane, v, src, dst):
    t, off = dst // 128, dst % 128
    v = lroll(jnp.where((lane >= src) & (lane < src + W), v, 0.0), off - src)
    if off + W > 128:
        tiles[t] = tiles[t] + jnp.where(lane >= off, v, 0.0)
        tiles[t + 1] = tiles[t + 1] + jnp.where(lane < off + W - 128, v, 0.0)
    else:
        tiles[t] = tiles[t] + v


def build_band(w1_ref, t1):
    t1[...] = jnp.zeros_like(t1)
    row = iota((16, 128), 0)
    lane = iota((16, 128), 1)
    for ao in range(12):
        w = w1_ref[ao // 3, ao % 3].astype(F32)
        left = jnp.concatenate([w, jnp.zeros((12, 64), F32)], 0)
        patch = jnp.concatenate([left, pltpu.roll(left, 2, 0)], 1)
        for s in (13, 1, 5, 9):
            rolled = pltpu.roll(patch, s, 0)
            parts = [(0, rolled)]
            if s == 13:
                parts = [(0, jnp.where(row >= 13, rolled, 0.0)), (1, jnp.where(row < 13, rolled, 0.0))]
            for v in range(13):
                start = 4 * v - 3
                if start % 16 != s:
                    continue
                for over, tile in parts:
                    g = start // 16 + over
                    if g < 0 or g > 2:
                        continue
                    if v == 0:
                        tile = jnp.where(lane >= 64, tile, 0.0)
                    if v == 12:
                        tile = jnp.where(lane < 64, tile, 0.0)
                    r0 = ao * 64 + g * 16
                    t1[r0 : r0 + 16, v * 128 : v * 128 + 128] = tile.astype(BF16)


def silu_pair(v):
    s = jax.nn.sigmoid(v)
    return v * s, s * (1.0 + v * (1.0 - s))


def rows16(v, k):
    return v[k * 16 : k * 16 + 16]


def head_term(head_ref, hg):
    rr = iota((160, 16), 0)
    tap = iota((160, 16), 1)
    y4 = 2 * (rr % 16) + rr // 80
    x4 = (rr % 80) // 16
    py = y4 + 1 - tap // 4
    px = x4 + 1 - tap % 4
    ok = (py >= 0) & (py <= 29) & (px >= 0) & (px <= 3) & (y4 <= 30)
    mask = jnp.where(ok, -SCALE, 0.0).astype(BF16)
    head = jnp.concatenate([head_ref[a].astype(F32) for a in range(4)], 0).astype(BF16)
    hg[...] = dot(mask, head)


def disc_stage(
    recv_ref, w2_ref, w3_ref, w4_ref, w3t, w4t, t1t, hg, out_ref, between,
    t1, pp, a1, s1, a2, s2, a3, s3, c4, c3, c2, c1,
):
    lane = iota((16, 128), 1)
    x = []
    for o in range(3):
        tiles = [recv_ref[pl.ds(3 * t + o, 16, stride=32), :] for t in range(7)]
        first = tiles[0] + recv_ref[pl.ds(21 + o, 16, stride=32), :]
        last = tiles[6] + recv_ref[pl.ds(24 + o, 16, stride=32), :]
        tiles[0] = first + jnp.where((lane >= W) & (lane < 2 * W), down1(last), 0.0)
        tiles[6] = last + jnp.where(lane < W, up1(first), 0.0)
        x.append([rnd(v) for v in tiles])
    halves = {}
    for m in range(16):
        s = 1 - m % 2
        for o in range(3):
            q = s * 3 + o
            halves[m, q] = place(x[o], lane, W * (m + 1), (q % 2) * 64)
    for i in range(9):
        piece = {}
        for q in range(6):
            m = 2 * i - 1 if q < 3 else 2 * i
            if m == -1:
                piece[q] = down1(halves[15, q])
            elif m == 16:
                piece[q] = up1(halves[0, q])
            else:
                piece[q] = halves[m, q]
        for j in range(3):
            pp[i, :, j * 128 : j * 128 + 128] = (piece[2 * j] + piece[2 * j + 1]).astype(BF16)
    lhs = jnp.concatenate([pp[0:8].reshape(128, 384), pp[1:9].reshape(128, 384)], 1)
    for v0 in range(0, 13, 2):
        n = min(2, 13 - v0)
        pre = dot(lhs, t1[:, v0 * 128 : (v0 + n) * 128])
        for v in range(v0, v0 + n):
            act, slope = silu_pair(pre[:, (v - v0) * 128 : (v - v0 + 1) * 128])
            s1[:, v] = slope.reshape(8, 16, 128)
            a1[1:9, v] = act.astype(BF16).reshape(8, 16, 128)
            a1[0, v] = down1(rows16(act, 7)).astype(BF16)
            a1[9, v] = up1(rows16(act, 0)).astype(BF16)
    zero = jnp.zeros((16, 128), BF16)
    for m in range(6):
        a2[m, 0, 0] = zero
        a2[m, 1, 6] = zero
        c2[m, 0] = zero
        c2[m, 13] = zero
    for m in range(4):
        lhs = jnp.concatenate(
            [a1[2 * m + a, k : k + 12].reshape(192, 128) for a in range(4) for k in range(2)], 1
        )
        pre = dot(lhs, w2_ref[...].reshape(1024, 128))
        act, slope = silu_pair(pre)
        s2[m] = slope.reshape(12, 16, 128)
        for c in range(12):
            v = rows16(act, c)
            e, p = (c + 1) % 2, (c + 1) // 2
            a2[m + 1, e, p] = v.astype(BF16)
            if m == 3:
                a2[0, e, p] = down1(v).astype(BF16)
            if m == 0:
                a2[5, e, p] = up1(v).astype(BF16)
    zero = jnp.zeros((16, 256), BF16)
    for k in range(5):
        a3[k, 0] = zero
        a3[k, 7] = zero
    for k in range(4):
        c3[k, 0] = zero
        c3[k, 7] = zero
    acc = None
    for a in range(4):
        lhs = jnp.concatenate(
            [
                jnp.concatenate(
                    [a2[2 * m + a, b % 2, b // 2 : b // 2 + 6].reshape(96, 128) for m in range(2)], 0
                )
                for b in range(4)
            ],
            1,
        )
        term = dot(lhs, w3_ref[a * 4 : a * 4 + 4].reshape(512, 256))
        acc = term if acc is None else acc + term
    act, slope = silu_pair(acc)
    s3[...] = slope.reshape(2, 6, 16, 256)
    for c in range(6):
        v0, v1 = rows16(act, c), rows16(act, 6 + c)
        a3[0, c + 1] = down1(v1).astype(BF16)
        a3[1, c + 1] = v0.astype(BF16)
        a3[2, c + 1] = v1.astype(BF16)
        a3[3, c + 1] = up1(v0).astype(BF16)
        a3[4, c + 1] = up1(v1).astype(BF16)
    acc = None
    for a in range(4):
        lhs = jnp.concatenate(
            [
                jnp.concatenate([a3[m + a, b : b + 5].reshape(80, 256) for m in range(2)], 0)
                for b in range(4)
            ],
            1,
        )
        term = dot(lhs, w4_ref[a * 4 : a * 4 + 4].reshape(1024, 512))
        acc = term if acc is None else acc + term
    _, slope = silu_pair(acc)
    cot = hg[...] * slope
    zero = jnp.zeros((16, 512), BF16)
    for k in range(5):
        for c in (0, 1, 7, 8):
            c4[k, c] = zero
    for c in range(5):
        v0, v1 = rows16(cot, c), rows16(cot, 5 + c)
        c4[0, c + 2] = down1(v0).astype(BF16)
        c4[1, c + 2] = down1(v1).astype(BF16)
        c4[2, c + 2] = v0.astype(BF16)
        c4[3, c + 2] = v1.astype(BF16)
        c4[4, c + 2] = up1(v0).astype(BF16)
    between()
    acc = None
    for a in range(4):
        lhs = jnp.concatenate(
            [
                jnp.concatenate(
                    [c4[m + 3 - a, 3 - b : 9 - b].reshape(96, 512) for m in range(2)], 0
                )
                for b in range(4)
            ],
            1,
        )
        term = dot(lhs, w4t[a * 4 : a * 4 + 4].reshape(2048, 256))
        acc = term if acc is None else acc + term
    cot = acc * s3[...].reshape(192, 256)
    for c in range(6):
        v0, v1 = rows16(cot, c), rows16(cot, 6 + c)
        c3[0, c + 1] = down1(v1).astype(BF16)
        c3[1, c + 1] = v0.astype(BF16)
        c3[2, c + 1] = v1.astype(BF16)
        c3[3, c + 1] = up1(v0).astype(BF16)
    for first in (0, 1):
        rows = (1, 3) if first == 0 else (0, 2)
        lhs = jnp.concatenate(
            [
                jnp.concatenate(
                    [c3[(m + 1 - a) // 2 + 1, off : off + 6].reshape(96, 256) for m in rows], 0
                )
                for a in (first, first + 2)
                for off in range(3)
            ],
            1,
        )
        rhs = jnp.concatenate([w3t[a].reshape(768, 256) for a in (first, first + 2)], 0)
        acc = dot(lhs, rhs)
        for n, m in enumerate(rows):
            for p in range(6):
                for e in range(2):
                    c = 2 * p + 1 - e
                    v = rows16(acc, n * 6 + p)[:, e * 128 : e * 128 + 128] * s2[m, c]
                    c2[m + 1, c + 1] = v.astype(BF16)
                    if m == 3:
                        c2[0, c + 1] = down1(v).astype(BF16)
                    if m == 0:
                        c2[5, c + 1] = up1(v).astype(BF16)
    for first in (0, 1):
        rhs = jnp.concatenate(
            [w2_ref[a, h * 128 : h * 128 + 128] for a in (first, first + 2) for h in range(2)], 1
        )
        for i in range(4):
            m = 2 * i + 1 - first
            lhs = jnp.concatenate(
                [
                    c2[(m + 1 - a) // 2 + 1, 1 - h : 14 - h].reshape(208, 128)
                    for a in (first, first + 2)
                    for h in range(2)
                ],
                1,
            )
            cot = dot(lhs, rhs, NT) * s1[m].reshape(208, 128)
            for v in range(13):
                c1[m * 16 : m * 16 + 16, v * 128 : v * 128 + 128] = rows16(cot, v).astype(BF16)
    grad = dot(c1[...], t1t[...])
    halves = {}
    for j in range(3):
        ps = []
        for i in range(9):
            v = None
            if i <= 7:
                v = grad[i * 16 : i * 16 + 16, j * 128 : j * 128 + 128]
            if i >= 1:
                u = grad[(i - 1) * 16 : i * 16, 384 + j * 128 : 512 + j * 128]
                v = u if v is None else v + u
            ps.append(v)
        for h in range(2):
            q = 2 * j + h
            for i in range(9):
                m = 2 * i - 1 if q < 3 else 2 * i
                if 0 <= m <= 15:
                    v = ps[i]
                    if m == 15:
                        v = v + up1(ps[0])
                    if m == 0:
                        v = v + down1(ps[8])
                    halves[m, q] = rnd(v)
    for o in range(3):
        tiles = [jnp.zeros((16, 128), F32) for _ in range(7)]
        for m in range(16):
            q = (1 - m % 2) * 3 + o
            spread(tiles, lane, halves[m, q], (q % 2) * 64, W * (m + 1))
        first, last = tiles[0], tiles[6]
        tiles[0] = first + jnp.where(lane < W, down1(last), 0.0)
        tiles[6] = last + jnp.where((lane >= W) & (lane < 2 * W), up1(first), 0.0)
        for t in range(7):
            out_ref[pl.ds(4 * t + o, 16, stride=32), :] = tiles[t]

def edge_mask(v, b, col):
    if b == 0:
        return jnp.where(col <= W - 2, v, 0.0)
    if b == 2:
        return jnp.where(col >= 1, v, 0.0)
    return v


def shifted(g, col):
    rows = []
    for ab in range(9):
        a, b = ab // 3, ab % 3
        rows.append(edge_mask(lroll(g, -((2 - a) * W + 1 - b))[:, 0:768], b, col))
    rows.append(jnp.zeros((8, 768), F32))
    return jnp.concatenate(rows, 0).astype(BF16)


def compact(dst, acc):
    dst[...] = jnp.zeros_like(dst)
    for ab in range(9):
        k = ab * 8
        dst[ab * 3 : ab * 3 + 3, :] = acc[k : k + 3, 0:128] + acc[k + 4 : k + 7, 128:256]


def drain(ref, sem):
    pltpu.make_async_copy(ref, ref, sem).wait()


def hops(d):
    return min(d, 4 - d)


ROW_OFFSETS = sorted(
    ((dy, dz) for dy in range(4) for dz in range(4) if dy or dz),
    key=lambda t: -(hops(t[0]) + hops(t[1])),
)
CLIP_OFFSETS = sorted(
    ((dx, dc) for dx in range(4) for dc in range(2) if dx or dc), key=lambda t: -(2 * hops(t[0]) + t[1])
)


def row_peers():
    r = lax.axis_index("row")
    y, z = r // 4, lax.rem(r, 4)
    return [lax.rem(y + dy, 4) * 4 + lax.rem(z + dz, 4) for dy, dz in ROW_OFFSETS]


def tree(parts):
    while len(parts) > 1:
        parts = [a + b for a, b in zip(parts[::2], parts[1::2])]
    return parts[0]


class Total:
    def __init__(self, src, clip_buf, row_buf, out, sems):
        clip, row = lax.axis_index("clip"), lax.axis_index("row")
        x, core = clip // 2, lax.rem(clip, 2)
        self.src, self.clip_buf, self.row_buf, self.out, self.sems = src, clip_buf, row_buf, out, sems
        self.clip, self.row = clip, row
        self.half = pl.ds(pl.multiple_of(core * 16, 16), 16)
        self.first = []
        for dx, dc in CLIP_OFFSETS:
            other = lax.rem(core + dc, 2)
            self.first.append(
                pltpu.make_async_remote_copy(
                    src_ref=src.at[pl.ds(pl.multiple_of(other * 16, 16), 16)],
                    dst_ref=clip_buf.at[clip],
                    send_sem=sems.at[0],
                    recv_sem=sems.at[1],
                    device_id={"clip": lax.rem(x + dx, 4) * 2 + other},
                    device_id_type=MESH,
                )
            )
        self.second = [
            pltpu.make_async_remote_copy(
                src_ref=row_buf.at[row],
                dst_ref=row_buf.at[row],
                send_sem=sems.at[2],
                recv_sem=sems.at[3],
                device_id={"row": peer},
                device_id_type=MESH,
            )
            for peer in row_peers()
        ]
        self.third = pltpu.make_async_remote_copy(
            src_ref=out.at[self.half],
            dst_ref=out.at[self.half],
            send_sem=sems.at[4],
            recv_sem=sems.at[5],
            device_id={"clip": x * 2 + 1 - core},
            device_id_type=MESH,
        )

    def start(self):
        start_all(self.first)
        self.clip_buf[self.clip] = self.src[self.half, :]

    def middle(self):
        for k in (1, 0):
            drain(self.clip_buf.at[pl.ds(0, 7)], self.sems.at[k])
        self.row_buf[self.row] = tree([self.clip_buf[k] for k in range(8)])
        start_all(self.second)

    def trade(self):
        for k in (3, 2):
            drain(self.row_buf.at[pl.ds(0, FR - 1)], self.sems.at[k])
        self.out[self.half, :] = tree([self.row_buf[k] for k in range(FR)])
        self.third.start()

    def finish(self):
        self.third.wait()


class EdgeExchange:
    def __init__(self, src, dst, send, got):
        r = lax.axis_index("row")
        self.src, self.dst, self.send, self.got = src, dst, send, got
        self.copies = [
            pltpu.make_async_remote_copy(
                src_ref=src.at[k],
                dst_ref=dst.at[1 - k],
                send_sem=send,
                recv_sem=got,
                device_id={"row": lax.rem(r + d, FR)},
                device_id_type=MESH,
            )
            for d, k in ((FR - 1, 0), (1, 1))
        ]

    def start(self):
        for c in self.copies:
            c.start()

    def wait(self):
        drain(self.dst, self.got)
        drain(self.src, self.send)


def start_all(copies):
    for c in copies:
        c.start()


def wait_all(copies):
    for c in copies:
        c.wait()


def core_body(
    w_hbm, f_hbm, t_hbm, w1_hbm, w2_hbm, w3_hbm, w4_hbm, head_hbm,
    sums_ref, a_ref, b_ref, back_ref,
    fs, w_ref, t_ref, w1_ref, w2s, w3s, w4s, head_ref, wm, parts, parts16, edges, recv, recvf, nb, wide, want, rec,
    redges, ne, msg, msgf, gan,
    gg, gts, xsum, clip_buf, row_buf, w3t, w4t, t1t, hg,
    t1, pp, a1, s1, a2, s2, a3, s3, c4, c3, c2, c1,
    fsem, wsem, xsem, gsem, tsem,
):
    r = lax.axis_index("row")
    clip = lax.axis_index("clip")
    y, z = r // 4, lax.rem(r, 4)
    weights = [
        pltpu.make_async_copy(a, b, wsem.at[k])
        for k, (a, b) in enumerate(
            (
                (w2_hbm, w2s), (w3_hbm, w3s), (w4_hbm, w4s), (head_hbm, head_ref),
                (w1_hbm, w1_ref), (t_hbm, t_ref), (w_hbm, w_ref),
            )
        )
    ]
    weights[6].start()
    start_all(weights[3:6])
    barrier = pltpu.get_barrier_semaphore()
    for d in range(1, FR):
        pl.semaphore_signal(
            barrier, inc=1, device_id={"row": lax.rem(r + d, FR)}, device_id_type=MESH
        )
    clips = 8
    for d in range(1, clips):
        pl.semaphore_signal(
            barrier, inc=1, device_id={"clip": lax.rem(clip + d, clips)}, device_id_type=MESH
        )
    pairs = [
        [yy * 4 + lax.rem(z + dz, 4) for dz in dzs for yy in range(2)] for dzs in ((2,), (1, 3), (0,))
    ]
    loads = [
        [
            pltpu.make_async_copy(f_hbm.at[f], fs.at[f], fsem.at[k])
            for p in group
            for f in (p, p + 8)
        ]
        for k, group in enumerate((pairs[0] + pairs[1][0:2], pairs[1][2:4] + pairs[2]))
    ]
    for group in loads:
        start_all(group)
    weights[6].wait()

    wm[...] = jnp.zeros_like(wm)
    for ab in range(9):
        v = w_ref[ab // 3, ab % 3].astype(F32)
        wm[ab * 8 : ab * 8 + 3, 0:128] = v
        wm[ab * 8 + 4 : ab * 8 + 7, 128:256] = v
    wmb = wm[...].astype(BF16)
    col = iota((8, 768), 1) % W
    lane = iota((16, 128), 1)
    pad = jnp.zeros((8, 128), F32)
    for k in range(27, 32):
        parts[:, k, :] = jnp.zeros((FR, 128), F32)

    def pair_features(p):
        return jnp.concatenate([fs[p].reshape(768, 128), fs[p + 8].reshape(768, 128)], 1)

    steps = ((pairs[0] + pairs[1][0:2], (1, 2)), (pairs[1][2:4], (3,)), (pairs[2], (0,)))
    for k, (group, sent) in enumerate(steps):
        if k < 2:
            drain(fs.at[pl.ds(0, 8)], fsem.at[k])
        if k == 0:
            weights[0].start()
            for n in range(8):
                part = pl.ds(2 * n, 2)
                pltpu.make_async_copy(w3_hbm.at[part], w3s.at[part], wsem.at[1]).start()
                pltpu.make_async_copy(w4_hbm.at[part], w4s.at[part], wsem.at[2]).start()
        for n, p in enumerate(group):
            if n % 2:
                out = dot(pair_features(p), wmb, NT).T
            else:
                out = dot(wmb, pair_features(p), NT)
            total = None
            for ab in range(9):
                a, b = ab // 3, ab % 3
                g = edge_mask(out[ab * 8 : ab * 8 + 8, :], b, col)
                g = lroll(jnp.concatenate([g, pad], 1), (2 - a) * W + 1 - b)
                total = g if total is None else total + g
            for h in range(2):
                f = p + 8 * h
                for t in range(7):
                    tile = total[4 * h : 4 * h + 3, t * 128 : t * 128 + 128]
                    parts[f, 3 * t : 3 * t + 3, :] = tile
                    if t in (0, 6):
                        parts[f, 21 + t // 2 : 24 + t // 2, :] = tile - rnd(tile)
                parts16[f] = parts[f].astype(BF16)
        if k == 0:
            pl.semaphore_wait(barrier, FR + clips - 2)
        for peer, (_, dz) in zip(row_peers(), ROW_OFFSETS):
            if dz in sent:
                pltpu.make_async_remote_copy(
                    src_ref=parts16.at[peer],
                    dst_ref=recv.at[r],
                    send_sem=xsem.at[0],
                    recv_sem=xsem.at[1],
                    device_id={"row": peer},
                    device_id_type=MESH,
                ).start()
    pltpu.make_async_copy(parts16.at[r], recv.at[r], xsem.at[1]).start()
    flat = parts.reshape(FR * 32, 128)
    for t in (0, 6):
        for o in range(3):
            edges[t // 6, o] = flat[pl.ds(3 * t + o, 16, stride=32), :]
    ends = EdgeExchange(edges, nb, xsem.at[2], xsem.at[3])
    ends.start()

    weights[4].wait()
    build_band(w1_ref, t1)
    weights[5].wait()
    wide[:, 0:W] = t_ref[...].astype(F32)
    for o in range(3):
        tiles = [jnp.zeros((16, 128), F32) for _ in range(7)]
        for y in range(16):
            spread(tiles, lane, wide[pl.ds(o * 16 + y, 16, stride=48), :], 0, W * (y + 1))
        for t in range(7):
            want[t, o] = tiles[t]
    msgf[...] = jnp.zeros_like(msgf)
    wait_all(weights[0:4])
    head_term(head_ref, hg)
    for k in range(4):
        w3t[k, 2, :, 0:128] = w3s[k * 4].T
        w3t[k, 1, :, 0:128] = w3s[k * 4 + 2].T
        w3t[k, 1, :, 128:256] = w3s[k * 4 + 1].T
        w3t[k, 0, :, 128:256] = w3s[k * 4 + 3].T
        w3t[k, 2, :, 128:256] = jnp.zeros((256, 128), BF16)
        w3t[k, 0, :, 0:128] = jnp.zeros((256, 128), BF16)
    for k in range(16):
        w4t[k] = w4s[k].T
    for k in range(6):
        t1t[:, k * 128 : k * 128 + 128] = t1[k * 128 : k * 128 + 128, :].T
    rends = EdgeExchange(redges, ne, xsem.at[4], xsem.at[5])

    def reconstruction():
        ends.wait()
        for o in range(3):
            for t in range(7):
                v = flat[pl.ds(3 * t + o, 16, stride=32), :]
                if t == 0:
                    v = v + jnp.where((lane >= W) & (lane < 2 * W) & (r > 0), nb[0, o], 0.0)
                if t == 6:
                    v = v + jnp.where((lane < W) & (r < FR - 1), nb[1, o], 0.0)
                v = SCALE * (v - want[t, o])
                if t == 0:
                    v = jnp.where(lane >= W, v, 0.0)
                if t == 6:
                    v = jnp.where(lane < W, v, 0.0)
                rec[t, o] = v
                if t in (0, 6):
                    redges[t // 6, o] = v
        rends.start()

    drain(recv, xsem.at[1])
    drain(parts16.at[pl.ds(0, FR - 1)], xsem.at[0])
    recvf[...] = recv.reshape(FR * 32, 128)[...].astype(F32)

    disc_stage(
        recvf, w2s, w3s, w4s, w3t, w4t, t1t, hg, msgf, reconstruction,
        t1, pp, a1, s1, a2, s2, a3, s3, c4, c3, c2, c1,
    )
    msg.reshape(FR * 32, 128)[...] = msgf[...].astype(BF16)
    for peer, (_, dz) in zip(row_peers(), ROW_OFFSETS):
        pltpu.make_async_remote_copy(
            src_ref=msg.at[peer],
            dst_ref=gan.at[r],
            send_sem=xsem.at[6],
            recv_sem=gsem.at[hops(dz)],
            device_id={"row": peer},
            device_id_type=MESH,
        ).start()
    pltpu.make_async_copy(msg.at[r], gan.at[r], gsem.at[0]).start()

    gg[...] = jnp.zeros_like(gg)
    rends.wait()

    for o in range(3):
        for t in range(7):
            v = rec[t, o]
            if t == 0:
                v = v + jnp.where((lane < W) & (r > 0), ne[0, o], 0.0)
            if t == 6:
                v = v + jnp.where((lane >= W) & (lane < 2 * W) & (r < FR - 1), ne[1, o], 0.0)
            gg[pl.ds(t * 8 + o, 8, stride=56), :] = v[0:8]
            gg[pl.ds(t * 8 + 4 + o, 8, stride=56), :] = v[8:16]

    def weight_part(g, p, acc):
        gt = shifted(g, col)
        gts[p] = gt
        term = dot(gt, pair_features(p))
        return term if acc is None else acc + term

    def feature_part(part_ref):
        for p in range(8):
            out = dot(gts[p], wmb, TN)
            part_ref[p] = out[:, 0:128]
            part_ref[p + 8] = out[:, 128:256]

    rec_total = Total(xsum.at[0], clip_buf.at[0], row_buf.at[0], sums_ref.at[pl.ds(0, 32)], tsem.at[0])
    gan_total = Total(xsum.at[1], clip_buf.at[1], row_buf.at[1], sums_ref.at[pl.ds(32, 32)], tsem.at[1])
    acc = None
    for p in range(8):
        g = jnp.concatenate([gg[p * 56 + t * 8 : p * 56 + t * 8 + 8, :] for t in range(7)], 1)
        acc = weight_part(g, p, acc)
    compact(xsum.at[0], acc)
    rec_total.start()
    feature_part(a_ref)

    low = iota((8, 128), 0) < 4
    acc = None
    for k, group in enumerate(pairs[::-1]):
        drain(gan.at[pl.ds(0, 2 * len(group))], gsem.at[k])
        for p in group:
            va, vb = gan[p].astype(F32), gan[p + 8].astype(F32)
            ua, ub = pltpu.roll(va, 28, 0), pltpu.roll(vb, 4, 0)
            tiles = []
            for t in range(7):
                k = t // 2 * 8
                if t % 2 == 0:
                    tiles.append(jnp.where(low, va[k : k + 8], ub[k : k + 8]))
                else:
                    tiles.append(jnp.where(low, ua[k : k + 8], vb[k : k + 8]))
            acc = weight_part(jnp.concatenate(tiles, 1), p, acc)
    compact(xsum.at[1], acc)
    gan_total.start()
    rec_total.middle()
    feature_part(b_ref)
    drain(msg.at[pl.ds(0, FR - 1)], xsem.at[6])
    msgf[...] = gan.reshape(FR * 32, 128)[...].astype(F32)
    for o in range(3):
        tiles = [msgf[pl.ds(4 * t + o, 16, stride=32), :] for t in range(7)]
        for y in range(16):
            wide[pl.ds(o * 16 + y, 16, stride=48), :] = place(tiles, lane, W * (y + 1), 0)
    back_ref[...] = wide[:, 0:W].astype(BF16)
    gan_total.middle()
    rec_total.trade()
    rec_total.finish()
    gan_total.trade()
    gan_total.finish()


def core(conv_weight, features, target, w1, w2, w3, w4, head):
    hbm = lambda: pl.BlockSpec(memory_space=pltpu.HBM)
    dma = pltpu.SemaphoreType.DMA
    return pl.pallas_call(
        core_body,
        out_shape=(
            VM((64, 128), F32),
            VM((FR, 768, 128), F32),
            VM((FR, 768, 128), F32),
            VM((768, W), BF16),
        ),
        in_specs=[hbm()] * 8,
        out_specs=(vspec(), vspec(), vspec(), vspec()),
        scratch_shapes=[
            VM((FR, 16, W, 128), BF16),
            VM((3, 3, 3, 128), BF16),
            VM((768, W), BF16),
            VM((4, 3, 4, 64), BF16),
            VM((4, 256, 128), BF16),
            VM((16, 128, 256), BF16),
            VM((16, 256, 512), BF16),
            VM((4, 4, 512), BF16),
            VM((80, 256), F32),
            VM((FR, 32, 128), F32),
            VM((FR, 32, 128), BF16),
            VM((2, 3, FR, 128), F32),
            VM((FR, 32, 128), BF16),
            VM((FR * 32, 128), F32),
            VM((2, 3, FR, 128), F32),
            VM((768, 128), F32),
            VM((7, 3, FR, 128), F32),
            VM((7, 3, FR, 128), F32),
            VM((2, 3, FR, 128), F32),
            VM((2, 3, FR, 128), F32),
            VM((FR, 32, 128), BF16),
            VM((FR * 32, 128), F32),
            VM((FR, 32, 128), BF16),
            VM((448, 128), F32),
            VM((8, 80, 768), BF16),
            VM((2, 32, 128), F32),
            VM((2, 8, 16, 128), F32),
            VM((2, FR, 16, 128), F32),
            VM((4, 3, 256, 256), BF16),
            VM((16, 512, 256), BF16),
            VM((1664, 768), BF16),
            VM((160, 512), F32),
            VM((768, 1664), BF16),
            VM((9, 16, 384), BF16),
            VM((10, 13, 16, 128), BF16),
            VM((8, 13, 16, 128), F32),
            VM((6, 2, 7, 16, 128), BF16),
            VM((4, 12, 16, 128), F32),
            VM((5, 8, 16, 256), BF16),
            VM((2, 6, 16, 256), F32),
            VM((5, 9, 16, 512), BF16),
            VM((4, 8, 16, 256), BF16),
            VM((6, 14, 16, 128), BF16),
            VM((128, 1664), BF16),
            dma((2,)),
            dma((7,)),
            dma((8,)),
            dma((3,)),
            dma((2, 6)),
        ],
        compiler_params=pltpu.CompilerParams(
            collective_id=0, has_side_effects=True, vmem_limit_bytes=44 << 20
        ),
        name="core",
    )(
        *(
            pltpu.with_memory_space_constraint(v, pltpu.HBM)
            for v in (conv_weight, features, target, w1, w2, w3, w4, head)
        )
    )


def final_body(pixels, s_ref, a_ref, b_ref, g_ref, out_hbm, wg_hbm, ad_hbm, back_hbm, buf, wg, ad, sem, side):
    sides = [
        pltpu.make_async_copy(g_ref, back_hbm, side.at[0]),
        pltpu.make_async_copy(wg, wg_hbm, side.at[1]),
        pltpu.make_async_copy(ad, ad_hbm, side.at[2]),
    ]
    sides[0].start()
    rec, gan = s_ref[0:32], s_ref[32:64]
    adaptive = jnp.sqrt(jnp.sum(rec * rec, keepdims=True)) / (
        jnp.sqrt(jnp.sum(gan * gan, keepdims=True)) + EPS
    )
    scale = jnp.broadcast_to(adaptive, (8, 128))[None]
    ad[...] = adaptive
    sides[2].start()
    for f in range(FR):
        v = a_ref[f].reshape(96, 8, 128) + scale * b_ref[f].reshape(96, 8, 128)
        buf[f] = v.reshape(16, W, 128).astype(BF16)
        pltpu.make_async_copy(buf.at[f], out_hbm.at[f], sem).start()
    mixed = (rec + adaptive * gan) / pixels
    for ab in range(9):
        wg[ab // 3, ab % 3] = mixed[ab * 3 : ab * 3 + 3]
    sides[1].start()
    drain(buf, sem)
    wait_all(sides)


def final(sums, a, b, back, pixels):
    hbm = lambda: pl.BlockSpec(memory_space=pltpu.HBM)
    return pl.pallas_call(
        functools.partial(final_body, pixels),
        out_shape=(
            jax.ShapeDtypeStruct((FR, 16, W, 128), BF16),
            jax.ShapeDtypeStruct((3, 3, 3, 128), F32),
            jax.ShapeDtypeStruct((1, 1), F32),
            jax.ShapeDtypeStruct((768, W), BF16),
        ),
        in_specs=[vspec()] * 4,
        out_specs=(hbm(), hbm(), hbm(), hbm()),
        scratch_shapes=[
            VM((FR, 16, W, 128), BF16),
            VM((3, 3, 3, 128), F32),
            VM((1, 1), F32),
            pltpu.SemaphoreType.DMA,
            pltpu.SemaphoreType.DMA((3,)),
        ],
        compiler_params=pltpu.CompilerParams(vmem_limit_bytes=24 << 20),
        name="final",
    )(sums, a, b, back)


def per_device(
    features, target, conv_weight, disc_first, disc_second, disc_third, disc_fourth, disc_head
):
    clips = lax.axis_size("clip")
    wanted = jnp.transpose(target[0], (0, 2, 1, 3)).reshape(768, W)
    w1 = jnp.transpose(disc_first, (0, 2, 1, 3))
    w2 = disc_second.reshape(4, 256, 128)
    w3 = disc_third.reshape(16, 128, 256)
    w4 = disc_fourth.reshape(16, 256, 512)
    head = disc_head.reshape(4, 4, 512)
    pixels = float(clips * FR * 256 * W)
    sums, a, b, back = core(conv_weight, features[0], wanted, w1, w2, w3, w4, head)
    feature_grad, weight_grad, adaptive, back = final(sums, a, b, back, pixels)
    image_back = jnp.transpose(back.reshape(1, FR, 3, 16, W), (0, 1, 3, 2, 4))
    return (feature_grad[None], image_back, weight_grad, adaptive[0, 0])


def solution(mesh):
    return jax.shard_map(
        per_device,
        mesh=mesh,
        in_specs=(
            P("clip", None, "row", None, None),
            P("clip", None, "row", None, None),
            P(),
            P(),
            P(),
            P(),
            P(),
            P(),
        ),
        out_specs=(
            P("clip", None, "row", None, None),
            P("clip", None, "row", None, None),
            P(),
            P(),
        ),
        check_vma=False,
    )
```
